32 devices in a mesh: seq: 8 (over z, x), tp: 4 (over y, core).
Axes of the slice: x: 2, y: 2, z: 4, core: 2. Of those that a mesh axis runs over, the one named last changes fastest.
Arguments:
- byte_states: bfloat16 [4096, 1024], P('seq'), may hold values from -6 to 6
- flags: int32 [4096], P('seq'), may hold values from 0 to 1, as said below
- stretch_owner: int32 [1024, 1], P('seq'), may hold values from 0 to 7; in each aligned block of 128 rows (0 to 127, 128 to 255, ...) at most 32 rows name the same one
- log_decay: float32 [4096, 16], P('seq', 'tp'), may hold values from -2 to 0, as said below
- w_x: bfloat16 [1024, 2048], P(None, 'tp'), may hold values from -0.1875 to 0.1875
- w_z: bfloat16 [1024, 2048], P(None, 'tp'), may hold values from -0.1875 to 0.1875
- w_bc: bfloat16 [1024, 256], replicated, may hold values from -0.1875 to 0.1875
- w_out: bfloat16 [2048, 1024], P('tp'), may hold values from -0.125 to 0.125
- pad_vector: bfloat16 [512], replicated, may hold values from -5 to 5
- w_q: bfloat16 [1536, 1536], P(None, 'tp'), may hold values from -8 to 8
- w_k: bfloat16 [1536, 1536], P(None, 'tp'), may hold values from -8 to 8
- w_v: bfloat16 [1536, 1536], P(None, 'tp'), may hold values from -0.15625 to 0.15625
- w_o: bfloat16 [1536, 1536], P('tp'), may hold values from -0.15625 to 0.15625
Outputs:
- enc_out: bfloat16 [4096, 1024], P('seq', 'tp')
- main_out: bfloat16 [2048, 1536], P('seq')
The draws below stay inside these ranges and needn't reach their ends.
Inputs may be any that keep to these rules, and one draw needn't show every extreme that they name: `flags`: exactly 128 ones among each aligned block of 512 bytes. `stretch_owner`: in each aligned block of 128 stretches no owner is named more than 32 times. `log_decay`: negative.
All inputs are finite; a program needn't handle non-finite values.
Results may differ from the reference program's by a relative error of at most 0.015.
Values may be sent and summed in bfloat16 or wider, within the bound.
A program may use at most 128 MiB of HBM per device.

```python
import math
import jax
import jax.numpy as jnp
import numpy as np
from jax import lax

D = 1024
INNER = 2048
RECURRENT_UNITS = 16
HEAD_P = 128
STATE = 128
DM = 1536
HM = 12
HD = 128
BLOCK = 256
BYTES_DEV = 512
CH_DEV = 128
OWNERS = 8
CAP = 32
ROWS_OWN = 256
TEXT_OCTETS = 4096
STRETCHES = 1024
SLOTS = 2048


def draw_flags(key, part):
    groups = TEXT_OCTETS // BYTES_DEV
    sampler_seeds = jax.random.split(key, groups)

    def shuffled(subkey):
        return jax.random.permutation(subkey, BYTES_DEV)
    orders = jax.vmap(shuffled)(sampler_seeds)
    return (orders < CH_DEV).astype(jnp.int32).reshape(TEXT_OCTETS)


def draw_log_decay(key, part):
    sampler_seeds = jax.random.split(key, 7)
    fast_share = 0.5
    fast = jax.random.uniform(sampler_seeds[0], (RECURRENT_UNITS,), jnp.float32) < fast_share
    fast_rate = jnp.exp(jax.random.uniform(sampler_seeds[1], (RECURRENT_UNITS,), jnp.float32, math.log(1.0 / 50.0), math.log(1.0 / 30.0)))
    slow_rate = jnp.exp(jax.random.uniform(sampler_seeds[2], (RECURRENT_UNITS,), jnp.float32, math.log(0.1), math.log(0.5))) / TEXT_OCTETS
    widening_ratio = jnp.where(fast, fast_rate, slow_rate)
    groups = TEXT_OCTETS // BYTES_DEV
    device_factor = jnp.exp2(jax.random.uniform(sampler_seeds[3], (groups, RECURRENT_UNITS), jnp.float32))
    octet_codes = jnp.repeat(device_factor, BYTES_DEV, axis=0)
    rough_guess = jnp.exp(jax.random.uniform(sampler_seeds[4], (TEXT_OCTETS, RECURRENT_UNITS), jnp.float32, math.log(0.5), math.log(2.0)))
    spurt_displacement = jax.random.randint(sampler_seeds[5], (2,), 0, TEXT_OCTETS)
    spurt_extent = jax.random.uniform(sampler_seeds[6], (2, RECURRENT_UNITS), jnp.float32, 0.22, 0.5)
    octet_location = jnp.arange(TEXT_OCTETS)
    agreement_tally = (octet_location[:, None] == spurt_displacement[None, :]).astype(jnp.float32)
    spurt_batches = jnp.sum(agreement_tally[:, :, None] * spurt_extent[None, :, :], axis=1)
    return -(widening_ratio[None, :] * octet_codes * rough_guess) - spurt_batches


def key_basis(key):
    return jax.random.truncated_normal(jax.random.fold_in(key, 11), -4.0, 4.0, (DM, HM * HD), jnp.float32)


def draw_w_k(key, part):
    return (key_basis(key) / math.sqrt(DM)).astype(jnp.bfloat16)


def draw_w_q(key, part):
    noise = jax.random.truncated_normal(jax.random.fold_in(key, 13), -4.0, 4.0, (DM, HM * HD), jnp.float32)
    mixed = noise
    return (mixed / math.sqrt(DM)).astype(jnp.bfloat16)


def block_levels(own_key, extent, pieces, smallest, high):
    level, own = 1.0, jax.random.fold_in(own_key, 6)
    for dim, blocks in pieces:
        draws = jnp.exp(jax.random.uniform(jax.random.fold_in(own, dim), (blocks,), jnp.float32, smallest / len(pieces), high / len(pieces)))
        level = level * jnp.repeat(draws, extent[dim] // blocks).reshape([-1 if axis == dim else 1 for axis in range(len(extent))])
    return level


def deal_out(own_key, own, number, rows, amount, top, most, slope):
    sequence = jax.random.permutation(own_key, amount)
    crowded, common = portions_of(amount, rows * top, most, slope, True), portions_of(amount, rows * top, most, slope, False)
    places = jnp.arange(amount)

    def named(lengths, turn):
        used = int((lengths > 0).sum())
        fixed = max(1, used // 4)
        passed = fixed + (places - fixed + turn * (used - fixed)) % max(1, amount - fixed)
        return jnp.zeros((amount,), jnp.int32).at[sequence[jnp.where(places < fixed, places, passed)]].set(jnp.asarray(lengths, jnp.int32))

    lengths = jnp.where(number % 4 == 0, named(crowded, number // 4), named(common, number - number // 4 - 1))
    mixed = jax.random.permutation(jax.random.fold_in(own, 3), amount)
    source_of, taker = mixed[0:amount // 2 * 2:2], mixed[1:amount // 2 * 2:2]
    margin = jnp.minimum(lengths[source_of] - 1, most - lengths[taker]) // 2
    margin = jnp.where((source_of == sequence[0]) | (taker == sequence[0]) | (lengths[taker] == 0), 0, jnp.maximum(margin, 0))
    passed = jax.random.randint(jax.random.fold_in(own, 4), (amount // 2,), 0, 1 << 20) % (margin + 1)
    lengths = lengths.at[source_of].add(-passed).at[taker].add(passed)
    labels = jnp.searchsorted(jnp.cumsum(lengths), jnp.arange(rows * top), side="right").astype(jnp.int32)
    table = labels.reshape(top, rows).T
    table = table[jax.random.permutation(jax.random.fold_in(own, 1), rows)]
    turn = jax.random.randint(jax.random.fold_in(own, 2), (rows, 1), 0, top)
    return jnp.take_along_axis(table, (jnp.arange(top)[None, :] + turn) % top, axis=1)


def portions_of(count, total, most, lean, full):
    weights = [(1 << 20) // math.isqrt(grade ** lean) + 1 for grade in range(1, count + 1)]
    largest = most if full else min(most, max(-(-total // count), total * weights[0] // sum(weights)))
    least = 1 if total - largest >= count - 1 else 0
    given, spare = [largest] + [least] * (count - 1), total - largest - least * (count - 1)
    while spare > 0:
        free = [i for i in range(1, count) if given[i] < largest] or [i for i in range(1, count) if given[i] < most]
        whole, remaining = sum([weights[i] for i in free]), spare
        for i in free:
            extra = min(most - given[i], max(1, remaining * weights[i] // whole), spare)
            given[i] = given[i] + extra
            spare = spare - extra
    return np.array(given)


def bell_draw(own_key, dims, width, limit, cuts=(), held_as=jnp.bfloat16):
    array = width * jax.random.normal(own_key, dims, jnp.float32)
    if cuts:
        array = array * block_levels(own_key, dims, cuts, -0.22, 0.18)
    return jnp.clip(array, -limit, limit).astype(held_as)


def setup_inputs(seed: int = 0) -> dict:
    seeds = jax.random.split(jax.random.key(seed), 14)
    byte_states = bell_draw(seeds[0], (TEXT_OCTETS, D), 1.0, 6.0, ((0, 8),))
    flags = draw_flags(jax.random.fold_in(seeds[13], 71), 0)
    stretch_owner_keys = jax.random.split(jax.random.fold_in(seeds[2], 1), STRETCHES // CH_DEV)
    stretch_owner_turns = jax.random.permutation(jax.random.fold_in(seeds[2], 3), STRETCHES // CH_DEV)
    stretch_owner = jax.vmap(lambda own, number: deal_out(jax.random.fold_in(seeds[2], 2), own, number, CH_DEV, OWNERS, 1, CAP, 2))(stretch_owner_keys, stretch_owner_turns).reshape((STRETCHES, 1))
    log_decay = draw_log_decay(jax.random.fold_in(seeds[13], 71), 0)
    w_x = bell_draw(seeds[4], (D, INNER), D ** -0.5, 0.1875, ((1, 4),))
    w_z = bell_draw(seeds[5], (D, INNER), D ** -0.5, 0.1875, ((1, 4),))
    w_bc = bell_draw(seeds[6], (D, 2 * STATE), D ** -0.5, 0.1875)
    w_out = bell_draw(seeds[7], (INNER, D), INNER ** -0.5, 0.125, ((0, 4),))
    pad_vector = bell_draw(seeds[8], (DM - D,), 1.0, 5.0)
    w_q = draw_w_q(jax.random.fold_in(seeds[13], 71), 0)
    w_k = draw_w_k(jax.random.fold_in(seeds[13], 71), 0)
    w_v = bell_draw(seeds[11], (DM, HM * HD), DM ** -0.5, 0.15625, ((1, 4),))
    w_o = bell_draw(seeds[12], (HM * HD, DM), (HM * HD) ** -0.5, 0.15625, ((0, 4),))
    return dict(byte_states=byte_states, flags=flags, stretch_owner=stretch_owner, log_decay=log_decay, w_x=w_x, w_z=w_z, w_bc=w_bc, w_out=w_out, pad_vector=pad_vector, w_q=w_q, w_k=w_k, w_v=w_v, w_o=w_o)


eps = 1e-05
highest = lax.Precision.HIGHEST

def rms_rows(values):
    wide = values.astype(jnp.float32)
    return wide * lax.rsqrt(lax.optimization_barrier(jnp.mean(wide * wide, axis=-1, keepdims=True)) + eps)

def ssd_blocks(xh, bmat, cmat, decay, start_state):
    rows, heads, width_p = xh.shape
    nblk = rows // BLOCK

    def advance(state, block):
        x_blk, b_blk, c_blk, a_blk = block
        cum = jnp.cumsum(a_blk, axis=0)
        later = lax.broadcasted_iota(jnp.int32, (BLOCK, BLOCK), 0)
        earlier = lax.broadcasted_iota(jnp.int32, (BLOCK, BLOCK), 1)
        causal = (later >= earlier)[:, :, None]
        spans = jnp.where(causal, cum[:, None, :] - cum[None, :, :], -1e+30)
        intersection = jnp.dot(c_blk, b_blk.T, preferred_element_type=jnp.float32)
        mixing = intersection[:, :, None] * jnp.exp(spans)
        x_wide = x_blk.astype(jnp.float32)
        inside = jnp.einsum('tsh,shp->thp', mixing, x_wide, precision=highest)
        carried = jnp.einsum('tn,hnp->thp', c_blk.astype(jnp.float32), state, precision=highest) * jnp.exp(cum)[:, :, None]
        tail = jnp.exp(cum[-1][None, :] - cum)
        fresh = jnp.einsum('sh,sn,shp->hnp', tail, b_blk.astype(jnp.float32), x_wide, precision=highest)
        new_state = state * jnp.exp(cum[-1])[:, None, None] + fresh
        return (new_state, inside + carried)
    blocks = (xh.reshape(nblk, BLOCK, heads, width_p), bmat.reshape(nblk, BLOCK, -1), cmat.reshape(nblk, BLOCK, -1), decay.reshape(nblk, BLOCK, heads))
    final, outs = lax.scan(advance, start_state, blocks)
    return (outs.reshape(rows, heads, width_p), final)

def attention_rows(queries, keys, values):
    count = queries.shape[0]
    size = math.gcd(count, 256)
    scale = 1.0 / math.sqrt(HD)
    key_wide = keys.astype(jnp.float32)
    value_wide = values.astype(jnp.float32)
    key_pos = jnp.arange(count).astype(jnp.int32)

    def one_block(start):
        q_blk = lax.dynamic_slice_in_dim(queries, start, size, 0).astype(jnp.float32)
        scores = jnp.einsum('qhd,khd->hqk', q_blk, key_wide) * scale
        query_pos = start + jnp.arange(size).astype(jnp.int32)
        allowed = key_pos[None, None, :] <= query_pos[None, :, None]
        scores = jnp.where(allowed, scores, -1e+30)
        top = lax.optimization_barrier(jnp.max(scores, axis=2, keepdims=True))
        expo = jnp.where(allowed, jnp.exp(scores - top), 0.0)
        total = lax.optimization_barrier(jnp.sum(expo, axis=2))
        rounded = lax.optimization_barrier(expo.astype(jnp.bfloat16))
        numer = jnp.einsum('hqk,khd->qhd', rounded.astype(jnp.float32), value_wide)
        return (numer / jnp.transpose(total)[:, :, None]).astype(jnp.bfloat16)
    starts = (jnp.arange(count // size) * size).astype(jnp.int32)
    result = lax.map(one_block, starts)
    return result.reshape(count, queries.shape[1] * queries.shape[2])

def reference(byte_states, flags, stretch_owner, log_decay, w_x, w_z, w_bc, w_out, pad_vector, w_q, w_k, w_v, w_o):
    normed = rms_rows(byte_states).astype(jnp.bfloat16)
    xs = jnp.dot(normed, w_x, preferred_element_type=jnp.float32).astype(jnp.bfloat16)
    zgate = jnp.dot(normed, w_z, preferred_element_type=jnp.float32)
    projected = jnp.dot(normed, w_bc, preferred_element_type=jnp.float32).astype(jnp.bfloat16)
    bmat = projected[:, :STATE]
    cmat = projected[:, STATE:]
    start_state = jnp.zeros((RECURRENT_UNITS, STATE, HEAD_P), jnp.float32)
    mixed, final = ssd_blocks(xs.reshape(TEXT_OCTETS, RECURRENT_UNITS, HEAD_P), bmat, cmat, log_decay, start_state)
    gated = mixed * jax.nn.silu(zgate).reshape(TEXT_OCTETS, RECURRENT_UNITS, HEAD_P)
    scaled = gated * lax.rsqrt(lax.optimization_barrier(jnp.mean(gated * gated, axis=2, keepdims=True)) + eps)
    scaled = scaled.reshape(TEXT_OCTETS, INNER).astype(jnp.bfloat16)
    enc_out = (byte_states.astype(jnp.float32) + jnp.dot(scaled, w_out, preferred_element_type=jnp.float32)).astype(jnp.bfloat16)
    picked = jnp.nonzero(flags == 1, size=STRETCHES)[0].astype(jnp.int32)
    stretch_rows = enc_out[picked]
    owners = stretch_owner[:, 0].astype(jnp.int32)
    owner_hot = (owners[:, None] == jnp.arange(OWNERS).astype(jnp.int32)[None, :]).astype(jnp.int32)
    owner_hot = owner_hot.reshape(OWNERS, CH_DEV, OWNERS)
    before = jnp.cumsum(owner_hot, axis=1) - owner_hot
    order = lax.optimization_barrier(jnp.sum(before * owner_hot, axis=2)).reshape(STRETCHES).astype(jnp.int32)
    source = (jnp.arange(STRETCHES) // CH_DEV).astype(jnp.int32)
    slot = owners * ROWS_OWN + source * CAP + order
    padding = jnp.broadcast_to(pad_vector[None, :], (STRETCHES, DM - D))
    stream = jnp.concatenate([stretch_rows, padding], axis=1)
    stream_norm = rms_rows(stream).astype(jnp.bfloat16)
    queries = jnp.dot(stream_norm, w_q, preferred_element_type=jnp.float32).astype(jnp.bfloat16).reshape(STRETCHES, HM, HD)
    keys = jnp.dot(stream_norm, w_k, preferred_element_type=jnp.float32).astype(jnp.bfloat16).reshape(STRETCHES, HM, HD)
    values = jnp.dot(stream_norm, w_v, preferred_element_type=jnp.float32).astype(jnp.bfloat16).reshape(STRETCHES, HM, HD)
    attended = attention_rows(queries, keys, values)
    main = (stream.astype(jnp.float32) + jnp.dot(attended, w_o, preferred_element_type=jnp.float32)).astype(jnp.bfloat16)
    main_out = jnp.zeros((SLOTS, DM), jnp.bfloat16).at[slot].set(main)
    return (enc_out, main_out)
```

```python
import functools
import math
import types

import jax
import jax.numpy as jnp
from jax import lax
from jax.experimental import pallas as pl
from jax.experimental.pallas import tpu as pltpu
from jax.sharding import PartitionSpec as P

HD = 128
eps = 1e-05
f32 = jnp.float32
bf16 = jnp.bfloat16
MESH = pl.DeviceIdType.MESH
VM = pl.BlockSpec(memory_space=pltpu.VMEM)
HBM = pl.BlockSpec(memory_space=pltpu.HBM)
DMA = pltpu.SemaphoreType.DMA
GRANT = 60000000


def cost(us):
    return pl.CostEstimate(flops=us * 10**9, bytes_accessed=us * 3 * 10**6, transcendentals=0)


def mm(a, b):
    return jnp.dot(a, b, preferred_element_type=f32)


def mm_t(a, b):
    return lax.dot_general(a, b, (((1,), (1,)), ((), ())), preferred_element_type=f32)


def t_mm(a, b):
    return lax.dot_general(a, b, (((0,), (0,)), ((), ())), preferred_element_type=f32)


def three(a):
    hi = a.astype(bf16)
    rest = a - hi.astype(f32)
    mid = rest.astype(bf16)
    low = (rest - mid.astype(f32)).astype(bf16)
    return hi, mid, low


def iota(shape, dim):
    return lax.broadcasted_iota(jnp.int32, shape, dim)


def loop(start, stop, body):
    if stop - start <= 8:
        for i in range(start, stop):
            body(i)
    else:
        lax.fori_loop(start, stop, lambda i, _: (body(i), 0)[1], 0)


def others(axis):
    me, n = lax.axis_index(axis), lax.axis_size(axis)
    return [lax.rem(me + d, n) for d in range(1, n)]


def remote(src, dst, send, recv, device):
    return pltpu.make_async_remote_copy(
        src_ref=src, dst_ref=dst, send_sem=send, recv_sem=recv, device_id=device, device_id_type=MESH
    )


def whole_kernel(names, *refs):
    r = types.SimpleNamespace(**dict(zip(names, refs)))
    n, split = lax.axis_size("seq"), lax.axis_size("tp")
    line, groups = n // 2, split // 2
    seq, tp = lax.axis_index("seq"), lax.axis_index("tp")
    z, x = seq // 2, lax.rem(seq, 2)
    hi, lo = tp // 2, lax.rem(tp, 2)
    pair = {"seq": z * 2 + 1 - x}
    core = {"tp": hi * 2 + 1 - lo}
    rest = [lax.rem(hi + e, groups) for e in range(1, groups)]

    def column(g):
        return {"tp": g * 2 + lo}

    def across(g):
        return {"seq": z * 2 + 1 - x, "tp": g * 2 + lo}

    rows, width = r.bytes_in.shape
    heads = r.decay_in.shape[0]
    half = heads // 2
    state_n = r.wbc_in.shape[1] // 2
    p = r.wx_in.shape[1] // heads
    count = r.owner_in.shape[1]
    quarter = width // split
    wide = r.wq_in.shape[0]
    size = wide // split
    part = r.wq_in.shape[1]
    units = part // HD
    cap = r.out.shape[1]

    fetches = {}
    moves = [
        ("decay", r.decay_in, r.decay),
        ("bytes", r.bytes_in, r.bytes),
        ("wbc", r.wbc_in, r.wbc),
        ("wx", r.wx_in, r.wx),
        ("flags", r.flags_in, r.flags),
        ("wz", r.wz_in, r.wz),
        ("pad", r.pad_in, r.pad),
        ("owner", r.owner_in, r.owner),
        ("wout", r.wout_in, r.wout),
        ("wk", r.wk_in, r.wkv.at[:, pl.ds(0, part)]),
        ("wv", r.wv_in, r.wkv.at[:, pl.ds(part, part)]),
        ("wq", r.wq_in, r.wq),
        ("wo", r.wo_in, r.wo),
    ]
    for i, (name, src, dst) in enumerate(moves):
        fetches[name] = pltpu.make_async_copy(src, dst, r.own.at[i])
        fetches[name].start()

    barrier = pltpu.get_barrier_semaphore()

    def knock(device):
        pl.semaphore_signal(barrier, inc=1, device_id=device, device_id_type=MESH)

    loop(1, n, lambda d: knock({"seq": lax.rem(seq + d, n)}))
    for peer in others("tp"):
        knock({"tp": peer})
    for g in rest:
        knock(across(g))

    fetches["decay"].wait()
    parts = three(r.decay[...])
    lower = (iota((rows, rows), 0) >= iota((rows, rows), 1)).astype(f32).astype(bf16)
    upper = (iota((rows, rows), 0) <= iota((rows, rows), 1)).astype(f32).astype(bf16)
    ones = jnp.ones((rows, state_n), bf16)
    total = sum(mm(piece, ones) for piece in parts)
    filler = jnp.zeros((r.tots.shape[1] - heads, state_n), f32)
    r.tots[seq] = jnp.concatenate([total, filler], axis=0)
    cum = sum(mm_t(lower, piece) for piece in parts)
    cum_row = sum(mm(piece, upper) for piece in parts)
    pl.semaphore_wait(barrier, n - 1 + split - 1 + groups - 1)

    def tot_copy(d):
        return remote(r.tots.at[seq], r.tots.at[seq], r.ts.at[d], r.tr.at[seq], {"seq": lax.rem(seq + d, n)})

    def tot_wait(d):
        peer = lax.rem(seq + d, n)
        remote(r.tots.at[peer], r.tots.at[peer], r.ts.at[d], r.tr.at[peer], pair).wait_recv()

    loop(1, n, lambda d: tot_copy(d).start())

    fetches["bytes"].wait()
    raw = r.bytes[...].astype(f32)
    normed = (raw * lax.rsqrt(jnp.mean(raw * raw, axis=-1, keepdims=True) + eps)).astype(bf16)
    fetches["wbc"].wait()
    bc = mm(normed, r.wbc[...]).astype(bf16)
    bmat, cmat = bc[:, :state_n], bc[:, state_n:]
    fetches["wx"].wait()
    xs = mm(normed, r.wx[...]).astype(bf16)
    tail = jnp.exp(cum[rows - 1 : rows, :] - cum)
    for h in range(heads):
        shrunk = (xs[:, h * p : (h + 1) * p].astype(f32) * tail[:, h : h + 1]).astype(bf16)
        state = t_mm(bmat, shrunk)
        r.state[h] = state
        r.state_out[h] = state.astype(bf16)

    def state_copy(h):
        return remote(r.state_out.at[h], r.state_got.at[h], r.s1s.at[h], r.s1r.at[h], pair)

    upward = z < line - 1

    for i in range(half):

        @pl.when((x == 0) | upward)
        def _():
            state_copy((1 - x) * half + i).start()

    @pl.when(x == 0)
    def _():
        for i in range(half):
            state_copy(i).start()

    fetches["wz"].wait()
    gate = mm(normed, r.wz[...])
    gate = gate * jax.nn.sigmoid(gate)
    r.gate[...] = gate
    fetches["flags"].wait()
    flags = r.flags[...]
    many = jnp.broadcast_to(flags.astype(f32), (16, rows)).astype(bf16)
    rank = mm(many, upper)[0:1, :].astype(jnp.int32) - 1
    hit = (rank == iota((count, rows), 0)) & (flags == 1)
    picker = jnp.where(hit, 1.0, 0.0).astype(bf16)

    def pick(values):
        return sum(mm(picker, piece) for piece in three(values))

    loop(1, n, tot_wait)

    def tot_rows(shard):
        tots = r.tots[shard]
        return [jnp.where(x == 0, tots[i : i + 1], tots[half + i : half + i + 1]) for i in range(half)]

    def slab_copy(d, i):
        return remote(
            r.slab_out.at[i], r.slab_got.at[z, i], r.s2s.at[d, i], r.s2r.at[z, i], {"seq": (z + d) * 2 + x}
        )

    def slab_wait(source, i):
        remote(r.slab_got.at[source, i], r.slab_got.at[source, i], r.s2s.at[0, i], r.s2r.at[source, i], pair).wait_recv()

    @pl.when(upward)
    def _():
        later = tot_rows(z * 2 + 1)
        for i in range(half):
            h = x * half + i
            state_copy(h).wait_recv()
            mine, got = r.state[h], r.state_got[h].astype(f32)
            first, second = jnp.where(x == 0, mine, got), jnp.where(x == 0, got, mine)
            r.slab_out[i] = (first * jnp.exp(later[i]) + second).astype(bf16)

            def reach(k):
                d = line - k

                @pl.when(z + d < line)
                def _():
                    slab_copy(d, i).start()

            loop(1, line, reach)

    middle = rows // 2
    for k in range(2):
        a, b = k * middle, (k + 1) * middle
        inter = mm_t(cmat[a:b], bmat[:b])
        causal = iota((middle, b), 0) + a >= iota((middle, b), 1)
        for h in range(heads):
            spans = cum[a:b, h : h + 1] - cum_row[h : h + 1, :b]
            mixing = (inter * jnp.exp(jnp.where(causal, spans, -1e30))).astype(bf16)
            r.mixed[a:b, h * p : (h + 1) * p] = mm(mixing, xs[:b, h * p : (h + 1) * p])
    mixed_picked = pick(r.mixed[...])
    gate_picked = pick(gate)
    grow_picked = jnp.exp(pick(cum))
    c_picked = mm(picker, cmat).astype(bf16)
    for g in range(groups):
        for k in range(2):
            q = g * 2 + k
            r.base[k, g] = mm(picker, r.bytes[:, q * quarter : (q + 1) * quarter]).astype(bf16)
    fetches["pad"].wait()
    fetches["wk"].wait()
    fetches["wv"].wait()
    fetches["wq"].wait()
    pad = jnp.broadcast_to(r.pad[...].astype(f32).reshape(1, -1), (count, r.pad.shape[0]))
    pad_square = jnp.sum(pad * pad, axis=1, keepdims=True)
    pad = pad.astype(bf16)
    pad_kv = mm(pad[:16], r.wkv[width:, :])[0:1]
    pad_q = mm(pad[:16], r.wq[width:, :])[0:1]
    fetches["owner"].wait()
    owner = r.owner[...]
    ranks = -(-n // 128) * 128
    hot = jnp.where(owner == iota((ranks, count), 0), 1.0, 0.0)
    strict = jnp.where(iota((count, count), 0) < iota((count, count), 1), 1.0, 0.0)
    before = mm(hot.astype(bf16), strict.astype(bf16))
    order = jnp.sum(before * hot, axis=0, keepdims=True).astype(jnp.int32)
    slot = owner * cap + order
    r.place[...] = jnp.where(slot == iota((n * cap, count), 0), 1.0, 0.0).astype(bf16)

    def step(k, carry):
        first, second = tot_rows(k * 2), tot_rows(k * 2 + 1)
        new = []
        for i in range(half):
            slab_wait(k, i)
            new.append(carry[i] * jnp.exp(first[i] + second[i]) + r.slab_got[k, i].astype(f32))
        return tuple(new)

    prefix = lax.fori_loop(0, z, step, tuple(jnp.zeros((state_n, p), f32) for _ in range(half)))

    def prefix_copy(i):
        return remote(r.prefix_out.at[i], r.prefix_got.at[i], r.s3s.at[i], r.s3r.at[i], pair)

    for i in range(half):
        r.prefix_out[i] = prefix[i].astype(bf16)

        @pl.when(z > 0)
        def _():
            prefix_copy(i).start()

    @pl.when(x == 1)
    def _():
        for i in range(half):
            state_copy(i).wait_recv()

    @pl.when((x == 1) & (z == line - 1))
    def _():
        for i in range(half):
            state_copy(half + i).wait_recv()

    tots = r.tots[z * 2]

    def settle(h, i, base, same):
        a, b = tots[i : i + 1], tots[half + i : half + i + 1]
        shrink = jnp.exp(jnp.where((x == 0) == same, a, b))
        moved = base * shrink + r.state_got[h].astype(f32)
        r.start[h] = jnp.where(x == 1, moved, base).astype(bf16)

    for i in range(half):
        settle(x * half + i, i, prefix[i], True)

    @pl.when(z > 0)
    def _():
        for i in range(half):
            prefix_copy(i).wait_recv()

    for i in range(half):
        got = jnp.where(z > 0, r.prefix_got[i].astype(f32), 0.0)
        settle((1 - x) * half + i, i, got, False)

    def finish(mixed, gate, cs, grow):
        scaled = []
        for h in range(heads):
            cols = slice(h * p, (h + 1) * p)
            gated = (mixed[:, cols] + mm(cs, r.start[h]) * grow[:, h : h + 1]) * gate[:, cols]
            norm = lax.rsqrt(jnp.mean(gated * gated, axis=1, keepdims=True) + eps)
            scaled.append((gated * norm).astype(bf16))
        return jnp.concatenate(scaled, axis=1)

    def cols(k, g, n):
        return pl.ds(pl.multiple_of((g * 2 + k) * n, 128), n)

    def core_swap(left, weight, n, send, got, sems):
        for g in range(groups):
            send[g] = mm(left, weight[:, cols(1 - lo, g, n)]).astype(bf16)
        copy = remote(send, got, sems.at[0], sems.at[1], core)
        copy.start()
        return copy

    def line_swap(send, got, sems):
        copies = []
        for e, g in enumerate(rest):
            copy = remote(send.at[g], got.at[hi], sems.at[0, e], sems.at[1, e], column(g))
            copy.start()
            copies.append(copy)
        return copies

    fetches["wout"].wait()
    scaled_picked = finish(mixed_picked, gate_picked, c_picked, grow_picked)
    pick_core = core_swap(scaled_picked, r.wout, quarter, r.d_send, r.d_got, r.d_core)
    mine = [mm(scaled_picked, r.wout[:, cols(lo, g, quarter)]) for g in range(groups)]
    scaled = finish(r.mixed[...], r.gate[...], cmat, jnp.exp(cum))
    pick_core.wait_recv()
    for g in range(groups):
        both = mine[g] + r.d_got[g].astype(f32)
        r.d_sum[g] = both
        r.d_line_send[g] = both.astype(bf16)
    pick_line = line_swap(r.d_line_send, r.d_line_got, r.d_line)
    enc_core = core_swap(scaled, r.wout, quarter, r.e_send, r.e_got, r.e_core)
    for g in range(groups):
        r.e_sum[g] = mm(scaled, r.wout[:, cols(lo, g, quarter)])
    summed = r.base[lo, hi].astype(f32) + r.d_sum[hi]
    for e, g in enumerate(rest):
        pick_line[e].wait_recv()
    for g in rest:
        summed = summed + r.d_line_got[g].astype(f32)
    r.rows[z, lo, x, hi] = summed.astype(bf16)

    def piece(slab, xx, g):
        return r.rows.at[slab, lo, xx, g]

    def up_copy(d):
        here = piece(z, x, hi)
        return remote(here, here, r.gz.at[d], r.gr.at[z, x, hi], {"seq": (z + d) * 2 + x})

    def line_copy(d, e):
        here = piece(z - d, x, hi)
        return remote(here, here, r.gy.at[d, e], r.gr.at[z - d, x, hi], column(rest[e]))

    def pair_copy(d):
        here = piece(z - d, x, hi)
        return remote(here, here, r.gx.at[d], r.gr.at[z - d, x, hi], pair)

    def far_copy(d, e):
        here = piece(z - d, x, hi)
        return remote(here, here, r.gd.at[d, e], r.gr.at[z - d, x, hi], across(rest[e]))

    def core_copy(d, xx):
        here = r.rows.at[z - d, lo, xx]
        return remote(here, here, r.gc.at[d, xx], r.gcr.at[z - d, xx], core)

    def core_wait(d, xx):
        there = r.rows.at[z - d, 1 - lo, xx]
        remote(there, there, r.gc.at[d, xx], r.gcr.at[z - d, xx], core).wait_recv()

    def piece_wait(slab, xx, g):
        here = piece(slab, xx, g)
        remote(here, here, r.gx.at[0], r.gr.at[slab, xx, g], pair).wait_recv()

    def spread(d):
        @pl.when((d > 0) | (x == 0))
        def _():
            for e in range(groups - 1):
                far_copy(d, e).start()
            pair_copy(d).start()

        for e in range(groups - 1):
            line_copy(d, e).start()

    def relay(d):
        for g in rest:
            piece_wait(z - d, x, g)
        core_copy(d, x).start()

        @pl.when((d > 0) | (x == 1))
        def _():
            for g in range(groups):
                piece_wait(z - d, 1 - x, g)
            core_copy(d, 1 - x).start()

    def climb(k):
        d = line - k

        @pl.when(z + d < line)
        def _():
            up_copy(d).start()

    loop(1, line, climb)
    spread(0)
    enc_core.wait_recv()
    for g in range(groups):
        both = r.e_sum[g] + r.e_got[g].astype(f32)
        r.e_sum[g] = both
        r.e_line_send[g] = both.astype(bf16)
    enc_line = line_swap(r.e_line_send, r.e_line_got, r.e_line)

    scale = 1.0 / math.sqrt(HD)

    def project(blocks, weight, pads):
        square = sum(jnp.sum(jnp.square(b.astype(f32)), axis=1, keepdims=True) for b in blocks)
        norm = lax.rsqrt((square + pad_square[0:1]) / wide + eps)
        product = sum(mm(b, weight[q * quarter : (q + 1) * quarter, :]) for q, b in enumerate(blocks))
        return ((product + pads) * norm).astype(bf16)

    def attend(blocks, allowed=None):
        kv = project(blocks, r.wkv, pad_kv)
        for h in range(units):
            span = slice(h * HD, (h + 1) * HD)
            scores = mm_t(r.query[:, span], kv[:, span]) * scale
            if allowed is not None:
                scores = jnp.where(allowed, scores, -1e30)
            best = r.best[h]
            top = jnp.maximum(best, jnp.max(scores, axis=1, keepdims=True))
            shrink = jnp.exp(best - top)
            expo = jnp.exp(scores - top)
            r.best[h] = top
            r.total[h] = r.total[h] * shrink + jnp.sum(expo, axis=1, keepdims=True)
            r.accum[h] = r.accum[h] * shrink + mm(expo.astype(bf16), kv[:, part + h * HD : part + (h + 1) * HD])

    def block(xx):
        return [r.rows[z, q % 2, xx, q // 2] for q in range(split)]

    def slab(d):
        return [r.rows[z - d, q % 2, :, q // 2].reshape(2 * count, quarter) for q in range(split)]

    def own_slab():
        core_wait(0, x)
        mine = block(x)
        stream = jnp.concatenate(mine + [pad], axis=1)
        for q in range(split):
            r.stream[q] = stream[:, q * size : (q + 1) * size]
        r.query[...] = project(mine, r.wq, pad_q)
        r.best[...] = jnp.full(r.best.shape, -1e30, f32)
        r.total[...] = jnp.zeros(r.total.shape, f32)
        r.accum[...] = jnp.zeros(r.accum.shape, f32)
        attend(mine, iota((count, count), 0) >= iota((count, count), 1))

        @pl.when(x == 1)
        def _():
            core_wait(0, 0)
            attend(block(0))

    def turn(d, _):
        @pl.when(d <= z)
        def _():
            piece_wait(z - d, x, hi)
            spread(d)

        @pl.when(d - 1 <= z)
        def _():
            relay(d - 1)

        @pl.when(d == 2)
        def _():
            own_slab()

        @pl.when(d > 2)
        def _():
            core_wait(d - 2, 0)
            core_wait(d - 2, 1)
            attend(slab(d - 2))

        return 0

    lax.fori_loop(1, z + 3, turn, 0)
    attended = jnp.concatenate([(r.accum[h] / r.total[h]).astype(bf16) for h in range(units)], axis=1)

    fetches["wo"].wait()
    main_core = core_swap(attended, r.wo, size, r.f_send, r.f_got, r.f_core)
    mine = [mm(attended, r.wo[:, cols(lo, g, size)]) for g in range(groups)]
    main_core.wait_recv()
    for g in range(groups):
        both = mine[g] + r.f_got[g].astype(f32)
        r.f_sum[g] = both
        r.f_line_send[g] = both.astype(bf16)
    main_line = line_swap(r.f_line_send, r.f_line_got, r.f_line)
    for copy in enc_line:
        copy.wait_recv()
    enc = r.bytes[:, pl.ds(pl.multiple_of(tp * quarter, 128), quarter)].astype(f32) + r.e_sum[hi]
    for g in rest:
        enc = enc + r.e_line_got[g].astype(f32)
    r.enc[...] = enc.astype(bf16)
    summed = r.stream[tp].astype(f32) + r.f_sum[hi]
    for copy in main_line:
        copy.wait_recv()
    for g in rest:
        summed = summed + r.f_line_got[g].astype(f32)
    r.send[...] = mm(r.place[...], summed.astype(bf16)).astype(bf16).reshape(n, cap, size)

    def spot(e, d):
        column = (lax.rem(hi - e + groups, groups) * 2 + lo) * size
        return r.out.at[lax.rem(seq - d + n, n), :, pl.ds(pl.multiple_of(column, 128), size)]

    def far(d):
        there = r.out.at[seq, :, pl.ds(pl.multiple_of(tp * size, 128), size)]
        peer = lax.rem(seq + d, n)
        return remote(r.send.at[peer], there, r.hs.at[d], r.hr.at[d], {"seq": peer})

    def far_wait(d):
        remote(spot(0, d), spot(0, d), r.hs.at[d], r.hr.at[d], pair).wait_recv()

    def direct(e, d):
        return remote(spot(0, d), spot(0, d), r.hys.at[e, d], r.hyr.at[e, d], {"tp": lax.rem(hi + e, groups) * 2 + lo})

    def beside(e, d):
        return remote(spot(e, d), spot(e, d), r.hcs.at[e, d], r.hcr.at[e, d], core)

    def pass_on(d):
        for e in range(1, groups):
            direct(e, d).start()
        beside(0, d).start()

    def pass_across(d):
        for e in range(1, groups):
            direct(e, d).wait_recv()
            beside(e, d).start()

    loop(1, n, lambda d: far(d).start())
    r.out[seq, :, pl.ds(pl.multiple_of(tp * size, 128), size)] = r.send[seq]
    pass_on(0)

    def deliver(d):
        far_wait(d)
        pass_on(d)
        pass_across(d - 1)

    loop(1, n, deliver)
    pass_across(n - 1)

    def close(d):
        for e in range(groups):
            beside(e, d).wait_recv()
            beside(e, d).wait_send()
            if e > 0:
                direct(e, d).wait_send()

    loop(0, n, close)
    loop(1, n, lambda d: far(d).wait_send())
    loop(1, n, lambda d: tot_copy(d).wait_send())
    for copy in [pick_core, enc_core, main_core] + pick_line + enc_line + main_line:
        copy.wait_send()
    for i in range(half):

        @pl.when((x == 0) | upward)
        def _():
            state_copy((1 - x) * half + i).wait_send()

        @pl.when(x == 0)
        def _():
            state_copy(i).wait_send()

        @pl.when(z > 0)
        def _():
            prefix_copy(i).wait_send()

    def close_up(d):
        @pl.when(z + d < line)
        def _():
            up_copy(d).wait_send()
            for i in range(half):
                slab_copy(d, i).wait_send()

    loop(1, line, close_up)

    def close_row(d, _):
        for e in range(groups - 1):
            line_copy(d, e).wait_send()
        core_copy(d, x).wait_send()

        @pl.when((d > 0) | (x == 0))
        def _():
            for e in range(groups - 1):
                far_copy(d, e).wait_send()
            pair_copy(d).wait_send()

        @pl.when((d > 0) | (x == 1))
        def _():
            core_copy(d, 1 - x).wait_send()

        return 0

    lax.fori_loop(0, z + 1, close_row, 0)


def on_device(
    byte_states, flags, stretch_owner, log_decay, w_x, w_z, w_bc, w_out, pad_vector, w_q, w_k, w_v, w_o
):
    rows, width = byte_states.shape
    heads = log_decay.shape[1]
    inner = w_x.shape[1]
    p = inner // heads
    state_n = w_bc.shape[1] // 2
    n = lax.axis_size("seq")
    split = lax.axis_size("tp")
    line, groups, half = n // 2, split // 2, heads // 2
    count = stretch_owner.shape[0]
    quarter = width // split
    cap = max(2, 2 * count // n)
    wide, part = w_q.shape
    size = wide // split
    units = part // HD
    shape = jax.ShapeDtypeStruct
    args = dict(
        bytes_in=byte_states, flags_in=flags.reshape(1, rows), owner_in=stretch_owner.reshape(1, count),
        decay_in=log_decay.T, wx_in=w_x, wz_in=w_z, wbc_in=w_bc, wout_in=w_out, pad_in=pad_vector,
        wq_in=w_q, wk_in=w_k, wv_in=w_v, wo_in=w_o,
    )
    outs = dict(enc=shape((rows, quarter), bf16), out=shape((n, cap, wide), bf16))

    def wide_vmem(*dims):
        return pltpu.VMEM(dims, f32)

    def vmem(*dims):
        return pltpu.VMEM(dims, bf16)

    others_n = max(groups - 1, 1)
    scratch = dict(
        bytes=vmem(rows, width), flags=pltpu.VMEM((1, rows), jnp.int32), owner=pltpu.VMEM((1, count), jnp.int32),
        decay=wide_vmem(heads, rows), wx=vmem(*w_x.shape), wz=vmem(*w_z.shape), wbc=vmem(*w_bc.shape),
        wout=vmem(*w_out.shape), pad=vmem(*pad_vector.shape), wq=vmem(*w_q.shape), wkv=vmem(wide, 2 * part),
        wo=vmem(*w_o.shape), own=DMA((len(args),)),
        tots=wide_vmem(n, -(-heads // 8) * 8, state_n), ts=DMA((n,)), tr=DMA((n,)),
        state=wide_vmem(heads, state_n, p), state_out=vmem(heads, state_n, p), state_got=vmem(heads, state_n, p),
        s1s=DMA((heads,)), s1r=DMA((heads,)),
        slab_out=vmem(half, state_n, p), slab_got=vmem(line, half, state_n, p),
        s2s=DMA((line, half)), s2r=DMA((line, half)),
        prefix_out=vmem(half, state_n, p), prefix_got=vmem(half, state_n, p), s3s=DMA((half,)), s3r=DMA((half,)),
        start=vmem(heads, state_n, p), gate=wide_vmem(rows, inner), mixed=wide_vmem(rows, inner),
        base=vmem(2, groups, count, quarter), place=vmem(n * cap, count),
        d_send=vmem(groups, count, quarter), d_got=vmem(groups, count, quarter), d_core=DMA((2,)),
        d_sum=wide_vmem(groups, count, quarter), d_line_send=vmem(groups, count, quarter),
        d_line_got=vmem(groups, count, quarter), d_line=DMA((2, others_n)),
        e_send=vmem(groups, rows, quarter), e_got=vmem(groups, rows, quarter), e_core=DMA((2,)),
        e_sum=wide_vmem(groups, rows, quarter), e_line_send=vmem(groups, rows, quarter),
        e_line_got=vmem(groups, rows, quarter), e_line=DMA((2, others_n)),
        f_send=vmem(groups, count, size), f_got=vmem(groups, count, size), f_core=DMA((2,)),
        f_sum=wide_vmem(groups, count, size), f_line_send=vmem(groups, count, size),
        f_line_got=vmem(groups, count, size), f_line=DMA((2, others_n)),
        rows=vmem(line, 2, 2, groups, count, quarter), gr=DMA((line, 2, groups)), gcr=DMA((line, 2)),
        gz=DMA((line,)), gx=DMA((line,)), gy=DMA((line, others_n)), gd=DMA((line, others_n)), gc=DMA((line, 2)),
        stream=vmem(split, count, size), query=vmem(count, part),
        best=wide_vmem(units, count, 1), total=wide_vmem(units, count, 1), accum=wide_vmem(units, count, HD),
        send=vmem(n, cap, size), hs=DMA((n,)), hr=DMA((n,)),
        hys=DMA((groups, n)), hyr=DMA((groups, n)), hcs=DMA((groups, n)), hcr=DMA((groups, n)),
    )
    enc_out, main_out = pl.pallas_call(
        functools.partial(whole_kernel, list(args) + list(outs) + list(scratch)),
        out_shape=list(outs.values()),
        in_specs=[HBM] * len(args),
        out_specs=[VM] * len(outs),
        scratch_shapes=list(scratch.values()),
        cost_estimate=cost(60),
        compiler_params=pltpu.CompilerParams(
            collective_id=0, has_side_effects=True, vmem_limit_bytes=GRANT
        ),
    )(*args.values())
    return (enc_out, main_out.reshape(n * cap, wide))


def solution(mesh):
    placed = (
        P("seq", None),
        P("seq"),
        P("seq", None),
        P("seq", "tp"),
        P(None, "tp"),
        P(None, "tp"),
        P(),
        P("tp", None),
        P(),
        P(None, "tp"),
        P(None, "tp"),
        P(None, "tp"),
        P("tp", None),
    )
    return jax.shard_map(
        on_device,
        mesh=mesh,
        in_specs=placed,
        out_specs=(P("seq", "tp"), P("seq", None)),
        check_vma=False,
    )
```

```python
import functools
import math
import types

import jax
import jax.numpy as jnp
from jax import lax
from jax.experimental import pallas as pl
from jax.experimental.pallas import tpu as pltpu
from jax.sharding import PartitionSpec as P

HD = 128
eps = 1e-05
f32 = jnp.float32
bf16 = jnp.bfloat16
MESH = pl.DeviceIdType.MESH
VM = pl.BlockSpec(memory_space=pltpu.VMEM)
HBM = pl.BlockSpec(memory_space=pltpu.HBM)
DMA = pltpu.SemaphoreType.DMA
GRANT = 61000000
PIECES = 4


def cost(us):
    return pl.CostEstimate(flops=us * 10**9, bytes_accessed=us * 3 * 10**6, transcendentals=0)


def mm(a, b):
    return jnp.dot(a, b, preferred_element_type=f32)


def mm_t(a, b):
    return lax.dot_general(a, b, (((1,), (1,)), ((), ())), preferred_element_type=f32)


def t_mm(a, b):
    return lax.dot_general(a, b, (((0,), (0,)), ((), ())), preferred_element_type=f32)


def three(a):
    hi = a.astype(bf16)
    rest = a - hi.astype(f32)
    mid = rest.astype(bf16)
    low = (rest - mid.astype(f32)).astype(bf16)
    return hi, mid, low


def iota(shape, dim):
    return lax.broadcasted_iota(jnp.int32, shape, dim)


def loop(start, stop, body):
    if stop - start <= 8:
        for i in range(start, stop):
            body(i)
    else:
        lax.fori_loop(start, stop, lambda i, _: (body(i), 0)[1], 0)


def others(axis):
    me, n = lax.axis_index(axis), lax.axis_size(axis)
    return [lax.rem(me + d, n) for d in range(1, n)]


def remote(src, dst, send, recv, device):
    return pltpu.make_async_remote_copy(
        src_ref=src, dst_ref=dst, send_sem=send, recv_sem=recv, device_id=device, device_id_type=MESH
    )


def whole_kernel(names, *refs):
    r = types.SimpleNamespace(**dict(zip(names, refs)))
    n, split = lax.axis_size("seq"), lax.axis_size("tp")
    line, groups = n // 2, split // 2
    seq, tp = lax.axis_index("seq"), lax.axis_index("tp")
    z, x = seq // 2, lax.rem(seq, 2)
    hi, lo = tp // 2, lax.rem(tp, 2)
    pair = {"seq": z * 2 + 1 - x}
    core = {"tp": hi * 2 + 1 - lo}
    rest = [lax.rem(hi + e, groups) for e in range(1, groups)]

    def column(g):
        return {"tp": g * 2 + lo}

    def across(g):
        return {"seq": z * 2 + 1 - x, "tp": g * 2 + lo}

    rows, width = r.bytes_in.shape
    heads = r.decay_in.shape[0]
    half = heads // 2
    state_n = r.wbc_in.shape[1] // 2
    p = r.wx_in.shape[1] // heads
    count = r.owner_in.shape[1]
    quarter = width // split
    wide = r.wq_in.shape[0]
    size = wide // split
    part = r.wq_in.shape[1]
    units = part // HD
    cap = r.out_hbm.shape[1]

    fetches = {}
    moves = [
        ("decay", r.decay_in, r.decay),
        ("bytes", r.bytes_in, r.bytes),
        ("wbc", r.wbc_in, r.wbc),
        ("wx", r.wx_in, r.wx),
        ("flags", r.flags_in, r.flags),
        ("wz", r.wz_in, r.wz),
        ("pad", r.pad_in, r.pad),
        ("owner", r.owner_in, r.owner),
        ("wout", r.wout_in, r.wout),
        ("wk", r.wk_in, r.wkv.at[:, pl.ds(0, part)]),
        ("wv", r.wv_in, r.wkv.at[:, pl.ds(part, part)]),
        ("wq", r.wq_in, r.wq),
        ("wo", r.wo_in, r.wo),
    ]
    for i, (name, src, dst) in enumerate(moves):
        fetches[name] = pltpu.make_async_copy(src, dst, r.own.at[i])
        fetches[name].start()

    barrier = pltpu.get_barrier_semaphore()

    def knock(device):
        pl.semaphore_signal(barrier, inc=1, device_id=device, device_id_type=MESH)

    loop(1, n, lambda d: knock({"seq": lax.rem(seq + d, n)}))
    for peer in others("tp"):
        knock({"tp": peer})
    for g in rest:
        knock(across(g))

    fetches["decay"].wait()
    cum_row = r.decay[...]
    lane = iota(cum_row.shape, 1)
    reach = 1
    while reach < rows:
        cum_row = cum_row + jnp.where(lane >= reach, pltpu.roll(cum_row, reach, 1), 0.0)
        reach *= 2
    last = cum_row[:, rows - 1 : rows]
    filler = jnp.zeros((r.tots.shape[1] - heads, state_n), f32)
    r.tots[seq] = jnp.concatenate([jnp.broadcast_to(last, (heads, state_n)), filler], axis=0)
    pl.semaphore_wait(barrier, n - 1 + split - 1 + groups - 1)

    def tot_copy(d):
        return remote(r.tots.at[seq], r.tots.at[seq], r.ts.at[d], r.tr.at[seq], {"seq": lax.rem(seq + d, n)})

    def tot_wait(d):
        peer = lax.rem(seq + d, n)
        remote(r.tots.at[peer], r.tots.at[peer], r.ts.at[d], r.tr.at[peer], pair).wait_recv()

    loop(1, n, lambda d: tot_copy(d).start())

    fetches["bytes"].wait()
    raw = r.bytes[...].astype(f32)
    normed = (raw * lax.rsqrt(jnp.mean(raw * raw, axis=-1, keepdims=True) + eps)).astype(bf16)
    fetches["wbc"].wait()
    bc = mm(normed, r.wbc[...]).astype(bf16)
    bmat, cmat = bc[:, :state_n], bc[:, state_n:]
    fetches["wx"].wait()
    xs = mm(normed, r.wx[...]).astype(bf16)
    cum = jnp.concatenate([cum_row, jnp.zeros((128 - heads, rows), f32)], axis=0).T[:, :heads]
    tail = jnp.exp(cum[rows - 1 : rows, :] - cum)
    for h in range(heads):
        shrunk = (xs[:, h * p : (h + 1) * p].astype(f32) * tail[:, h : h + 1]).astype(bf16)
        state = t_mm(bmat, shrunk)
        r.state[h] = state
        r.state_out[h] = state.astype(bf16)

    def state_copy(h):
        return remote(r.state_out.at[h], r.state_got.at[h], r.s1s.at[h], r.s1r.at[h], pair)

    upward = z < line - 1

    for i in range(half):

        @pl.when((x == 0) | upward)
        def _():
            state_copy((1 - x) * half + i).start()

    @pl.when(x == 0)
    def _():
        for i in range(half):
            state_copy(i).start()

    fetches["wz"].wait()
    gate = mm(normed, r.wz[...])
    gate = gate * jax.nn.sigmoid(gate)
    r.gate[...] = gate
    fetches["flags"].wait()
    flags = r.flags[...]
    upper = (iota((rows, rows), 0) <= iota((rows, rows), 1)).astype(f32).astype(bf16)
    many = jnp.broadcast_to(flags.astype(f32), (16, rows)).astype(bf16)
    rank = mm(many, upper)[0:1, :].astype(jnp.int32) - 1
    hit = (rank == iota((count, rows), 0)) & (flags == 1)
    picker = jnp.where(hit, 1.0, 0.0).astype(bf16)

    def pick(values):
        return sum(mm(picker, piece) for piece in three(values))

    loop(1, n, tot_wait)

    def tot_rows(shard):
        tots = r.tots[shard]
        return [jnp.where(x == 0, tots[i : i + 1], tots[half + i : half + i + 1]) for i in range(half)]

    def slab_copy(d, i):
        return remote(
            r.slab_out.at[i], r.slab_got.at[z, i], r.s2s.at[d, i], r.s2r.at[z, i], {"seq": (z + d) * 2 + x}
        )

    def slab_wait(source, i):
        remote(r.slab_got.at[source, i], r.slab_got.at[source, i], r.s2s.at[0, i], r.s2r.at[source, i], pair).wait_recv()

    @pl.when(upward)
    def _():
        later = tot_rows(z * 2 + 1)
        for i in range(half):
            h = x * half + i
            state_copy(h).wait_recv()
            mine, got = r.state[h], r.state_got[h].astype(f32)
            first, second = jnp.where(x == 0, mine, got), jnp.where(x == 0, got, mine)
            r.slab_out[i] = (first * jnp.exp(later[i]) + second).astype(bf16)

            def reach(k):
                d = line - k

                @pl.when(z + d < line)
                def _():
                    slab_copy(d, i).start()

            loop(1, line, reach)

    middle = rows // 2
    for k in range(2):
        a, b = k * middle, (k + 1) * middle
        inter = mm_t(cmat[a:b], bmat[:b])
        causal = iota((middle, b), 0) + a >= iota((middle, b), 1)
        for h in range(heads):
            spans = cum[a:b, h : h + 1] - cum_row[h : h + 1, :b]
            mixing = (inter * jnp.exp(jnp.where(causal, spans, -1e30))).astype(bf16)
            r.mixed[a:b, h * p : (h + 1) * p] = mm(mixing, xs[:b, h * p : (h + 1) * p])
    mixed_picked = pick(r.mixed[...])
    gate_picked = pick(gate)
    grow_picked = jnp.exp(pick(cum))
    c_picked = mm(picker, cmat).astype(bf16)
    for g in range(groups):
        for k in range(2):
            q = g * 2 + k
            r.base[k, g] = mm(picker, r.bytes[:, q * quarter : (q + 1) * quarter]).astype(bf16)
    fetches["pad"].wait()
    fetches["wk"].wait()
    fetches["wv"].wait()
    fetches["wq"].wait()
    pad = jnp.broadcast_to(r.pad[...].astype(f32).reshape(1, -1), (count, r.pad.shape[0]))
    pad_square = jnp.sum(pad * pad, axis=1, keepdims=True)
    pad = pad.astype(bf16)
    pad_kv = mm(pad[:16], r.wkv[width:, :])[0:1]
    pad_q = mm(pad[:16], r.wq[width:, :])[0:1]
    fetches["owner"].wait()
    owner = r.owner[...]
    ranks = -(-n // 128) * 128
    hot = jnp.where(owner == iota((ranks, count), 0), 1.0, 0.0)
    strict = jnp.where(iota((count, count), 0) < iota((count, count), 1), 1.0, 0.0)
    before = mm(hot.astype(bf16), strict.astype(bf16))
    order = jnp.sum(before * hot, axis=0, keepdims=True).astype(jnp.int32)
    slot = owner * cap + order
    r.place[...] = jnp.where(slot == iota((n * cap, count), 0), 1.0, 0.0).astype(bf16)

    def step(k, carry):
        first, second = tot_rows(k * 2), tot_rows(k * 2 + 1)
        new = []
        for i in range(half):
            slab_wait(k, i)
            new.append(carry[i] * jnp.exp(first[i] + second[i]) + r.slab_got[k, i].astype(f32))
        return tuple(new)

    prefix = lax.fori_loop(0, z, step, tuple(jnp.zeros((state_n, p), f32) for _ in range(half)))

    def prefix_copy(i):
        return remote(r.prefix_out.at[i], r.prefix_got.at[i], r.s3s.at[i], r.s3r.at[i], pair)

    for i in range(half):
        r.prefix_out[i] = prefix[i].astype(bf16)

        @pl.when(z > 0)
        def _():
            prefix_copy(i).start()

    @pl.when(x == 1)
    def _():
        for i in range(half):
            state_copy(i).wait_recv()

    @pl.when((x == 1) & (z == line - 1))
    def _():
        for i in range(half):
            state_copy(half + i).wait_recv()

    tots = r.tots[z * 2]

    def settle(h, i, base, same):
        a, b = tots[i : i + 1], tots[half + i : half + i + 1]
        shrink = jnp.exp(jnp.where((x == 0) == same, a, b))
        moved = base * shrink + r.state_got[h].astype(f32)
        r.start[h] = jnp.where(x == 1, moved, base).astype(bf16)

    for i in range(half):
        settle(x * half + i, i, prefix[i], True)

    @pl.when(z > 0)
    def _():
        for i in range(half):
            prefix_copy(i).wait_recv()

    for i in range(half):
        got = jnp.where(z > 0, r.prefix_got[i].astype(f32), 0.0)
        settle((1 - x) * half + i, i, got, False)

    def finish(mixed, gate, cs, grow):
        scaled = []
        for h in range(heads):
            cols = slice(h * p, (h + 1) * p)
            gated = (mixed[:, cols] + mm(cs, r.start[h]) * grow[:, h : h + 1]) * gate[:, cols]
            norm = lax.rsqrt(jnp.mean(gated * gated, axis=1, keepdims=True) + eps)
            scaled.append((gated * norm).astype(bf16))
        return jnp.concatenate(scaled, axis=1)

    def cols(k, g, n):
        return pl.ds(pl.multiple_of((g * 2 + k) * n, 128), n)

    def core_swap(left, weight, n, send, got, sems):
        for g in range(groups):
            send[g] = mm(left, weight[:, cols(1 - lo, g, n)]).astype(bf16)
        copy = remote(send, got, sems.at[0], sems.at[1], core)
        copy.start()
        return copy

    def line_swap(send, got, sems):
        copies = []
        for e, g in enumerate(rest):
            copy = remote(send.at[g], got.at[hi], sems.at[0, e], sems.at[1, e], column(g))
            copy.start()
            copies.append(copy)
        return copies

    fetches["wout"].wait()
    scaled_picked = finish(mixed_picked, gate_picked, c_picked, grow_picked)
    pick_core = core_swap(scaled_picked, r.wout, quarter, r.d_send, r.d_got, r.d_core)
    mine = [mm(scaled_picked, r.wout[:, cols(lo, g, quarter)]) for g in range(groups)]
    scaled = finish(r.mixed[...], r.gate[...], cmat, jnp.exp(cum))
    pick_core.wait_recv()
    for g in range(groups):
        both = mine[g] + r.d_got[g].astype(f32)
        r.d_sum[g] = both
        r.d_line_send[g] = both.astype(bf16)
    pick_line = line_swap(r.d_line_send, r.d_line_got, r.d_line)
    enc_core = core_swap(scaled, r.wout, quarter, r.e_send, r.e_got, r.e_core)
    for g in range(groups):
        r.e_sum[g] = mm(scaled, r.wout[:, cols(lo, g, quarter)])
    summed = r.base[lo, hi].astype(f32) + r.d_sum[hi]
    for e, g in enumerate(rest):
        pick_line[e].wait_recv()
    for g in rest:
        summed = summed + r.d_line_got[g].astype(f32)
    r.rows[z, lo, x, hi] = summed.astype(bf16)

    def piece(slab, xx, g):
        return r.rows.at[slab, lo, xx, g]

    def up_copy(d):
        here = piece(z, x, hi)
        return remote(here, here, r.gz.at[d], r.gr.at[z, x, hi], {"seq": (z + d) * 2 + x})

    def line_copy(d, e):
        here = piece(z - d, x, hi)
        return remote(here, here, r.gy.at[d, e], r.gr.at[z - d, x, hi], column(rest[e]))

    def pair_copy(d):
        here = piece(z - d, x, hi)
        return remote(here, here, r.gx.at[d], r.gr.at[z - d, x, hi], pair)

    def far_copy(d, e):
        here = piece(z - d, x, hi)
        return remote(here, here, r.gd.at[d, e], r.gr.at[z - d, x, hi], across(rest[e]))

    def core_copy(d, xx):
        here = r.rows.at[z - d, lo, xx]
        return remote(here, here, r.gc.at[d, xx], r.gcr.at[z - d, xx], core)

    def core_wait(d, xx):
        there = r.rows.at[z - d, 1 - lo, xx]
        remote(there, there, r.gc.at[d, xx], r.gcr.at[z - d, xx], core).wait_recv()

    def piece_wait(slab, xx, g):
        here = piece(slab, xx, g)
        remote(here, here, r.gx.at[0], r.gr.at[slab, xx, g], pair).wait_recv()

    def spread(d):
        @pl.when((d > 0) | (x == 0))
        def _():
            for e in range(groups - 1):
                far_copy(d, e).start()
            pair_copy(d).start()

        for e in range(groups - 1):
            line_copy(d, e).start()

    def relay(d):
        for g in rest:
            piece_wait(z - d, x, g)
        core_copy(d, x).start()

        @pl.when((d > 0) | (x == 1))
        def _():
            for g in range(groups):
                piece_wait(z - d, 1 - x, g)
            core_copy(d, 1 - x).start()

    def climb(k):
        d = line - k

        @pl.when(z + d < line)
        def _():
            up_copy(d).start()

    loop(1, line, climb)
    spread(0)
    enc_core.wait_recv()
    for g in range(groups):
        both = r.e_sum[g] + r.e_got[g].astype(f32)
        r.e_sum[g] = both
        r.e_line_send[g] = both.astype(bf16)

    scale = 1.0 / math.sqrt(HD)

    def project(blocks, weight, pads):
        square = sum(jnp.sum(jnp.square(b.astype(f32)), axis=1, keepdims=True) for b in blocks)
        norm = lax.rsqrt((square + pad_square[0:1]) / wide + eps)
        product = sum(mm(b, weight[q * quarter : (q + 1) * quarter, :]) for q, b in enumerate(blocks))
        return ((product + pads) * norm).astype(bf16)

    def attend(blocks, allowed=None):
        kv = project(blocks, r.wkv, pad_kv)
        for h in range(units):
            span = slice(h * HD, (h + 1) * HD)
            scores = mm_t(r.query[:, span], kv[:, span]) * scale
            if allowed is not None:
                scores = jnp.where(allowed, scores, -1e30)
            best = r.best[h]
            top = jnp.maximum(best, jnp.max(scores, axis=1, keepdims=True))
            shrink = jnp.exp(best - top)
            expo = jnp.exp(scores - top)
            r.best[h] = top
            r.total[h] = r.total[h] * shrink + jnp.sum(expo, axis=1, keepdims=True)
            r.accum[h] = r.accum[h] * shrink + mm(expo.astype(bf16), kv[:, part + h * HD : part + (h + 1) * HD])

    def block(xx):
        return [r.rows[z, q % 2, xx, q // 2] for q in range(split)]

    def slab(d):
        return [r.rows[z - d, q % 2, :, q // 2].reshape(2 * count, quarter) for q in range(split)]

    def own_slab():
        core_wait(0, x)
        mine = block(x)
        stream = jnp.concatenate(mine + [pad], axis=1)
        for q in range(split):
            r.stream[q] = stream[:, q * size : (q + 1) * size]
        r.query[...] = project(mine, r.wq, pad_q)
        r.best[...] = jnp.full(r.best.shape, -1e30, f32)
        r.total[...] = jnp.zeros(r.total.shape, f32)
        r.accum[...] = jnp.zeros(r.accum.shape, f32)
        attend(mine, iota((count, count), 0) >= iota((count, count), 1))

        @pl.when(x == 1)
        def _():
            core_wait(0, 0)
            attend(block(0))

    def arrive(d, _):
        piece_wait(z - d, x, hi)
        spread(d)
        return 0

    def turn(d, _):
        @pl.when(d < z)
        def _():
            relay(d + 1)

        core_wait(d, 0)
        core_wait(d, 1)
        attend(slab(d))
        return 0

    relay(0)
    lax.fori_loop(1, z + 1, arrive, 0)
    own_slab()

    @pl.when(z > 0)
    def _():
        relay(1)

    lax.fori_loop(1, z + 1, turn, 0)
    attended = jnp.concatenate([(r.accum[h] / r.total[h]).astype(bf16) for h in range(units)], axis=1)

    fetches["wo"].wait()
    main_core = core_swap(attended, r.wo, size, r.f_send, r.f_got, r.f_core)
    mine = [mm(attended, r.wo[:, cols(lo, g, size)]) for g in range(groups)]
    main_core.wait_recv()
    for g in range(groups):
        both = mine[g] + r.f_got[g].astype(f32)
        r.f_sum[g] = both
        r.f_line_send[g] = both.astype(bf16)
    main_line = line_swap(r.f_line_send, r.f_line_got, r.f_line)
    summed = r.stream[tp].astype(f32) + r.f_sum[hi]
    for copy in main_line:
        copy.wait_recv()
    for g in rest:
        summed = summed + r.f_line_got[g].astype(f32)
    r.send[...] = mm(r.place[...], summed.astype(bf16)).astype(bf16).reshape(n, cap, size)

    def spot(e, source):
        column = (lax.rem(hi - e + groups, groups) * 2 + lo) * size
        return r.out.at[source, :, pl.ds(pl.multiple_of(column, 128), size)]

    def far(d):
        peer = lax.rem(seq + d, n)
        return remote(r.send.at[peer], spot(0, seq), r.hs.at[d], r.hr.at[seq], {"seq": peer})

    def far_wait(source):
        remote(spot(0, source), spot(0, source), r.hs.at[0], r.hr.at[source], pair).wait_recv()

    def direct(e, source):
        here = spot(0, source)
        return remote(here, here, r.hys.at[e, source], r.hyr.at[e, source], {"tp": lax.rem(hi + e, groups) * 2 + lo})

    def beside(e, source):
        here = spot(e, source)
        return remote(here, here, r.hcs.at[e, source], r.hcr.at[e, source], core)

    def pass_on(source):
        for e in range(1, groups):
            direct(e, source).start()
        beside(0, source).start()

    def pass_across(source):
        for e in range(1, groups):
            direct(e, source).wait_recv()
            beside(e, source).start()

    def other(k):
        return k + jnp.where(k >= seq, 1, 0)

    loop(1, n, lambda d: far(n - d).start())
    enc_line = line_swap(r.e_line_send, r.e_line_got, r.e_line)
    r.out[seq, :, pl.ds(pl.multiple_of(tp * size, 128), size)] = r.send[seq]
    pass_on(seq)

    def deliver(k):
        far_wait(other(k))
        pass_on(other(k))

    loop(0, n - 1, deliver)
    pass_across(seq)
    loop(0, n - 1, lambda k: pass_across(other(k)))
    for copy in enc_line:
        copy.wait_recv()
    enc = r.bytes[:, pl.ds(pl.multiple_of(tp * quarter, 128), quarter)].astype(f32) + r.e_sum[hi]
    for g in rest:
        enc = enc + r.e_line_got[g].astype(f32)
    r.enc[...] = enc.astype(bf16)
    enc_write = pltpu.make_async_copy(r.enc, r.enc_hbm, r.enc_sem)
    enc_write.start()
    def close(d):
        for e in range(groups):
            beside(e, d).wait_recv()
            beside(e, d).wait_send()
            if e > 0:
                direct(e, d).wait_send()
        write(d).start()

    def write(d):
        return pltpu.make_async_copy(r.out.at[d], r.out_hbm.at[d], r.out_sems.at[d])

    loop(0, n, close)
    loop(1, n, lambda d: far(d).wait_send())
    loop(1, n, lambda d: tot_copy(d).wait_send())
    for copy in [pick_core, enc_core, main_core] + pick_line + enc_line + main_line:
        copy.wait_send()
    for i in range(half):

        @pl.when((x == 0) | upward)
        def _():
            state_copy((1 - x) * half + i).wait_send()

        @pl.when(x == 0)
        def _():
            state_copy(i).wait_send()

        @pl.when(z > 0)
        def _():
            prefix_copy(i).wait_send()

    def close_up(d):
        @pl.when(z + d < line)
        def _():
            up_copy(d).wait_send()
            for i in range(half):
                slab_copy(d, i).wait_send()

    loop(1, line, close_up)

    def close_row(d, _):
        for e in range(groups - 1):
            line_copy(d, e).wait_send()
        core_copy(d, x).wait_send()

        @pl.when((d > 0) | (x == 0))
        def _():
            for e in range(groups - 1):
                far_copy(d, e).wait_send()
            pair_copy(d).wait_send()

        @pl.when((d > 0) | (x == 1))
        def _():
            core_copy(d, 1 - x).wait_send()

        return 0

    lax.fori_loop(0, z + 1, close_row, 0)
    enc_write.wait()
    loop(0, n, lambda d: write(d).wait())


def hand_out(enc_ref, main_ref, enc_out, main_out, enc, main, sems):
    ways = []
    for i, (src, through, dst) in enumerate(((main_ref, main, main_out), (enc_ref, enc, enc_out))):
        step = src.shape[0] // PIECES
        for j in range(PIECES):
            span = pl.ds(j * step, step)
            fetch = pltpu.make_async_copy(src.at[span], through.at[span], sems.at[0, i, j])
            ways.append((fetch, pltpu.make_async_copy(through.at[span], dst.at[span], sems.at[1, i, j])))
    for fetch, _ in ways:
        fetch.start()
    for fetch, write in ways:
        fetch.wait()
        write.start()
    for _, write in ways:
        write.wait()


def on_device(
    byte_states, flags, stretch_owner, log_decay, w_x, w_z, w_bc, w_out, pad_vector, w_q, w_k, w_v, w_o
):
    rows, width = byte_states.shape
    heads = log_decay.shape[1]
    inner = w_x.shape[1]
    p = inner // heads
    state_n = w_bc.shape[1] // 2
    n = lax.axis_size("seq")
    split = lax.axis_size("tp")
    line, groups, half = n // 2, split // 2, heads // 2
    count = stretch_owner.shape[0]
    quarter = width // split
    cap = max(2, 2 * count // n)
    wide, part = w_q.shape
    size = wide // split
    units = part // HD
    shape = jax.ShapeDtypeStruct
    args = dict(
        bytes_in=byte_states, flags_in=flags.reshape(1, rows), owner_in=stretch_owner.reshape(1, count),
        decay_in=log_decay.T, wx_in=w_x, wz_in=w_z, wbc_in=w_bc, wout_in=w_out, pad_in=pad_vector,
        wq_in=w_q, wk_in=w_k, wv_in=w_v, wo_in=w_o,
    )
    outs = dict(enc_hbm=shape((rows, quarter), bf16), out_hbm=shape((n, cap, wide), bf16))

    def wide_vmem(*dims):
        return pltpu.VMEM(dims, f32)

    def vmem(*dims):
        return pltpu.VMEM(dims, bf16)

    others_n = max(groups - 1, 1)
    scratch = dict(
        bytes=vmem(rows, width), flags=pltpu.VMEM((1, rows), jnp.int32), owner=pltpu.VMEM((1, count), jnp.int32),
        decay=wide_vmem(heads, rows), wx=vmem(*w_x.shape), wz=vmem(*w_z.shape), wbc=vmem(*w_bc.shape),
        wout=vmem(*w_out.shape), pad=vmem(*pad_vector.shape), wq=vmem(*w_q.shape), wkv=vmem(wide, 2 * part),
        wo=vmem(*w_o.shape), own=DMA((len(args),)),
        tots=wide_vmem(n, -(-heads // 8) * 8, state_n), ts=DMA((n,)), tr=DMA((n,)),
        state=wide_vmem(heads, state_n, p), state_out=vmem(heads, state_n, p), state_got=vmem(heads, state_n, p),
        s1s=DMA((heads,)), s1r=DMA((heads,)),
        slab_out=vmem(half, state_n, p), slab_got=vmem(line, half, state_n, p),
        s2s=DMA((line, half)), s2r=DMA((line, half)),
        prefix_out=vmem(half, state_n, p), prefix_got=vmem(half, state_n, p), s3s=DMA((half,)), s3r=DMA((half,)),
        start=vmem(heads, state_n, p), gate=wide_vmem(rows, inner), mixed=wide_vmem(rows, inner),
        base=vmem(2, groups, count, quarter), place=vmem(n * cap, count),
        d_send=vmem(groups, count, quarter), d_got=vmem(groups, count, quarter), d_core=DMA((2,)),
        d_sum=wide_vmem(groups, count, quarter), d_line_send=vmem(groups, count, quarter),
        d_line_got=vmem(groups, count, quarter), d_line=DMA((2, others_n)),
        e_send=vmem(groups, rows, quarter), e_got=vmem(groups, rows, quarter), e_core=DMA((2,)),
        e_sum=wide_vmem(groups, rows, quarter), e_line_send=vmem(groups, rows, quarter),
        e_line_got=vmem(groups, rows, quarter), e_line=DMA((2, others_n)),
        f_send=vmem(groups, count, size), f_got=vmem(groups, count, size), f_core=DMA((2,)),
        f_sum=wide_vmem(groups, count, size), f_line_send=vmem(groups, count, size),
        f_line_got=vmem(groups, count, size), f_line=DMA((2, others_n)),
        rows=vmem(line, 2, 2, groups, count, quarter), gr=DMA((line, 2, groups)), gcr=DMA((line, 2)),
        gz=DMA((line,)), gx=DMA((line,)), gy=DMA((line, others_n)), gd=DMA((line, others_n)), gc=DMA((line, 2)),
        stream=vmem(split, count, size), query=vmem(count, part),
        best=wide_vmem(units, count, 1), total=wide_vmem(units, count, 1), accum=wide_vmem(units, count, HD),
        enc=vmem(rows, quarter), enc_sem=DMA, out=vmem(n, cap, wide), out_sems=DMA((n,)),
        send=vmem(n, cap, size), hs=DMA((n,)), hr=DMA((n,)),
        hys=DMA((groups, n)), hyr=DMA((groups, n)), hcs=DMA((groups, n)), hcr=DMA((groups, n)),
    )
    results = pl.pallas_call(
        functools.partial(whole_kernel, list(args) + list(outs) + list(scratch)),
        out_shape=list(outs.values()),
        in_specs=[HBM] * len(args),
        out_specs=[HBM] * len(outs),
        scratch_shapes=list(scratch.values()),
        cost_estimate=cost(60),
        compiler_params=pltpu.CompilerParams(
            collective_id=0, has_side_effects=True, vmem_limit_bytes=GRANT
        ),
    )(*args.values())
    enc_out, main_out = pl.pallas_call(
        hand_out,
        out_shape=list(outs.values()),
        in_specs=[HBM] * len(outs),
        out_specs=[HBM] * len(outs),
        scratch_shapes=[pltpu.VMEM(o.shape, o.dtype) for o in outs.values()] + [DMA((2, 2, PIECES))],
        cost_estimate=cost(1),
        compiler_params=pltpu.CompilerParams(vmem_limit_bytes=GRANT),
    )(*results)
    return (enc_out, main_out.reshape(n * cap, wide))


def solution(mesh):
    placed = (
        P("seq", None),
        P("seq"),
        P("seq", None),
        P("seq", "tp"),
        P(None, "tp"),
        P(None, "tp"),
        P(),
        P("tp", None),
        P(),
        P(None, "tp"),
        P(None, "tp"),
        P(None, "tp"),
        P("tp", None),
    )
    return jax.shard_map(
        on_device,
        mesh=mesh,
        in_specs=placed,
        out_specs=(P("seq", "tp"), P("seq", None)),
        check_vma=False,
    )
```

```python
import functools
import math
import types

import jax
import jax.numpy as jnp
from jax import lax
from jax.experimental import pallas as pl
from jax.experimental.pallas import tpu as pltpu
from jax.sharding import PartitionSpec as P

HD = 128
eps = 1e-05
f32 = jnp.float32
bf16 = jnp.bfloat16
MESH = pl.DeviceIdType.MESH
VM = pl.BlockSpec(memory_space=pltpu.VMEM)
HBM = pl.BlockSpec(memory_space=pltpu.HBM)
DMA = pltpu.SemaphoreType.DMA
GRANT = 61000000
PIECES = 4


def cost(us):
    return pl.CostEstimate(flops=us * 10**9, bytes_accessed=us * 3 * 10**6, transcendentals=0)


def mm(a, b):
    return jnp.dot(a, b, preferred_element_type=f32)


def mm_t(a, b):
    return lax.dot_general(a, b, (((1,), (1,)), ((), ())), preferred_element_type=f32)


def t_mm(a, b):
    return lax.dot_general(a, b, (((0,), (0,)), ((), ())), preferred_element_type=f32)


def three(a):
    hi = a.astype(bf16)
    rest = a - hi.astype(f32)
    mid = rest.astype(bf16)
    low = (rest - mid.astype(f32)).astype(bf16)
    return hi, mid, low


def iota(shape, dim):
    return lax.broadcasted_iota(jnp.int32, shape, dim)


def loop(start, stop, body):
    if stop - start <= 8:
        for i in range(start, stop):
            body(i)
    else:
        lax.fori_loop(start, stop, lambda i, _: (body(i), 0)[1], 0)


def others(axis):
    me, n = lax.axis_index(axis), lax.axis_size(axis)
    return [lax.rem(me + d, n) for d in range(1, n)]


def remote(src, dst, send, recv, device):
    return pltpu.make_async_remote_copy(
        src_ref=src, dst_ref=dst, send_sem=send, recv_sem=recv, device_id=device, device_id_type=MESH
    )


def whole_kernel(names, *refs):
    r = types.SimpleNamespace(**dict(zip(names, refs)))
    n, split = lax.axis_size("seq"), lax.axis_size("tp")
    line, groups = n // 2, split // 2
    seq, tp = lax.axis_index("seq"), lax.axis_index("tp")
    z, x = seq // 2, lax.rem(seq, 2)
    hi, lo = tp // 2, lax.rem(tp, 2)
    pair = {"seq": z * 2 + 1 - x}
    core = {"tp": hi * 2 + 1 - lo}
    rest = [lax.rem(hi + e, groups) for e in range(1, groups)]

    def column(g):
        return {"tp": g * 2 + lo}

    def across(g):
        return {"seq": z * 2 + 1 - x, "tp": g * 2 + lo}

    rows, width = r.bytes_in.shape
    heads = r.decay_in.shape[0]
    half = heads // 2
    state_n = r.wbc_in.shape[1] // 2
    p = r.wx_in.shape[1] // heads
    count = r.owner_in.shape[1]
    quarter = width // split
    wide = r.wq_in.shape[0]
    size = wide // split
    part = r.wq_in.shape[1]
    units = part // HD
    cap = r.out_hbm.shape[1]

    fetches = {}
    moves = [
        ("decay", r.decay_in, r.decay),
        ("bytes", r.bytes_in, r.bytes),
        ("wbc", r.wbc_in, r.wbc),
        ("wx", r.wx_in, r.wx),
        ("flags", r.flags_in, r.flags),
        ("wz", r.wz_in, r.wz),
        ("pad", r.pad_in, r.pad),
        ("owner", r.owner_in, r.owner),
        ("wout", r.wout_in, r.wout),
        ("wk", r.wk_in, r.wkv.at[:, pl.ds(0, part)]),
        ("wv", r.wv_in, r.wkv.at[:, pl.ds(part, part)]),
        ("wq", r.wq_in, r.wq),
        ("wo", r.wo_in, r.wo),
    ]
    for i, (name, src, dst) in enumerate(moves):
        fetches[name] = pltpu.make_async_copy(src, dst, r.own.at[i])
        fetches[name].start()

    barrier = pltpu.get_barrier_semaphore()

    def knock(device):
        pl.semaphore_signal(barrier, inc=1, device_id=device, device_id_type=MESH)

    loop(1, n, lambda d: knock({"seq": lax.rem(seq + d, n)}))
    for peer in others("tp"):
        knock({"tp": peer})
    for g in rest:
        knock(across(g))

    for name in ("decay", "bytes", "wbc", "wx"):
        fetches[name].wait()
    cum_row = r.decay[...]
    lane = iota(cum_row.shape, 1)
    reach = 1
    while reach < rows:
        cum_row = cum_row + jnp.where(lane >= reach, pltpu.roll(cum_row, reach, 1), 0.0)
        reach *= 2
    last = cum_row[:, rows - 1 : rows]
    filler = jnp.zeros((r.tots.shape[1] - heads, state_n), f32)
    r.tots[seq] = jnp.concatenate([jnp.broadcast_to(last, (heads, state_n)), filler], axis=0)
    def tot_copy(d):
        return remote(r.tots.at[seq], r.tots.at[seq], r.ts.at[d], r.tr.at[seq], {"seq": lax.rem(seq + d, n)})

    def tot_wait(d):
        peer = lax.rem(seq + d, n)
        remote(r.tots.at[peer], r.tots.at[peer], r.ts.at[d], r.tr.at[peer], pair).wait_recv()

    raw = r.bytes[...]
    norm = lax.rsqrt(jnp.mean(jnp.square(raw.astype(f32)), axis=-1, keepdims=True) + eps)
    bc = (mm(raw, r.wbc[...]) * norm).astype(bf16)
    bmat, cmat = bc[:, :state_n], bc[:, state_n:]
    xs = (mm(raw, r.wx[...]) * norm).astype(bf16)
    cum = jnp.concatenate([cum_row, jnp.zeros((128 - heads, rows), f32)], axis=0).T[:, :heads]
    tail = jnp.exp(cum[rows - 1 : rows, :] - cum)
    for h in range(heads):
        shrunk = (xs[:, h * p : (h + 1) * p].astype(f32) * tail[:, h : h + 1]).astype(bf16)
        state = t_mm(bmat, shrunk)
        r.state[h] = state
        r.state_out[h] = state.astype(bf16)

    def state_copy(h):
        return remote(r.state_out.at[h], r.state_got.at[h], r.s1s.at[h], r.s1r.at[h], pair)

    upward = z < line - 1
    pl.semaphore_wait(barrier, n - 1 + split - 1 + groups - 1)
    loop(1, n, lambda d: tot_copy(d).start())

    for i in range(half):

        @pl.when((x == 0) | upward)
        def _():
            state_copy((1 - x) * half + i).start()

    @pl.when(x == 0)
    def _():
        for i in range(half):
            state_copy(i).start()

    fetches["wz"].wait()
    gate = mm(raw, r.wz[...]) * norm
    gate = gate * jax.nn.sigmoid(gate)
    r.gate[...] = gate
    fetches["flags"].wait()
    flags = r.flags[...]
    upper = (iota((rows, rows), 0) <= iota((rows, rows), 1)).astype(f32).astype(bf16)
    many = jnp.broadcast_to(flags.astype(f32), (16, rows)).astype(bf16)
    rank = mm(many, upper)[0:1, :].astype(jnp.int32) - 1
    hit = (rank == iota((count, rows), 0)) & (flags == 1)
    picker = jnp.where(hit, 1.0, 0.0).astype(bf16)

    def pick(values):
        return sum(mm(picker, piece) for piece in three(values))

    loop(1, n, tot_wait)

    def tot_rows(shard):
        tots = r.tots[shard]
        return [jnp.where(x == 0, tots[i : i + 1], tots[half + i : half + i + 1]) for i in range(half)]

    def slab_copy(d, i):
        return remote(
            r.slab_out.at[i], r.slab_got.at[z, i], r.s2s.at[d, i], r.s2r.at[z, i], {"seq": (z + d) * 2 + x}
        )

    def slab_wait(source, i):
        remote(r.slab_got.at[source, i], r.slab_got.at[source, i], r.s2s.at[0, i], r.s2r.at[source, i], pair).wait_recv()

    @pl.when(upward)
    def _():
        later = tot_rows(z * 2 + 1)
        for i in range(half):
            h = x * half + i
            state_copy(h).wait_recv()
            mine, got = r.state[h], r.state_got[h].astype(f32)
            first, second = jnp.where(x == 0, mine, got), jnp.where(x == 0, got, mine)
            r.slab_out[i] = (first * jnp.exp(later[i]) + second).astype(bf16)

            def reach(d):
                @pl.when(z + d < line)
                def _():
                    slab_copy(d, i).start()

            loop(1, line, reach)


    middle = rows // 2
    for k in range(2):
        a, b = k * middle, (k + 1) * middle
        inter = mm_t(cmat[a:b], bmat[:b])
        causal = iota((middle, b), 0) + a >= iota((middle, b), 1)
        for h in range(heads):
            spans = cum[a:b, h : h + 1] - cum_row[h : h + 1, :b]
            mixing = (inter * jnp.exp(jnp.where(causal, spans, -1e30))).astype(bf16)
            r.mixed[a:b, h * p : (h + 1) * p] = mm(mixing, xs[:b, h * p : (h + 1) * p])
    mixed_picked = pick(r.mixed[...])
    gate_picked = pick(gate)
    grow_picked = jnp.exp(pick(cum))
    c_picked = mm(picker, cmat).astype(bf16)
    for g in range(groups):
        for k in range(2):
            q = g * 2 + k
            r.base[k, g] = mm(picker, r.bytes[:, q * quarter : (q + 1) * quarter]).astype(bf16)
    fetches["pad"].wait()
    fetches["wk"].wait()
    fetches["wv"].wait()
    fetches["wq"].wait()
    pad = jnp.broadcast_to(r.pad[...].astype(f32).reshape(1, -1), (count, r.pad.shape[0]))
    pad_square = jnp.sum(pad * pad, axis=1, keepdims=True)
    pad = pad.astype(bf16)
    pad_kv = mm(pad[:16], r.wkv[width:, :])[0:1]
    pad_q = mm(pad[:16], r.wq[width:, :])[0:1]
    fetches["owner"].wait()
    owner = r.owner[...]
    ranks = -(-n // 128) * 128
    hot = jnp.where(owner == iota((ranks, count), 0), 1.0, 0.0)
    strict = jnp.where(iota((count, count), 0) < iota((count, count), 1), 1.0, 0.0)
    before = mm(hot.astype(bf16), strict.astype(bf16))
    order = jnp.sum(before * hot, axis=0, keepdims=True).astype(jnp.int32)
    slot = owner * cap + order
    r.place[...] = jnp.where(slot == iota((n * cap, count), 0), 1.0, 0.0).astype(bf16)

    def prefix_copy(i):
        return remote(r.prefix_out.at[i], r.prefix_got.at[i], r.s3s.at[i], r.s3r.at[i], pair)

    prefix = []
    for i in range(half):

        def step(k, carry):
            moved = jnp.exp(tot_rows(k * 2)[i] + tot_rows(k * 2 + 1)[i])
            slab_wait(k, i)
            return carry * moved + r.slab_got[k, i].astype(f32)

        prefix.append(lax.fori_loop(0, z, step, jnp.zeros((state_n, p), f32)))
        r.prefix_out[i] = prefix[i].astype(bf16)

        @pl.when(z > 0)
        def _():
            prefix_copy(i).start()


    @pl.when(x == 1)
    def _():
        for i in range(half):
            state_copy(i).wait_recv()

    @pl.when((x == 1) & (z == line - 1))
    def _():
        for i in range(half):
            state_copy(half + i).wait_recv()

    tots = r.tots[z * 2]

    def settle(h, i, base, same):
        a, b = tots[i : i + 1], tots[half + i : half + i + 1]
        shrink = jnp.exp(jnp.where((x == 0) == same, a, b))
        moved = base * shrink + r.state_got[h].astype(f32)
        r.start[h] = jnp.where(x == 1, moved, base).astype(bf16)

    for i in range(half):
        settle(x * half + i, i, prefix[i], True)

    @pl.when(z > 0)
    def _():
        for i in range(half):
            prefix_copy(i).wait_recv()

    for i in range(half):
        got = jnp.where(z > 0, r.prefix_got[i].astype(f32), 0.0)
        settle((1 - x) * half + i, i, got, False)

    def finish(mixed, gate, cs, grow):
        scaled = []
        for h in range(heads):
            cols = slice(h * p, (h + 1) * p)
            gated = (mixed[:, cols] + mm(cs, r.start[h]) * grow[:, h : h + 1]) * gate[:, cols]
            norm = lax.rsqrt(jnp.mean(gated * gated, axis=1, keepdims=True) + eps)
            scaled.append((gated * norm).astype(bf16))
        return jnp.concatenate(scaled, axis=1)

    def cols(k, g, n):
        return pl.ds(pl.multiple_of((g * 2 + k) * n, 128), n)

    def core_swap(left, weight, n, send, got, sems):
        for g in range(groups):
            send[g] = mm(left, weight[:, cols(1 - lo, g, n)]).astype(bf16)
        copy = remote(send, got, sems.at[0], sems.at[1], core)
        copy.start()
        return copy

    def line_copies(send, got, sems):
        return [
            remote(send.at[g], got.at[hi], sems.at[0, e], sems.at[1, e], column(g))
            for e, g in enumerate(rest)
        ]

    def line_swap(*refs):
        copies = line_copies(*refs)
        for copy in copies:
            copy.start()
        return copies

    fetches["wout"].wait()
    scaled_picked = finish(mixed_picked, gate_picked, c_picked, grow_picked)
    pick_core = core_swap(scaled_picked, r.wout, quarter, r.d_send, r.d_got, r.d_core)
    mine = [mm(scaled_picked, r.wout[:, cols(lo, g, quarter)]) for g in range(groups)]
    scaled = finish(r.mixed[...], r.gate[...], cmat, jnp.exp(cum))
    pick_core.wait_recv()
    for g in range(groups):
        both = mine[g] + r.d_got[g].astype(f32)
        r.d_sum[g] = both
        r.d_line_send[g] = both.astype(bf16)
    pick_line = line_swap(r.d_line_send, r.d_line_got, r.d_line)
    enc_core = core_swap(scaled, r.wout, quarter, r.e_send, r.e_got, r.e_core)
    for g in range(groups):
        r.e_sum[g] = mm(scaled, r.wout[:, cols(lo, g, quarter)])
    summed = r.base[lo, hi].astype(f32) + r.d_sum[hi]
    for e, g in enumerate(rest):
        pick_line[e].wait_recv()
    for g in rest:
        summed = summed + r.d_line_got[g].astype(f32)
    r.rows[z, lo, x, hi] = summed.astype(bf16)

    def piece(slab, xx, g):
        return r.rows.at[slab, lo, xx, g]

    def up_copy(d):
        here = piece(z, x, hi)
        return remote(here, here, r.gz.at[d], r.gr.at[z, x, hi], {"seq": (z + d) * 2 + x})

    def line_copy(d, e):
        here = piece(z - d, x, hi)
        return remote(here, here, r.gy.at[d, e], r.gr.at[z - d, x, hi], column(rest[e]))

    def pair_copy(d):
        here = piece(z - d, x, hi)
        return remote(here, here, r.gx.at[d], r.gr.at[z - d, x, hi], pair)

    def far_copy(d, e):
        here = piece(z - d, x, hi)
        return remote(here, here, r.gd.at[d, e], r.gr.at[z - d, x, hi], across(rest[e]))

    def core_copy(d, xx):
        here = r.rows.at[z - d, lo, xx]
        return remote(here, here, r.gc.at[d, xx], r.gcr.at[z - d, xx], core)

    def core_wait(d, xx):
        there = r.rows.at[z - d, 1 - lo, xx]
        remote(there, there, r.gc.at[d, xx], r.gcr.at[z - d, xx], core).wait_recv()

    def piece_wait(slab, xx, g):
        here = piece(slab, xx, g)
        remote(here, here, r.gx.at[0], r.gr.at[slab, xx, g], pair).wait_recv()

    def spread(d):
        @pl.when((d > 0) | (x == 0))
        def _():
            for e in range(groups - 1):
                far_copy(d, e).start()
            pair_copy(d).start()

        for e in range(groups - 1):
            line_copy(d, e).start()

    def relay_own(d):
        for g in rest:
            piece_wait(z - d, x, g)
        core_copy(d, x).start()

    def relay_pair(d):
        @pl.when((d > 0) | (x == 1))
        def _():
            for g in range(groups):
                piece_wait(z - d, 1 - x, g)
            core_copy(d, 1 - x).start()

    def relay(d):
        relay_own(d)
        relay_pair(d)

        @pl.when(d == z - 1)
        def _():
            for copy in enc_line:
                copy.start()

    def climb(k):
        d = line - k

        @pl.when(z + d < line)
        def _():
            up_copy(d).start()

    enc_line = line_copies(r.e_line_send, r.e_line_got, r.e_line)
    loop(1, line, climb)
    spread(0)
    enc_core.wait_recv()
    for g in range(groups):
        both = r.e_sum[g] + r.e_got[g].astype(f32)
        r.e_sum[g] = both
        r.e_line_send[g] = both.astype(bf16)

    scale = 1.0 / math.sqrt(HD)

    def project(blocks, weight, pads, factor=1.0):
        square = jnp.sum(sum(jnp.square(b.astype(f32)) for b in blocks), axis=1, keepdims=True)
        norm = lax.rsqrt((square + pad_square[0:1]) / wide + eps) * factor
        return ((mm(jnp.concatenate(blocks, axis=1), weight[:width, :]) + pads) * norm).astype(bf16)

    def attend(blocks, allowed=None):
        kv = project(blocks, r.wkv, pad_kv)
        for h in range(units):
            span = slice(h * HD, (h + 1) * HD)
            scores = mm_t(r.query[:, span], kv[:, span])
            if allowed is not None:
                scores = jnp.where(allowed, scores, -1e30)
            best = r.best[h]
            top = jnp.maximum(best, jnp.max(scores, axis=1, keepdims=True))
            shrink = jnp.exp(best - top)
            expo = jnp.exp(scores - top)
            r.best[h] = top
            r.total[h] = r.total[h] * shrink + jnp.sum(expo, axis=1, keepdims=True)
            r.accum[h] = r.accum[h] * shrink + mm(expo.astype(bf16), kv[:, part + h * HD : part + (h + 1) * HD])

    def block(xx):
        return [r.rows[z, q % 2, xx, q // 2] for q in range(split)]

    def slab(d):
        return [r.rows[z - d, q % 2, :, q // 2].reshape(2 * count, quarter) for q in range(split)]

    def own_slab():
        core_wait(0, x)
        mine = block(x)
        stream = jnp.concatenate(mine + [pad], axis=1)
        for q in range(split):
            r.stream[q] = stream[:, q * size : (q + 1) * size]
        r.query[...] = project(mine, r.wq, pad_q, scale)
        r.best[...] = jnp.full(r.best.shape, -1e30, f32)
        r.total[...] = jnp.zeros(r.total.shape, f32)
        r.accum[...] = jnp.zeros(r.accum.shape, f32)
        attend(mine, iota((count, count), 0) >= iota((count, count), 1))

    def own_pair():
        core_wait(0, 0)
        attend(block(0))

    def arrive(d, _):
        piece_wait(z - d, x, hi)
        spread(d)
        return 0

    def turn(d, _):
        @pl.when(d < z)
        def _():
            relay(d + 1)

        core_wait(d, 0)
        core_wait(d, 1)
        attend(slab(d))
        return 0

    lax.fori_loop(1, z + 1, arrive, 0)
    relay_own(0)
    own_slab()
    relay_pair(0)

    @pl.when(z <= 1)
    def _():
        for copy in enc_line:
            copy.start()


    @pl.when(z > 0)
    def _():
        relay(1)


    @pl.when(x == 1)
    def _():
        own_pair()

    lax.fori_loop(1, z + 1, turn, 0)
    attended = jnp.concatenate([(r.accum[h] / r.total[h]).astype(bf16) for h in range(units)], axis=1)

    fetches["wo"].wait()
    main_core = core_swap(attended, r.wo, size, r.f_send, r.f_got, r.f_core)
    mine = [mm(attended, r.wo[:, cols(lo, g, size)]) for g in range(groups)]
    main_core.wait_recv()
    for g in range(groups):
        both = mine[g] + r.f_got[g].astype(f32)
        r.f_sum[g] = both
        r.f_line_send[g] = both.astype(bf16)
    main_line = line_swap(r.f_line_send, r.f_line_got, r.f_line)
    summed = r.stream[tp].astype(f32) + r.f_sum[hi]
    for copy in main_line:
        copy.wait_recv()
    for g in rest:
        summed = summed + r.f_line_got[g].astype(f32)
    r.send[...] = mm(r.place[...], summed.astype(bf16)).astype(bf16).reshape(n, cap, size)

    def spot(e, source):
        column = (lax.rem(hi - e + groups, groups) * 2 + lo) * size
        return r.out.at[source, :, pl.ds(pl.multiple_of(column, 128), size)]

    def far(peer):
        return remote(r.send.at[peer], spot(0, seq), r.hs.at[peer], r.hr.at[seq], {"seq": peer})

    def far_wait(source):
        remote(spot(0, source), spot(0, source), r.hs.at[0], r.hr.at[source], pair).wait_recv()

    def direct(e, source):
        here = spot(0, source)
        return remote(here, here, r.hys.at[e, source], r.hyr.at[e, source], {"tp": lax.rem(hi + e, groups) * 2 + lo})

    def beside(e, source):
        here = spot(e, source)
        return remote(here, here, r.hcs.at[e, source], r.hcr.at[e, source], core)

    def pass_on(source):
        for e in range(1, groups):
            direct(e, source).start()
        beside(0, source).start()

    def pass_across(source):
        for e in range(1, groups):
            direct(e, source).wait_recv()
            beside(e, source).start()

    def other(k):
        return k + jnp.where(k >= seq, 1, 0)

    loop(0, n - 1, lambda k: far(other(k)).start())
    r.out[seq, :, pl.ds(pl.multiple_of(tp * size, 128), size)] = r.send[seq]
    pass_on(seq)

    loop(1, n, lambda d: tot_copy(d).wait_send())
    for copy in [pick_core, enc_core, main_core] + pick_line + enc_line + main_line:
        copy.wait_send()
    for i in range(half):

        @pl.when((x == 0) | upward)
        def _():
            state_copy((1 - x) * half + i).wait_send()

        @pl.when(x == 0)
        def _():
            state_copy(i).wait_send()

        @pl.when(z > 0)
        def _():
            prefix_copy(i).wait_send()

    def close_up(d):
        @pl.when(z + d < line)
        def _():
            up_copy(d).wait_send()
            for i in range(half):
                slab_copy(d, i).wait_send()

    loop(1, line, close_up)

    def close_row(d, _):
        for e in range(groups - 1):
            line_copy(d, e).wait_send()
        core_copy(d, x).wait_send()

        @pl.when((d > 0) | (x == 0))
        def _():
            for e in range(groups - 1):
                far_copy(d, e).wait_send()
            pair_copy(d).wait_send()

        @pl.when((d > 0) | (x == 1))
        def _():
            core_copy(d, 1 - x).wait_send()

        return 0

    lax.fori_loop(0, z + 1, close_row, 0)

    def deliver(k):
        far_wait(other(k))
        pass_on(other(k))

    loop(0, n - 1, deliver)
    pass_across(seq)
    loop(0, n - 1, lambda k: pass_across(other(k)))
    for copy in enc_line:
        copy.wait_recv()
    enc = r.bytes[:, pl.ds(pl.multiple_of(tp * quarter, 128), quarter)].astype(f32) + r.e_sum[hi]
    for g in rest:
        enc = enc + r.e_line_got[g].astype(f32)
    r.enc[...] = enc.astype(bf16)
    enc_write = pltpu.make_async_copy(r.enc, r.enc_hbm, r.enc_sem)
    enc_write.start()
    def close(d):
        for e in range(groups):
            beside(e, d).wait_recv()
            beside(e, d).wait_send()
            if e > 0:
                direct(e, d).wait_send()
        write(d).start()

    def write(d):
        return pltpu.make_async_copy(r.out.at[d], r.out_hbm.at[d], r.out_sems.at[d])

    loop(0, n, close)
    loop(0, n - 1, lambda k: far(other(k)).wait_send())
    enc_write.wait()
    loop(0, n, lambda d: write(d).wait())

def hand_out(enc_ref, main_ref, enc_out, main_out, enc, main, sems):
    ways = []
    for i, (src, through, dst) in enumerate(((main_ref, main, main_out), (enc_ref, enc, enc_out))):
        step = src.shape[0] // PIECES
        for j in range(PIECES):
            span = pl.ds(j * step, step)
            fetch = pltpu.make_async_copy(src.at[span], through.at[span], sems.at[0, i, j])
            ways.append((fetch, pltpu.make_async_copy(through.at[span], dst.at[span], sems.at[1, i, j])))
    for fetch, _ in ways:
        fetch.start()
    for fetch, write in ways:
        fetch.wait()
        write.start()
    for _, write in ways:
        write.wait()


def on_device(
    byte_states, flags, stretch_owner, log_decay, w_x, w_z, w_bc, w_out, pad_vector, w_q, w_k, w_v, w_o
):
    rows, width = byte_states.shape
    heads = log_decay.shape[1]
    inner = w_x.shape[1]
    p = inner // heads
    state_n = w_bc.shape[1] // 2
    n = lax.axis_size("seq")
    split = lax.axis_size("tp")
    line, groups, half = n // 2, split // 2, heads // 2
    count = stretch_owner.shape[0]
    quarter = width // split
    cap = max(2, 2 * count // n)
    wide, part = w_q.shape
    size = wide // split
    units = part // HD
    shape = jax.ShapeDtypeStruct
    args = dict(
        bytes_in=byte_states, flags_in=flags.reshape(1, rows), owner_in=stretch_owner.reshape(1, count),
        decay_in=log_decay.T, wx_in=w_x, wz_in=w_z, wbc_in=w_bc, wout_in=w_out, pad_in=pad_vector,
        wq_in=w_q, wk_in=w_k, wv_in=w_v, wo_in=w_o,
    )
    outs = dict(enc_hbm=shape((rows, quarter), bf16), out_hbm=shape((n, cap, wide), bf16))

    def wide_vmem(*dims):
        return pltpu.VMEM(dims, f32)

    def vmem(*dims):
        return pltpu.VMEM(dims, bf16)

    others_n = max(groups - 1, 1)
    scratch = dict(
        bytes=vmem(rows, width), flags=pltpu.VMEM((1, rows), jnp.int32), owner=pltpu.VMEM((1, count), jnp.int32),
        decay=wide_vmem(heads, rows), wx=vmem(*w_x.shape), wz=vmem(*w_z.shape), wbc=vmem(*w_bc.shape),
        wout=vmem(*w_out.shape), pad=vmem(*pad_vector.shape), wq=vmem(*w_q.shape), wkv=vmem(wide, 2 * part),
        wo=vmem(*w_o.shape), own=DMA((len(args),)),
        tots=wide_vmem(n, -(-heads // 8) * 8, state_n), ts=DMA((n,)), tr=DMA((n,)),
        state=wide_vmem(heads, state_n, p), state_out=vmem(heads, state_n, p), state_got=vmem(heads, state_n, p),
        s1s=DMA((heads,)), s1r=DMA((heads,)),
        slab_out=vmem(half, state_n, p), slab_got=vmem(line, half, state_n, p),
        s2s=DMA((line, half)), s2r=DMA((line, half)),
        prefix_out=vmem(half, state_n, p), prefix_got=vmem(half, state_n, p), s3s=DMA((half,)), s3r=DMA((half,)),
        start=vmem(heads, state_n, p), gate=wide_vmem(rows, inner), mixed=wide_vmem(rows, inner),
        base=vmem(2, groups, count, quarter), place=vmem(n * cap, count),
        d_send=vmem(groups, count, quarter), d_got=vmem(groups, count, quarter), d_core=DMA((2,)),
        d_sum=wide_vmem(groups, count, quarter), d_line_send=vmem(groups, count, quarter),
        d_line_got=vmem(groups, count, quarter), d_line=DMA((2, others_n)),
        e_send=vmem(groups, rows, quarter), e_got=vmem(groups, rows, quarter), e_core=DMA((2,)),
        e_sum=wide_vmem(groups, rows, quarter), e_line_send=vmem(groups, rows, quarter),
        e_line_got=vmem(groups, rows, quarter), e_line=DMA((2, others_n)),
        f_send=vmem(groups, count, size), f_got=vmem(groups, count, size), f_core=DMA((2,)),
        f_sum=wide_vmem(groups, count, size), f_line_send=vmem(groups, count, size),
        f_line_got=vmem(groups, count, size), f_line=DMA((2, others_n)),
        rows=vmem(line, 2, 2, groups, count, quarter), gr=DMA((line, 2, groups)), gcr=DMA((line, 2)),
        gz=DMA((line,)), gx=DMA((line,)), gy=DMA((line, others_n)), gd=DMA((line, others_n)), gc=DMA((line, 2)),
        stream=vmem(split, count, size), query=vmem(count, part),
        best=wide_vmem(units, count, 1), total=wide_vmem(units, count, 1), accum=wide_vmem(units, count, HD),
        enc=vmem(rows, quarter), enc_sem=DMA, out=vmem(n, cap, wide), out_sems=DMA((n,)),
        send=vmem(n, cap, size), hs=DMA((n,)), hr=DMA((n,)),
        hys=DMA((groups, n)), hyr=DMA((groups, n)), hcs=DMA((groups, n)), hcr=DMA((groups, n)),
    )
    results = pl.pallas_call(
        functools.partial(whole_kernel, list(args) + list(outs) + list(scratch)),
        out_shape=list(outs.values()),
        in_specs=[HBM] * len(args),
        out_specs=[HBM] * len(outs),
        scratch_shapes=list(scratch.values()),
        cost_estimate=cost(60),
        compiler_params=pltpu.CompilerParams(
            collective_id=0, has_side_effects=True, vmem_limit_bytes=GRANT
        ),
    )(*args.values())
    enc_out, main_out = pl.pallas_call(
        hand_out,
        out_shape=list(outs.values()),
        in_specs=[HBM] * len(outs),
        out_specs=[HBM] * len(outs),
        scratch_shapes=[pltpu.VMEM(o.shape, o.dtype) for o in outs.values()] + [DMA((2, 2, PIECES))],
        cost_estimate=cost(1),
        compiler_params=pltpu.CompilerParams(vmem_limit_bytes=GRANT),
    )(*results)
    return (enc_out, main_out.reshape(n * cap, wide))


def solution(mesh):
    placed = (
        P("seq", None),
        P("seq"),
        P("seq", None),
        P("seq", "tp"),
        P(None, "tp"),
        P(None, "tp"),
        P(),
        P("tp", None),
        P(),
        P(None, "tp"),
        P(None, "tp"),
        P(None, "tp"),
        P("tp", None),
    )
    return jax.shard_map(
        on_device,
        mesh=mesh,
        in_specs=placed,
        out_specs=(P("seq", "tp"), P("seq", None)),
        check_vma=False,
    )
```

```python
import functools
import math
import types

import jax
import jax.numpy as jnp
from jax import lax
from jax.experimental import pallas as pl
from jax.experimental.pallas import tpu as pltpu
from jax.sharding import PartitionSpec as P

HD = 128
eps = 1e-05
f32 = jnp.float32
bf16 = jnp.bfloat16
MESH = pl.DeviceIdType.MESH
VM = pl.BlockSpec(memory_space=pltpu.VMEM)
HBM = pl.BlockSpec(memory_space=pltpu.HBM)
DMA = pltpu.SemaphoreType.DMA
GRANT = 61000000
PIECES = 4


def cost(us):
    return pl.CostEstimate(flops=us * 10**9, bytes_accessed=us * 3 * 10**6, transcendentals=0)


def mm(a, b):
    return jnp.dot(a, b, preferred_element_type=f32)


def mm_t(a, b):
    return lax.dot_general(a, b, (((1,), (1,)), ((), ())), preferred_element_type=f32)


def t_mm(a, b):
    return lax.dot_general(a, b, (((0,), (0,)), ((), ())), preferred_element_type=f32)


def three(a):
    hi = a.astype(bf16)
    rest = a - hi.astype(f32)
    mid = rest.astype(bf16)
    low = (rest - mid.astype(f32)).astype(bf16)
    return hi, mid, low


def iota(shape, dim):
    return lax.broadcasted_iota(jnp.int32, shape, dim)


def loop(start, stop, body):
    if stop - start <= 8:
        for i in range(start, stop):
            body(i)
    else:
        lax.fori_loop(start, stop, lambda i, _: (body(i), 0)[1], 0)


def others(axis):
    me, n = lax.axis_index(axis), lax.axis_size(axis)
    return [lax.rem(me + d, n) for d in range(1, n)]


def remote(src, dst, send, recv, device):
    return pltpu.make_async_remote_copy(
        src_ref=src, dst_ref=dst, send_sem=send, recv_sem=recv, device_id=device, device_id_type=MESH
    )


def whole_kernel(names, *refs):
    r = types.SimpleNamespace(**dict(zip(names, refs)))
    n, split = lax.axis_size("seq"), lax.axis_size("tp")
    line, groups = n // 2, split // 2
    seq, tp = lax.axis_index("seq"), lax.axis_index("tp")
    z, x = seq // 2, lax.rem(seq, 2)
    hi, lo = tp // 2, lax.rem(tp, 2)
    pair = {"seq": z * 2 + 1 - x}
    core = {"tp": hi * 2 + 1 - lo}
    rest = [lax.rem(hi + e, groups) for e in range(1, groups)]

    def column(g):
        return {"tp": g * 2 + lo}

    def across(g):
        return {"seq": z * 2 + 1 - x, "tp": g * 2 + lo}

    rows, width = r.bytes_in.shape
    heads = r.decay_in.shape[0]
    half = heads // 2
    state_n = r.wbc_in.shape[1] // 2
    p = r.wx_in.shape[1] // heads
    count = r.owner_in.shape[1]
    quarter = width // split
    wide = r.wq_in.shape[0]
    size = wide // split
    part = r.wq_in.shape[1]
    units = part // HD
    cap = r.out_hbm.shape[1]

    fetches = {}
    moves = [
        ("decay", r.decay_in, r.decay),
        ("bytes", r.bytes_in, r.bytes),
        ("wbc", r.wbc_in, r.wbc),
        ("wx", r.wx_in, r.wx),
        ("flags", r.flags_in, r.flags),
        ("wz", r.wz_in, r.wz),
        ("pad", r.pad_in, r.pad),
        ("owner", r.owner_in, r.owner),
        ("wout", r.wout_in, r.wout),
        ("wk", r.wk_in, r.wkv.at[:, pl.ds(0, part)]),
        ("wv", r.wv_in, r.wkv.at[:, pl.ds(part, part)]),
        ("wq", r.wq_in, r.wq),
        ("wo", r.wo_in, r.wo),
    ]
    for i, (name, src, dst) in enumerate(moves):
        fetches[name] = pltpu.make_async_copy(src, dst, r.own.at[i])
    first = ("decay", "bytes", "wbc", "wx")
    for name in first:
        fetches[name].start()

    barrier = pltpu.get_barrier_semaphore()

    def knock(device):
        pl.semaphore_signal(barrier, inc=1, device_id=device, device_id_type=MESH)

    loop(1, n, lambda d: knock({"seq": lax.rem(seq + d, n)}))
    for peer in others("tp"):
        knock({"tp": peer})
    for g in rest:
        knock(across(g))

    for name in first:
        fetches[name].wait()
    for name in fetches:
        if name not in first:
            fetches[name].start()
    cum_row = r.decay[...]
    lane = iota(cum_row.shape, 1)
    reach = 1
    while reach < rows:
        cum_row = cum_row + jnp.where(lane >= reach, pltpu.roll(cum_row, reach, 1), 0.0)
        reach *= 2
    last = cum_row[:, rows - 1 : rows]
    filler = jnp.zeros((r.tots.shape[1] - heads, state_n), f32)
    r.tots[seq] = jnp.concatenate([jnp.broadcast_to(last, (heads, state_n)), filler], axis=0)
    def tot_copy(d):
        return remote(r.tots.at[seq], r.tots.at[seq], r.ts, r.tr, {"seq": lax.rem(seq + d, n)})

    tots_all = r.tots.at[pl.ds(0, n - 1)]
    tots_done = remote(tots_all, tots_all, r.ts, r.tr, pair)

    raw = r.bytes[...]
    norm = lax.rsqrt(jnp.mean(jnp.square(raw.astype(f32)), axis=-1, keepdims=True) + eps)
    bc = (mm(raw, r.wbc[...]) * norm).astype(bf16)
    bmat, cmat = bc[:, :state_n], bc[:, state_n:]
    xs = (mm(raw, r.wx[...]) * norm).astype(bf16)
    cum = jnp.concatenate([cum_row, jnp.zeros((128 - heads, rows), f32)], axis=0).T[:, :heads]
    tail = jnp.exp(cum[rows - 1 : rows, :] - cum)
    for h in range(heads):
        shrunk = (xs[:, h * p : (h + 1) * p].astype(f32) * tail[:, h : h + 1]).astype(bf16)
        state = t_mm(bmat, shrunk)
        r.state[h] = state
        r.state_out[h] = state.astype(bf16)

    def state_copy(h):
        return remote(r.state_out.at[h], r.state_got.at[h], r.own.at[h], r.s1r.at[h], pair)

    upward = z < line - 1
    pl.semaphore_wait(barrier, n - 1 + split - 1 + groups - 1)
    loop(1, n, lambda d: tot_copy(d).start())

    for i in range(half):

        @pl.when((x == 0) | upward)
        def _():
            state_copy((1 - x) * half + i).start()

    @pl.when(x == 0)
    def _():
        for i in range(half):
            state_copy(i).start()

    fetches["wz"].wait()
    gate = mm(raw, r.wz[...]) * norm
    gate = gate * jax.nn.sigmoid(gate)
    r.gate[...] = gate
    fetches["flags"].wait()
    flags = r.flags[...]
    upper = (iota((rows, rows), 0) <= iota((rows, rows), 1)).astype(f32).astype(bf16)
    many = jnp.broadcast_to(flags.astype(f32), (16, rows)).astype(bf16)
    rank = mm(many, upper)[0:1, :].astype(jnp.int32) - 1
    hit = (rank == iota((count, rows), 0)) & (flags == 1)
    picker = jnp.where(hit, 1.0, 0.0).astype(bf16)

    def pick(values):
        return sum(mm(picker, piece) for piece in three(values))

    tots_done.wait_recv()

    def tot_rows(shard):
        tots = r.tots[shard]
        return [jnp.where(x == 0, tots[i : i + 1], tots[half + i : half + i + 1]) for i in range(half)]

    def slab_copy(d, i):
        return remote(
            r.slab_out.at[i], r.slab_got.at[z, i], r.s2s.at[d, i], r.s2r.at[z, i], {"seq": (z + d) * 2 + x}
        )

    def slab_wait(source, i):
        remote(r.slab_got.at[source, i], r.slab_got.at[source, i], r.s2s.at[0, i], r.s2r.at[source, i], pair).wait_recv()

    @pl.when(upward)
    def _():
        later = tot_rows(z * 2 + 1)
        for i in range(half):
            h = x * half + i
            state_copy(h).wait_recv()
            mine, got = r.state[h], r.state_got[h].astype(f32)
            first, second = jnp.where(x == 0, mine, got), jnp.where(x == 0, got, mine)
            r.slab_out[i] = (first * jnp.exp(later[i]) + second).astype(bf16)

            def reach(d):
                @pl.when(z + d < line)
                def _():
                    slab_copy(d, i).start()

            loop(1, line, reach)


    middle = rows // 2
    for k in range(2):
        a, b = k * middle, (k + 1) * middle
        inter = mm_t(cmat[a:b], bmat[:b])
        causal = iota((middle, b), 0) + a >= iota((middle, b), 1)
        for h in range(heads):
            spans = cum[a:b, h : h + 1] - cum_row[h : h + 1, :b]
            mixing = (inter * jnp.exp(jnp.where(causal, spans, -1e30))).astype(bf16)
            r.mixed[a:b, h * p : (h + 1) * p] = mm(mixing, xs[:b, h * p : (h + 1) * p])
    mixed_picked = pick(r.mixed[...])
    gate_picked = pick(gate)
    grow_picked = jnp.exp(pick(cum))
    c_picked = mm(picker, cmat).astype(bf16)
    for g in range(groups):
        for k in range(2):
            q = g * 2 + k
            r.base[k, g] = mm(picker, r.bytes[:, q * quarter : (q + 1) * quarter]).astype(bf16)
    fetches["pad"].wait()
    fetches["wk"].wait()
    fetches["wv"].wait()
    fetches["wq"].wait()
    pad = jnp.broadcast_to(r.pad[...].astype(f32).reshape(1, -1), (count, r.pad.shape[0]))
    pad_square = jnp.sum(pad * pad, axis=1, keepdims=True)
    pad = pad.astype(bf16)
    pad_kv = mm(pad[:16], r.wkv[width:, :])[0:1]
    pad_q = mm(pad[:16], r.wq[width:, :])[0:1]
    fetches["owner"].wait()
    owner = r.owner[...]
    ranks = -(-n // 128) * 128
    hot = jnp.where(owner == iota((ranks, count), 0), 1.0, 0.0)
    strict = jnp.where(iota((count, count), 0) < iota((count, count), 1), 1.0, 0.0)
    before = mm(hot.astype(bf16), strict.astype(bf16))
    order = jnp.sum(before * hot, axis=0, keepdims=True).astype(jnp.int32)
    slot = owner * cap + order
    r.place[...] = jnp.where(slot == iota((n * cap, count), 0), 1.0, 0.0).astype(bf16)

    def prefix_copy(i):
        return remote(r.prefix_out.at[i], r.prefix_got.at[i], r.s3s.at[i], r.s3r.at[i], pair)

    prefix = []
    for i in range(half):

        def step(k, carry):
            moved = jnp.exp(tot_rows(k * 2)[i] + tot_rows(k * 2 + 1)[i])
            slab_wait(k, i)
            return carry * moved + r.slab_got[k, i].astype(f32)

        prefix.append(lax.fori_loop(0, z, step, jnp.zeros((state_n, p), f32)))
        r.prefix_out[i] = prefix[i].astype(bf16)

        @pl.when(z > 0)
        def _():
            prefix_copy(i).start()


    @pl.when(x == 1)
    def _():
        for i in range(half):
            state_copy(i).wait_recv()

    @pl.when((x == 1) & (z == line - 1))
    def _():
        for i in range(half):
            state_copy(half + i).wait_recv()

    tots = r.tots[z * 2]

    def settle(h, i, base, same):
        a, b = tots[i : i + 1], tots[half + i : half + i + 1]
        shrink = jnp.exp(jnp.where((x == 0) == same, a, b))
        moved = base * shrink + r.state_got[h].astype(f32)
        r.start[h] = jnp.where(x == 1, moved, base).astype(bf16)

    for i in range(half):
        settle(x * half + i, i, prefix[i], True)

    @pl.when(z > 0)
    def _():
        for i in range(half):
            prefix_copy(i).wait_recv()

    for i in range(half):
        got = jnp.where(z > 0, r.prefix_got[i].astype(f32), 0.0)
        settle((1 - x) * half + i, i, got, False)

    def piece(slab, xx, g):
        return r.rows.at[slab, lo, xx, g]

    def up_copy(d):
        here = piece(z, x, hi)
        return remote(here, here, r.gz.at[d], r.gr.at[z, x, hi], {"seq": (z + d) * 2 + x})

    def line_copy(d, e):
        here = piece(z - d, x, hi)
        return remote(here, here, r.gy.at[d, e], r.gr.at[z - d, x, hi], column(rest[e]))

    def pair_copy(d):
        here = piece(z - d, x, hi)
        return remote(here, here, r.gx.at[d], r.gr.at[z - d, x, hi], pair)

    def beyond_copy(e):
        here = piece(z, x, rest[e])
        return remote(here, here, r.gd.at[0, e], r.gr.at[z, x, rest[e]], pair)

    def far_copy(d, e):
        here = piece(z - d, x, hi)
        return remote(here, here, r.gd.at[d, e], r.gr.at[z - d, x, hi], across(rest[e]))

    def core_copy(d, xx):
        here = r.rows.at[z - d, lo, xx]
        return remote(here, here, r.gc.at[d, xx], r.gcr.at[z - d, xx], core)

    def core_wait(d, xx):
        there = r.rows.at[z - d, 1 - lo, xx]
        remote(there, there, r.gc.at[d, xx], r.gcr.at[z - d, xx], core).wait_recv()

    def piece_wait(slab, xx, g):
        here = piece(slab, xx, g)
        remote(here, here, r.gx.at[0], r.gr.at[slab, xx, g], pair).wait_recv()

    def spread(d):
        for e in range(groups - 1):
            far_copy(d, e).start()
        pair_copy(d).start()
        for e in range(groups - 1):
            line_copy(d, e).start()

    def relay_own():
        for e in range(groups - 1):
            complete(e)
        core_copy(0, x).start()

        @pl.when(x == 0)
        def _():
            for e in range(groups - 1):
                beyond_copy(e).start()

    def relay_pair(d):
        @pl.when((d > 0) | (x == 1))
        def _():
            for g in range(groups):
                piece_wait(z - d, 1 - x, g)
            core_copy(d, 1 - x).start()

    def relay(d):
        for g in rest:
            piece_wait(z - d, x, g)
        core_copy(d, x).start()
        relay_pair(d)

        @pl.when(d == 2)
        def _():
            for copy in enc_line:
                copy.start()

    def arrive(d):
        piece_wait(z - d, x, hi)
        spread(d)

    def climb(d):
        @pl.when(z + d < line)
        def _():
            up_copy(d).start()

    def finish(mixed, gate, cs, grow):
        scaled = []
        for h in range(heads):
            cols = slice(h * p, (h + 1) * p)
            gated = (mixed[:, cols] + mm(cs, r.start[h]) * grow[:, h : h + 1]) * gate[:, cols]
            norm = lax.rsqrt(jnp.mean(gated * gated, axis=1, keepdims=True) + eps)
            scaled.append((gated * norm).astype(bf16))
        return jnp.concatenate(scaled, axis=1)

    def cols(k, g, n):
        return pl.ds(pl.multiple_of((g * 2 + k) * n, 128), n)

    turns = rest + [hi]

    def core_swap(left, weight, n, send, got, sems):
        copies = []
        for e, g in enumerate(turns):
            send[g] = mm(left, weight[:, cols(1 - lo, g, n)]).astype(bf16)
            copies.append(remote(send.at[g], got.at[g], sems.at[0, e], sems.at[1, e], core))
            copies[-1].start()
        return copies

    def line_copies(send, got, sems):
        return [
            remote(send.at[g], got.at[hi], sems.at[0, e], sems.at[1, e], column(g))
            for e, g in enumerate(rest)
        ]

    fetches["wout"].wait()
    def partial_copy(e, k):
        here = r.d_line.at[hi, turns[k]]
        return remote(here, here, r.d_line_s.at[e, k], r.d_line_r.at[hi, turns[k]], column(rest[e]))

    def complete(k):
        g = turns[k]
        for peer in rest:
            there = r.d_line.at[peer, g]
            remote(there, there, r.d_line_s.at[0, 0], r.d_line_r.at[peer, g], core).wait_recv()
        summed = sum(r.d_line[peer, g].astype(f32) for peer in range(groups))
        r.rows[z, lo, x, g] = (r.base[lo, g].astype(f32) + summed).astype(bf16)

    scaled_picked = finish(mixed_picked, gate_picked, c_picked, grow_picked)
    pick_core = core_swap(scaled_picked, r.wout, quarter, r.d_send, r.d_got, r.d_core)
    mine = [mm(scaled_picked, r.wout[:, cols(lo, g, quarter)]) for g in turns]
    scaled = finish(r.mixed[...], r.gate[...], cmat, jnp.exp(cum))
    for e, g in enumerate(turns):
        pick_core[e].wait_recv()
        r.d_line[hi, g] = (mine[e] + r.d_got[g].astype(f32)).astype(bf16)
        if e < len(rest):
            partial_copy(e, e).start()
    for e in range(len(rest)):
        for k in range(groups):
            if k != e:
                partial_copy(e, k).start()
    enc_core = core_swap(scaled, r.wout, quarter, r.e_send, r.e_got, r.e_core)
    for g in range(groups):
        r.e_sum[g] = mm(scaled, r.wout[:, cols(lo, g, quarter)])

    @pl.when(z > 0)
    def _():
        arrive(z)

    complete(len(rest))

    enc_line = line_copies(r.e_line_send, r.e_line_got, r.e_line)
    loop(1, line, climb)

    @pl.when(x == 0)
    def _():
        pair_copy(0).start()

    relay_own()
    for copy in enc_core:
        copy.wait_recv()
    for g in range(groups):
        both = r.e_sum[g] + r.e_got[g].astype(f32)
        r.e_sum[g] = both
        r.e_line_send[g] = both.astype(bf16)

    scale = 1.0 / math.sqrt(HD)

    def project(blocks, weight, pads, factor=1.0):
        square = jnp.sum(sum(jnp.square(b.astype(f32)) for b in blocks), axis=1, keepdims=True)
        norm = lax.rsqrt((square + pad_square[0:1]) / wide + eps) * factor
        return ((mm(jnp.concatenate(blocks, axis=1), weight[:width, :]) + pads) * norm).astype(bf16)

    def attend(blocks, allowed=None):
        kv = project(blocks, r.wkv, pad_kv)
        for h in range(units):
            span = slice(h * HD, (h + 1) * HD)
            scores = mm_t(r.query[:, span], kv[:, span])
            if allowed is not None:
                scores = jnp.where(allowed, scores, -1e30)
            best = r.best[h]
            top = jnp.maximum(best, jnp.max(scores, axis=1, keepdims=True))
            shrink = jnp.exp(best - top)
            expo = jnp.exp(scores - top)
            r.best[h] = top
            r.total[h] = r.total[h] * shrink + jnp.sum(expo, axis=1, keepdims=True)
            r.accum[h] = r.accum[h] * shrink + mm(expo.astype(bf16), kv[:, part + h * HD : part + (h + 1) * HD])

    def block(xx):
        return [r.rows[z, q % 2, xx, q // 2] for q in range(split)]

    def slab(d):
        return [r.rows[z - d, q % 2, :, q // 2].reshape(2 * count, quarter) for q in range(split)]

    def own_slab():
        core_wait(0, x)
        mine = block(x)
        stream = jnp.concatenate(mine + [pad], axis=1)
        for q in range(split):
            r.stream[q] = stream[:, q * size : (q + 1) * size]
        r.query[...] = project(mine, r.wq, pad_q, scale)
        r.best[...] = jnp.full(r.best.shape, -1e30, f32)
        r.total[...] = jnp.zeros(r.total.shape, f32)
        r.accum[...] = jnp.zeros(r.accum.shape, f32)
        attend(mine, iota((count, count), 0) >= iota((count, count), 1))

    def own_pair():
        core_wait(0, 0)
        attend(block(0))

    lax.fori_loop(1, z, lambda k, _: (arrive(z - k), 0)[1], 0)
    @pl.when(z > 0)
    def _():
        relay(z)

    own_slab()

    def meet(d):
        core_wait(d, 0)
        core_wait(d, 1)
        attend(slab(d))

    @pl.when(z > 0)
    def _():
        meet(z)

    relay_pair(0)

    @pl.when(z <= 1)
    def _():
        for copy in enc_line:
            copy.start()


    @pl.when(z > 1)
    def _():
        relay(z - 1)


    @pl.when(x == 1)
    def _():
        own_pair()


    def turn(k, _):
        d = z - k

        @pl.when(d > 1)
        def _():
            relay(d - 1)

        meet(d)
        return 0

    lax.fori_loop(1, z, turn, 0)
    attended = jnp.concatenate([(r.accum[h] / r.total[h]).astype(bf16) for h in range(units)], axis=1)

    fetches["wo"].wait()
    main_core = core_swap(attended, r.wo, size, r.f_send, r.f_got, r.f_core)
    mine = [mm(attended, r.wo[:, cols(lo, g, size)]) for g in turns]
    main_line = line_copies(r.f_line_send, r.f_line_got, r.f_line)
    for e, g in enumerate(turns):
        main_core[e].wait_recv()
        both = mine[e] + r.f_got[g].astype(f32)
        r.f_sum[g] = both
        if e < len(rest):
            r.f_line_send[g] = both.astype(bf16)
            main_line[e].start()
    summed = r.stream[tp].astype(f32) + r.f_sum[hi]
    for copy in main_line:
        copy.wait_recv()
    for g in rest:
        summed = summed + r.f_line_got[g].astype(f32)
    r.send[...] = mm(r.place[...], summed.astype(bf16)).astype(bf16).reshape(n, cap, size)

    def spot(e, source):
        column = (lax.rem(hi - e + groups, groups) * 2 + lo) * size
        return r.out.at[source, :, pl.ds(pl.multiple_of(column, 128), size)]

    def far(peer):
        return remote(r.send.at[peer], spot(0, seq), r.hs, r.hr.at[seq], {"seq": peer})

    def far_wait(source):
        remote(spot(0, source), spot(0, source), r.hs, r.hr.at[source], pair).wait_recv()

    def direct(e, source):
        here = spot(0, source)
        return remote(here, here, r.hys.at[e - 1], r.hyr.at[e - 1, source], {"tp": lax.rem(hi + e, groups) * 2 + lo})

    def beside(e, source):
        here = spot(e, source)
        return remote(here, here, r.hcs.at[e], r.hcr.at[e, source], core)

    def pass_on(source):
        for e in range(1, groups):
            direct(e, source).start()
        beside(0, source).start()

    def pass_across(source):
        for e in range(1, groups):
            direct(e, source).wait_recv()
            beside(e, source).start()

    def other(k):
        return k + jnp.where(k >= seq, 1, 0)

    loop(0, n - 1, lambda k: far(other(k)).start())
    r.out[seq, :, pl.ds(pl.multiple_of(tp * size, 128), size)] = r.send[seq]
    pass_on(seq)

    tots_done.wait_send()
    for copy in pick_core + enc_core + main_core + enc_line + main_line:
        copy.wait_send()
    for i in range(half):

        @pl.when((x == 0) | upward)
        def _():
            state_copy((1 - x) * half + i).wait_send()

        @pl.when(x == 0)
        def _():
            state_copy(i).wait_send()

        @pl.when(z > 0)
        def _():
            prefix_copy(i).wait_send()

    def close_up(d):
        @pl.when(z + d < line)
        def _():
            up_copy(d).wait_send()
            for i in range(half):
                slab_copy(d, i).wait_send()

    loop(1, line, close_up)

    for e in range(groups - 1):
        for k in range(groups):
            partial_copy(e, k).wait_send()

    def close_row(d, _):
        core_copy(d, x).wait_send()

        @pl.when(d > 0)
        def _():
            for e in range(groups - 1):
                line_copy(d, e).wait_send()

        @pl.when((d > 0) | (x == 0))
        def _():
            for e in range(groups - 1):
                far_copy(d, e).wait_send()
            pair_copy(d).wait_send()

        @pl.when((d > 0) | (x == 1))
        def _():
            core_copy(d, 1 - x).wait_send()

        return 0

    lax.fori_loop(0, z + 1, close_row, 0)

    def deliver(k):
        far_wait(other(k))
        pass_on(other(k))

    loop(0, n - 1, deliver)
    pass_across(seq)
    loop(0, n - 1, lambda k: pass_across(other(k)))
    for copy in enc_line:
        copy.wait_recv()
    enc = r.bytes[:, pl.ds(pl.multiple_of(tp * quarter, 128), quarter)].astype(f32) + r.e_sum[hi]
    for g in rest:
        enc = enc + r.e_line_got[g].astype(f32)
    r.enc[...] = enc.astype(bf16)
    enc_write = pltpu.make_async_copy(r.enc, r.enc_hbm, r.enc_sem)
    enc_write.start()
    def close(d):
        for e in range(groups):
            beside(e, d).wait_recv()
        write(d).start()

    def write(d):
        return pltpu.make_async_copy(r.out.at[d], r.out_hbm.at[d], r.own.at[d])

    loop(0, n, close)
    sent = r.send.at[pl.ds(0, n - 1)]
    remote(sent, sent, r.hs, r.hr.at[seq], pair).wait_send()
    for e in range(groups):
        column = (lax.rem(hi - e + groups, groups) * 2 + lo) * size
        sent = r.out.at[:, :, pl.ds(pl.multiple_of(column, 128), size)]
        remote(sent, sent, r.hcs.at[e], r.hr.at[seq], core).wait_send()
        if e > 0:
            sent = r.out.at[:, :, pl.ds(pl.multiple_of(tp * size, 128), size)]
            remote(sent, sent, r.hys.at[e - 1], r.hr.at[seq], core).wait_send()
    enc_write.wait()
    loop(0, n, lambda d: write(d).wait())

def hand_out(enc_ref, main_ref, enc_out, main_out, enc, main, sems):
    ways = []
    for i, (src, through, dst) in enumerate(((main_ref, main, main_out), (enc_ref, enc, enc_out))):
        step = src.shape[0] // PIECES
        for j in range(PIECES):
            span = pl.ds(j * step, step)
            fetch = pltpu.make_async_copy(src.at[span], through.at[span], sems.at[0, i, j])
            ways.append((fetch, pltpu.make_async_copy(through.at[span], dst.at[span], sems.at[1, i, j])))
    for fetch, _ in ways:
        fetch.start()
    for fetch, write in ways:
        fetch.wait()
        write.start()
    for _, write in ways:
        write.wait()


def on_device(
    byte_states, flags, stretch_owner, log_decay, w_x, w_z, w_bc, w_out, pad_vector, w_q, w_k, w_v, w_o
):
    rows, width = byte_states.shape
    heads = log_decay.shape[1]
    inner = w_x.shape[1]
    p = inner // heads
    state_n = w_bc.shape[1] // 2
    n = lax.axis_size("seq")
    split = lax.axis_size("tp")
    line, groups, half = n // 2, split // 2, heads // 2
    count = stretch_owner.shape[0]
    quarter = width // split
    cap = max(2, 2 * count // n)
    wide, part = w_q.shape
    size = wide // split
    units = part // HD
    shape = jax.ShapeDtypeStruct
    args = dict(
        bytes_in=byte_states, flags_in=flags.reshape(1, rows), owner_in=stretch_owner.reshape(1, count),
        decay_in=log_decay.T, wx_in=w_x, wz_in=w_z, wbc_in=w_bc, wout_in=w_out, pad_in=pad_vector,
        wq_in=w_q, wk_in=w_k, wv_in=w_v, wo_in=w_o,
    )
    outs = dict(enc_hbm=shape((rows, quarter), bf16), out_hbm=shape((n, cap, wide), bf16))

    def wide_vmem(*dims):
        return pltpu.VMEM(dims, f32)

    def vmem(*dims):
        return pltpu.VMEM(dims, bf16)

    others_n = max(groups - 1, 1)
    scratch = dict(
        bytes=vmem(rows, width), flags=pltpu.VMEM((1, rows), jnp.int32), owner=pltpu.VMEM((1, count), jnp.int32),
        decay=wide_vmem(heads, rows), wx=vmem(*w_x.shape), wz=vmem(*w_z.shape), wbc=vmem(*w_bc.shape),
        wout=vmem(*w_out.shape), pad=vmem(*pad_vector.shape), wq=vmem(*w_q.shape), wkv=vmem(wide, 2 * part),
        wo=vmem(*w_o.shape), own=DMA((max(len(args), n),)),
        tots=wide_vmem(n, -(-heads // 8) * 8, state_n), ts=DMA, tr=DMA,
        state=wide_vmem(heads, state_n, p), state_out=vmem(heads, state_n, p), state_got=vmem(heads, state_n, p),
        s1r=DMA((heads,)),
        slab_out=vmem(half, state_n, p), slab_got=vmem(line, half, state_n, p),
        s2s=DMA((line, half)), s2r=DMA((line, half)),
        prefix_out=vmem(half, state_n, p), prefix_got=vmem(half, state_n, p), s3s=DMA((half,)), s3r=DMA((half,)),
        start=vmem(heads, state_n, p), gate=wide_vmem(rows, inner), mixed=wide_vmem(rows, inner),
        base=vmem(2, groups, count, quarter), place=vmem(n * cap, count),
        d_send=vmem(groups, count, quarter), d_got=vmem(groups, count, quarter), d_core=DMA((2, groups)),
        d_line=vmem(groups, groups, count, quarter), d_line_s=DMA((others_n, groups)), d_line_r=DMA((groups, groups)),
        e_send=vmem(groups, rows, quarter), e_got=vmem(groups, rows, quarter), e_core=DMA((2, groups)),
        e_sum=wide_vmem(groups, rows, quarter), e_line_send=vmem(groups, rows, quarter),
        e_line_got=vmem(groups, rows, quarter), e_line=DMA((2, others_n)),
        f_send=vmem(groups, count, size), f_got=vmem(groups, count, size), f_core=DMA((2, groups)),
        f_sum=wide_vmem(groups, count, size), f_line_send=vmem(groups, count, size),
        f_line_got=vmem(groups, count, size), f_line=DMA((2, others_n)),
        rows=vmem(line, 2, 2, groups, count, quarter), gr=DMA((line, 2, groups)), gcr=DMA((line, 2)),
        gz=DMA((line,)), gx=DMA((line,)), gy=DMA((line, others_n)), gd=DMA((line, others_n)), gc=DMA((line, 2)),
        stream=vmem(split, count, size), query=vmem(count, part),
        best=wide_vmem(units, count, 1), total=wide_vmem(units, count, 1), accum=wide_vmem(units, count, HD),
        enc=vmem(rows, quarter), enc_sem=DMA, out=vmem(n, cap, wide),
        send=vmem(n, cap, size), hs=DMA, hr=DMA((n,)),
        hys=DMA((others_n,)), hyr=DMA((others_n, n)), hcs=DMA((groups,)), hcr=DMA((groups, n)),
    )
    results = pl.pallas_call(
        functools.partial(whole_kernel, list(args) + list(outs) + list(scratch)),
        out_shape=list(outs.values()),
        in_specs=[HBM] * len(args),
        out_specs=[HBM] * len(outs),
        scratch_shapes=list(scratch.values()),
        cost_estimate=cost(60),
        compiler_params=pltpu.CompilerParams(
            collective_id=0, has_side_effects=True, vmem_limit_bytes=GRANT
        ),
    )(*args.values())
    enc_out, main_out = pl.pallas_call(
        hand_out,
        out_shape=list(outs.values()),
        in_specs=[HBM] * len(outs),
        out_specs=[HBM] * len(outs),
        scratch_shapes=[pltpu.VMEM(o.shape, o.dtype) for o in outs.values()] + [DMA((2, 2, PIECES))],
        cost_estimate=cost(1),
        compiler_params=pltpu.CompilerParams(vmem_limit_bytes=GRANT),
    )(*results)
    return (enc_out, main_out.reshape(n * cap, wide))


def solution(mesh):
    placed = (
        P("seq", None),
        P("seq"),
        P("seq", None),
        P("seq", "tp"),
        P(None, "tp"),
        P(None, "tp"),
        P(),
        P("tp", None),
        P(),
        P(None, "tp"),
        P(None, "tp"),
        P(None, "tp"),
        P("tp", None),
    )
    return jax.shard_map(
        on_device,
        mesh=mesh,
        in_specs=placed,
        out_specs=(P("seq", "tp"), P("seq", None)),
        check_vma=False,
    )
```

```python
import functools
import math
import types

import jax
import jax.numpy as jnp
from jax import lax
from jax.experimental import pallas as pl
from jax.experimental.pallas import tpu as pltpu
from jax.sharding import PartitionSpec as P

HD = 128
eps = 1e-05
f32 = jnp.float32
bf16 = jnp.bfloat16
MESH = pl.DeviceIdType.MESH
VM = pl.BlockSpec(memory_space=pltpu.VMEM)
HBM = pl.BlockSpec(memory_space=pltpu.HBM)
DMA = pltpu.SemaphoreType.DMA
GRANT = 61000000


def cost(us):
    return pl.CostEstimate(flops=us * 10**9, bytes_accessed=us * 3 * 10**6, transcendentals=0)


def mm(a, b):
    return jnp.dot(a, b, preferred_element_type=f32)


def mm_t(a, b):
    return lax.dot_general(a, b, (((1,), (1,)), ((), ())), preferred_element_type=f32)


def t_mm(a, b):
    return lax.dot_general(a, b, (((0,), (0,)), ((), ())), preferred_element_type=f32)


def three(a):
    hi = a.astype(bf16)
    rest = a - hi.astype(f32)
    mid = rest.astype(bf16)
    low = (rest - mid.astype(f32)).astype(bf16)
    return hi, mid, low


def iota(shape, dim):
    return lax.broadcasted_iota(jnp.int32, shape, dim)


def loop(start, stop, body):
    if stop - start <= 8:
        for i in range(start, stop):
            body(i)
    else:
        lax.fori_loop(start, stop, lambda i, _: (body(i), 0)[1], 0)


def others(axis):
    me, n = lax.axis_index(axis), lax.axis_size(axis)
    return [lax.rem(me + d, n) for d in range(1, n)]


def remote(src, dst, send, recv, device):
    return pltpu.make_async_remote_copy(
        src_ref=src, dst_ref=dst, send_sem=send, recv_sem=recv, device_id=device, device_id_type=MESH
    )


def whole_kernel(names, *refs):
    r = types.SimpleNamespace(**dict(zip(names, refs)))
    n, split = lax.axis_size("seq"), lax.axis_size("tp")
    line, groups = n // 2, split // 2
    seq, tp = lax.axis_index("seq"), lax.axis_index("tp")
    z, x = seq // 2, lax.rem(seq, 2)
    hi, lo = tp // 2, lax.rem(tp, 2)
    pair = {"seq": z * 2 + 1 - x}
    core = {"tp": hi * 2 + 1 - lo}
    rest = [lax.rem(hi + e, groups) for e in range(1, groups)]

    def column(g):
        return {"tp": g * 2 + lo}

    def across(g):
        return {"seq": z * 2 + 1 - x, "tp": g * 2 + lo}

    rows, width = r.bytes_in.shape
    heads = r.decay_in.shape[0]
    half = heads // 2
    state_n = r.wbc_in.shape[1] // 2
    p = r.wx_in.shape[1] // heads
    count = r.owner_in.shape[1]
    quarter = width // split
    wide = r.wq_in.shape[0]
    size = wide // split
    part = r.wq_in.shape[1]
    units = part // HD
    cap = r.out_hbm.shape[1]

    fetches = {}
    moves = [
        ("decay", r.decay_in, r.decay),
        ("bytes", r.bytes_in, r.bytes),
        ("wbc", r.wbc_in, r.wbc),
        ("wx", r.wx_in, r.wx),
        ("flags", r.flags_in, r.flags),
        ("wz", r.wz_in, r.wz),
        ("pad", r.pad_in, r.pad),
        ("owner", r.owner_in, r.owner),
        ("wout", r.wout_in, r.wout),
        ("wk", r.wk_in, r.wkv.at[:, pl.ds(0, part)]),
        ("wv", r.wv_in, r.wkv.at[:, pl.ds(part, part)]),
        ("wq", r.wq_in, r.wq),
        ("wo", r.wo_in, r.wo),
    ]
    for i, (name, src, dst) in enumerate(moves):
        fetches[name] = pltpu.make_async_copy(src, dst, r.own.at[i])
    first = ("decay", "bytes", "wbc", "wx")
    for name in first:
        fetches[name].start()

    barrier = pltpu.get_barrier_semaphore()

    def knock(device):
        pl.semaphore_signal(barrier, inc=1, device_id=device, device_id_type=MESH)

    loop(1, n, lambda d: knock({"seq": lax.rem(seq + d, n)}))
    for peer in others("tp"):
        knock({"tp": peer})
    for g in rest:
        knock(across(g))

    for name in first[:-1]:
        fetches[name].wait()
    cum_row = r.decay[...]
    lane = iota(cum_row.shape, 1)
    reach = 1
    while reach < rows:
        cum_row = cum_row + jnp.where(lane >= reach, pltpu.roll(cum_row, reach, 1), 0.0)
        reach *= 2
    last = cum_row[:, rows - 1 : rows]
    filler = jnp.zeros((r.tots.shape[1] - heads, state_n), f32)
    r.tots[seq] = jnp.concatenate([jnp.broadcast_to(last, (heads, state_n)), filler], axis=0)
    def tot_copy(d):
        return remote(r.tots.at[seq], r.tots.at[seq], r.ts, r.tr, {"seq": lax.rem(seq + d, n)})

    tots_all = r.tots.at[pl.ds(0, n - 1)]
    tots_done = remote(tots_all, tots_all, r.ts, r.tr, pair)

    raw = r.bytes[...]
    norm = lax.rsqrt(jnp.mean(jnp.square(raw.astype(f32)), axis=-1, keepdims=True) + eps)
    bc = (mm(raw, r.wbc[...]) * norm).astype(bf16)
    bmat, cmat = bc[:, :state_n], bc[:, state_n:]
    fetches[first[-1]].wait()
    for name in fetches:
        if name not in first:
            fetches[name].start()
    xs = (mm(raw, r.wx[...]) * norm).astype(bf16)
    cum = jnp.concatenate([cum_row, jnp.zeros((128 - heads, rows), f32)], axis=0).T[:, :heads]
    tail = jnp.exp(cum[rows - 1 : rows, :] - cum)
    for h in range(heads):
        shrunk = (xs[:, h * p : (h + 1) * p].astype(f32) * tail[:, h : h + 1]).astype(bf16)
        state = t_mm(bmat, shrunk)
        r.state[h] = state
        r.state_out[h] = state.astype(bf16)

    def state_copy(h):
        return remote(r.state_out.at[h], r.state_got.at[h], r.own.at[h], r.s1r.at[h], pair)

    upward = z < line - 1
    pl.semaphore_wait(barrier, n - 1 + split - 1 + groups - 1)
    loop(1, n, lambda d: tot_copy(d).start())

    for i in range(half):

        @pl.when((x == 0) | upward)
        def _():
            state_copy((1 - x) * half + i).start()

    @pl.when(x == 0)
    def _():
        for i in range(half):
            state_copy(i).start()

    fetches["wz"].wait()
    gate = mm(raw, r.wz[...]) * norm
    gate = gate * jax.nn.sigmoid(gate)
    r.gate[...] = gate
    fetches["flags"].wait()
    flags = r.flags[...]
    upper = (iota((rows, rows), 0) <= iota((rows, rows), 1)).astype(f32).astype(bf16)
    many = jnp.broadcast_to(flags.astype(f32), (16, rows)).astype(bf16)
    rank = mm(many, upper)[0:1, :].astype(jnp.int32) - 1
    hit = (rank == iota((count, rows), 0)) & (flags == 1)
    picker = jnp.where(hit, 1.0, 0.0).astype(bf16)

    def pick(values):
        return sum(mm(picker, piece) for piece in three(values))

    tots_done.wait_recv()

    def tot_rows(shard):
        tots = r.tots[shard]
        return [jnp.where(x == 0, tots[i : i + 1], tots[half + i : half + i + 1]) for i in range(half)]

    def slab_copy(d, i):
        return remote(
            r.slab_out.at[i], r.slab_got.at[z, i], r.s2s.at[d, i], r.s2r.at[z, i], {"seq": (z + d) * 2 + x}
        )

    def slab_wait(source, i):
        remote(r.slab_got.at[source, i], r.slab_got.at[source, i], r.s2s.at[0, i], r.s2r.at[source, i], pair).wait_recv()

    @pl.when(upward)
    def _():
        later = tot_rows(z * 2 + 1)
        for i in range(half):
            h = x * half + i
            state_copy(h).wait_recv()
            mine, got = r.state[h], r.state_got[h].astype(f32)
            first, second = jnp.where(x == 0, mine, got), jnp.where(x == 0, got, mine)
            r.slab_out[i] = (first * jnp.exp(later[i]) + second).astype(bf16)

            def reach(d):
                @pl.when(z + d < line)
                def _():
                    slab_copy(d, i).start()

            loop(1, line, reach)


    middle = rows // 2
    for k in range(2):
        a, b = k * middle, (k + 1) * middle
        inter = mm_t(cmat[a:b], bmat[:b])
        causal = iota((middle, b), 0) + a >= iota((middle, b), 1)
        for h in range(heads):
            spans = cum[a:b, h : h + 1] - cum_row[h : h + 1, :b]
            mixing = (inter * jnp.exp(jnp.where(causal, spans, -1e30))).astype(bf16)
            r.mixed[a:b, h * p : (h + 1) * p] = mm(mixing, xs[:b, h * p : (h + 1) * p])
    mixed_picked = pick(r.mixed[...])
    gate_picked = pick(gate)
    grow_picked = jnp.exp(pick(cum))
    c_picked = mm(picker, cmat).astype(bf16)
    for g in range(groups):
        for k in range(2):
            q = g * 2 + k
            r.base[k, g] = mm(picker, r.bytes[:, q * quarter : (q + 1) * quarter]).astype(bf16)
    fetches["pad"].wait()
    fetches["wk"].wait()
    fetches["wv"].wait()
    fetches["wq"].wait()
    pad = jnp.broadcast_to(r.pad[...].astype(f32).reshape(1, -1), (count, r.pad.shape[0]))
    pad_square = jnp.sum(pad * pad, axis=1, keepdims=True)
    pad = pad.astype(bf16)
    pad_kv = mm(pad[:16], r.wkv[width:, :])[0:1]
    pad_q = mm(pad[:16], r.wq[width:, :])[0:1]
    fetches["owner"].wait()
    owner = r.owner[...]
    ranks = -(-n // 128) * 128
    hot = jnp.where(owner == iota((ranks, count), 0), 1.0, 0.0)
    strict = jnp.where(iota((count, count), 0) < iota((count, count), 1), 1.0, 0.0)
    before = mm(hot.astype(bf16), strict.astype(bf16))
    order = jnp.sum(before * hot, axis=0, keepdims=True).astype(jnp.int32)
    slot = owner * cap + order
    r.place[...] = jnp.where(slot == iota((n * cap, count), 0), 1.0, 0.0).astype(bf16)

    def prefix_copy(i):
        return remote(r.prefix_out.at[i], r.prefix_got.at[i], r.s3s.at[i], r.s3r.at[i], pair)

    prefix = []
    for i in range(half):

        def step(k, carry):
            moved = jnp.exp(tot_rows(k * 2)[i] + tot_rows(k * 2 + 1)[i])
            slab_wait(k, i)
            return carry * moved + r.slab_got[k, i].astype(f32)

        prefix.append(lax.fori_loop(0, z, step, jnp.zeros((state_n, p), f32)))
        r.prefix_out[i] = prefix[i].astype(bf16)

        @pl.when(z > 0)
        def _():
            prefix_copy(i).start()


    @pl.when(x == 1)
    def _():
        for i in range(half):
            state_copy(i).wait_recv()

    @pl.when((x == 1) & (z == line - 1))
    def _():
        for i in range(half):
            state_copy(half + i).wait_recv()

    tots = r.tots[z * 2]

    def settle(h, i, base, same):
        a, b = tots[i : i + 1], tots[half + i : half + i + 1]
        shrink = jnp.exp(jnp.where((x == 0) == same, a, b))
        moved = base * shrink + r.state_got[h].astype(f32)
        r.start[h] = jnp.where(x == 1, moved, base).astype(bf16)

    for i in range(half):
        settle(x * half + i, i, prefix[i], True)

    @pl.when(z > 0)
    def _():
        for i in range(half):
            prefix_copy(i).wait_recv()

    for i in range(half):
        got = jnp.where(z > 0, r.prefix_got[i].astype(f32), 0.0)
        settle((1 - x) * half + i, i, got, False)

    def piece(slab, xx, g):
        return r.rows.at[slab, lo, xx, g]

    def up_copy(d):
        here = piece(z, x, hi)
        return remote(here, here, r.s2s.at[d, 0], r.gr.at[z, x, hi], {"seq": (z + d) * 2 + x})

    def line_copy(d, e):
        here = piece(z - d, x, hi)
        return remote(here, here, r.gy.at[d, e], r.gr.at[z - d, x, hi], column(rest[e]))

    def pair_copy(d):
        here = piece(z - d, x, hi)
        return remote(here, here, r.gx.at[d], r.gr.at[z - d, x, hi], pair)

    def beyond_copy(e):
        here = piece(z, x, rest[e])
        return remote(here, here, r.gd.at[0, e], r.gr.at[z, x, rest[e]], pair)

    def far_copy(d, e):
        here = piece(z - d, x, hi)
        return remote(here, here, r.gd.at[d, e], r.gr.at[z - d, x, hi], across(rest[e]))

    def core_copy(d, xx):
        here = r.rows.at[z - d, lo, xx]
        return remote(here, here, r.gc.at[d, xx], r.gcr.at[z - d, xx], core)

    def core_wait(d, xx):
        there = r.rows.at[z - d, 1 - lo, xx]
        remote(there, there, r.gc.at[d, xx], r.gcr.at[z - d, xx], core).wait_recv()

    def piece_wait(slab, xx, g):
        here = piece(slab, xx, g)
        remote(here, here, r.gx.at[0], r.gr.at[slab, xx, g], pair).wait_recv()

    def spread(d):
        for e in range(groups - 1):
            far_copy(d, e).start()
        pair_copy(d).start()
        for e in range(groups - 1):
            line_copy(d, e).start()

    def relay_own():
        for e in range(groups - 1):
            complete(e)
        core_copy(0, x).start()

        @pl.when(x == 0)
        def _():
            for e in range(groups - 1):
                beyond_copy(e).start()

    def relay_pair(d):
        @pl.when((d > 0) | (x == 1))
        def _():
            for g in range(groups):
                piece_wait(z - d, 1 - x, g)
            core_copy(d, 1 - x).start()

    def relay(d):
        for g in rest:
            piece_wait(z - d, x, g)
        core_copy(d, x).start()
        relay_pair(d)

        @pl.when(d == 2)
        def _():
            for copy in enc_line:
                copy.start()

    def arrive(d):
        piece_wait(z - d, x, hi)
        spread(d)

    def climb(k):
        d = line - k

        @pl.when(z + d < line)
        def _():
            up_copy(d).start()

    def finish(mixed, gate, cs, grow):
        scaled = []
        for h in range(heads):
            cols = slice(h * p, (h + 1) * p)
            gated = (mixed[:, cols] + mm(cs, r.start[h]) * grow[:, h : h + 1]) * gate[:, cols]
            norm = lax.rsqrt(jnp.mean(gated * gated, axis=1, keepdims=True) + eps)
            scaled.append((gated * norm).astype(bf16))
        return jnp.concatenate(scaled, axis=1)

    def cols(k, g, n):
        return pl.ds(pl.multiple_of((g * 2 + k) * n, 128), n)

    turns = rest + [hi]

    def core_swap(left, weight, n, send, got, sems):
        copies = []
        for e, g in enumerate(turns):
            send[g] = mm(left, weight[:, cols(1 - lo, g, n)]).astype(bf16)
            copies.append(remote(send.at[g], got.at[g], sems.at[0, e], sems.at[1, e], core))
            copies[-1].start()
        return copies

    def line_copies(send, got, sems):
        return [
            remote(send.at[g], got.at[hi], sems.at[0, e], sems.at[1, e], column(g))
            for e, g in enumerate(rest)
        ]

    fetches["wout"].wait()
    def partial_copy(e, k):
        here = r.d_line.at[hi, turns[k]]
        return remote(here, here, r.d_line_s.at[e, k], r.d_line_r.at[hi, turns[k]], column(rest[e]))

    def complete(k):
        g = turns[k]
        for peer in rest:
            there = r.d_line.at[peer, g]
            remote(there, there, r.d_line_s.at[0, 0], r.d_line_r.at[peer, g], core).wait_recv()
        summed = sum(r.d_line[peer, g].astype(f32) for peer in range(groups))
        r.rows[z, lo, x, g] = (r.base[lo, g].astype(f32) + summed).astype(bf16)

    scaled_picked = finish(mixed_picked, gate_picked, c_picked, grow_picked)
    pick_core = core_swap(scaled_picked, r.wout, quarter, r.d_send, r.d_got, r.d_core)
    mine = [mm(scaled_picked, r.wout[:, cols(lo, g, quarter)]) for g in turns]
    scaled = finish(r.mixed[...], r.gate[...], cmat, jnp.exp(cum))
    for e, g in enumerate(turns):
        pick_core[e].wait_recv()
        r.d_line[hi, g] = (mine[e] + r.d_got[g].astype(f32)).astype(bf16)
        if e < len(rest):
            partial_copy(e, e).start()
    for e in range(len(rest)):
        for k in range(groups):
            if k != e:
                partial_copy(e, k).start()
    enc_core = core_swap(scaled, r.wout, quarter, r.e_send, r.e_got, r.e_core)
    for g in range(groups):
        r.e_sum[g] = mm(scaled, r.wout[:, cols(lo, g, quarter)])

    @pl.when(z > 1)
    def _():
        arrive(z)

    complete(len(rest))

    enc_line = line_copies(r.e_line_send, r.e_line_got, r.e_line)
    def close_slab(d):
        @pl.when(z + d < line)
        def _():
            for i in range(half):
                slab_copy(d, i).wait_send()

    loop(1, line, close_slab)
    loop(1, line, climb)

    @pl.when(x == 0)
    def _():
        pair_copy(0).start()

    relay_own()
    for copy in enc_core:
        copy.wait_recv()
    for g in range(groups):
        both = r.e_sum[g] + r.e_got[g].astype(f32)
        r.e_sum[g] = both
        r.e_line_send[g] = both.astype(bf16)

    scale = 1.0 / math.sqrt(HD)

    def project(blocks, weight, pads, factor=1.0):
        square = jnp.sum(sum(jnp.square(b.astype(f32)) for b in blocks), axis=1, keepdims=True)
        norm = lax.rsqrt((square + pad_square[0:1]) / wide + eps) * factor
        return ((mm(jnp.concatenate(blocks, axis=1), weight[:width, :]) + pads) * norm).astype(bf16)

    def attend(blocks, allowed=None):
        kv = project(blocks, r.wkv, pad_kv)
        for h in range(units):
            span = slice(h * HD, (h + 1) * HD)
            scores = mm_t(r.query[:, span], kv[:, span])
            if allowed is not None:
                scores = jnp.where(allowed, scores, -1e30)
            best = r.best[h]
            top = jnp.maximum(best, jnp.max(scores, axis=1, keepdims=True))
            shrink = jnp.exp(best - top)
            expo = jnp.exp(scores - top)
            r.best[h] = top
            r.total[h] = r.total[h] * shrink + jnp.sum(expo, axis=1, keepdims=True)
            r.accum[h] = r.accum[h] * shrink + mm(expo.astype(bf16), kv[:, part + h * HD : part + (h + 1) * HD])

    def block(xx):
        return [r.rows[z, q % 2, xx, q // 2] for q in range(split)]

    def slab(d):
        return [r.rows[z - d, q % 2, :, q // 2].reshape(2 * count, quarter) for q in range(split)]

    def own_slab():
        core_wait(0, x)
        mine = block(x)
        stream = jnp.concatenate(mine + [pad], axis=1)
        for q in range(split):
            r.stream[q] = stream[:, q * size : (q + 1) * size]
        r.query[...] = project(mine, r.wq, pad_q, scale)
        r.best[...] = jnp.full(r.best.shape, -1e30, f32)
        r.total[...] = jnp.zeros(r.total.shape, f32)
        r.accum[...] = jnp.zeros(r.accum.shape, f32)
        attend(mine, iota((count, count), 0) >= iota((count, count), 1))

    def own_pair():
        core_wait(0, 0)
        attend(block(0))

    @pl.when(z == 1)
    def _():
        arrive(1)

    lax.fori_loop(1, z, lambda k, _: (arrive(z - k), 0)[1], 0)
    @pl.when(z > 0)
    def _():
        relay(z)

    own_slab()

    def meet(d):
        core_wait(d, 0)
        core_wait(d, 1)
        attend(slab(d))

    @pl.when(z > 0)
    def _():
        meet(z)

    relay_pair(0)

    @pl.when(z <= 1)
    def _():
        for copy in enc_line:
            copy.start()


    @pl.when(z > 1)
    def _():
        relay(z - 1)


    @pl.when(x == 1)
    def _():
        own_pair()


    def turn(k, _):
        d = z - k

        @pl.when(d > 1)
        def _():
            relay(d - 1)

        meet(d)
        return 0

    lax.fori_loop(1, z, turn, 0)
    attended = jnp.concatenate([(r.accum[h] / r.total[h]).astype(bf16) for h in range(units)], axis=1)

    fetches["wo"].wait()
    main_core = core_swap(attended, r.wo, size, r.f_send, r.f_got, r.f_core)
    mine = [mm(attended, r.wo[:, cols(lo, g, size)]) for g in turns]
    main_line = line_copies(r.f_line_send, r.f_line_got, r.f_line)
    for e, g in enumerate(turns):
        main_core[e].wait_recv()
        both = mine[e] + r.f_got[g].astype(f32)
        r.f_sum[g] = both
        if e < len(rest):
            r.f_line_send[g] = both.astype(bf16)
            main_line[e].start()
    summed = r.stream[tp].astype(f32) + r.f_sum[hi]
    for copy in main_line:
        copy.wait_recv()
    for g in rest:
        summed = summed + r.f_line_got[g].astype(f32)
    r.send[...] = mm(r.place[...], summed.astype(bf16)).astype(bf16).reshape(n, cap, size)

    def spot(e, source):
        column = (lax.rem(hi - e + groups, groups) * 2 + lo) * size
        return r.out.at[source, :, pl.ds(pl.multiple_of(column, 128), size)]

    def far(peer):
        return remote(r.send.at[peer], spot(0, seq), r.hs, r.hr.at[seq], {"seq": peer})

    def far_wait(source):
        remote(spot(0, source), spot(0, source), r.hs, r.hr.at[source], pair).wait_recv()

    def direct(e, source):
        here = spot(0, source)
        got = r.gr.at[source // 2, lax.rem(source, 2), e]
        return remote(here, here, r.hys.at[e - 1], got, {"tp": lax.rem(hi + e, groups) * 2 + lo})

    def beside(e, source):
        here = spot(e, source)
        got = r.gcr.at[source // 2, lax.rem(source, 2)] if e == 0 else r.hcr.at[e - 1, source]
        return remote(here, here, r.hcs.at[e], got, core)

    def pass_on(source):
        for e in range(1, groups):
            direct(e, source).start()
        beside(0, source).start()

    def pass_across(source):
        for e in range(1, groups):
            direct(e, source).wait_recv()
            beside(e, source).start()

    def other(k):
        return k + jnp.where(k >= seq, 1, 0)

    loop(0, n - 1, lambda k: far(other(k)).start())
    r.out[seq, :, pl.ds(pl.multiple_of(tp * size, 128), size)] = r.send[seq]
    pass_on(seq)

    tots_done.wait_send()
    for copy in pick_core + enc_core + main_core + enc_line + main_line:
        copy.wait_send()
    for i in range(half):

        @pl.when((x == 0) | upward)
        def _():
            state_copy((1 - x) * half + i).wait_send()

        @pl.when(x == 0)
        def _():
            state_copy(i).wait_send()

        @pl.when(z > 0)
        def _():
            prefix_copy(i).wait_send()

    def close_up(d):
        @pl.when(z + d < line)
        def _():
            up_copy(d).wait_send()

    loop(1, line, close_up)

    for e in range(groups - 1):
        for k in range(groups):
            partial_copy(e, k).wait_send()

    def close_row(d, _):
        core_copy(d, x).wait_send()

        @pl.when(d > 0)
        def _():
            for e in range(groups - 1):
                line_copy(d, e).wait_send()

        @pl.when((d > 0) | (x == 0))
        def _():
            for e in range(groups - 1):
                far_copy(d, e).wait_send()
            pair_copy(d).wait_send()

        @pl.when((d > 0) | (x == 1))
        def _():
            core_copy(d, 1 - x).wait_send()

        return 0

    lax.fori_loop(0, z + 1, close_row, 0)

    def deliver(k):
        far_wait(other(k))
        pass_on(other(k))

    loop(0, n - 1, deliver)
    pass_across(seq)
    loop(0, n - 1, lambda k: pass_across(other(k)))
    for copy in enc_line:
        copy.wait_recv()
    enc = r.bytes[:, pl.ds(pl.multiple_of(tp * quarter, 128), quarter)].astype(f32) + r.e_sum[hi]
    for g in rest:
        enc = enc + r.e_line_got[g].astype(f32)
    r.enc[...] = enc.astype(bf16)
    enc_write = pltpu.make_async_copy(r.enc, r.enc_hbm, r.enc_sem)
    enc_write.start()
    def close(d):
        for e in range(groups):
            beside(e, d).wait_recv()
        write(d).start()

    def write(d):
        return pltpu.make_async_copy(r.out.at[d], r.out_hbm.at[d], r.own.at[d])

    loop(0, n, close)
    sent = r.send.at[pl.ds(0, n - 1)]
    remote(sent, sent, r.hs, r.hr.at[seq], pair).wait_send()
    for e in range(groups):
        column = (lax.rem(hi - e + groups, groups) * 2 + lo) * size
        sent = r.out.at[:, :, pl.ds(pl.multiple_of(column, 128), size)]
        remote(sent, sent, r.hcs.at[e], r.hr.at[seq], core).wait_send()
        if e > 0:
            sent = r.out.at[:, :, pl.ds(pl.multiple_of(tp * size, 128), size)]
            remote(sent, sent, r.hys.at[e - 1], r.hr.at[seq], core).wait_send()
    enc_write.wait()
    loop(0, n, lambda d: write(d).wait())

def hand_out(enc_ref, main_ref, enc_out, main_out, enc, main, sems):
    ways = []
    for src, through, dst, pieces in ((main_ref, main, main_out, 2), (enc_ref, enc, enc_out, 1)):
        step = src.shape[0] // pieces
        for j in range(pieces):
            span, i = pl.ds(j * step, step), len(ways)
            fetch = pltpu.make_async_copy(src.at[span], through.at[span], sems.at[0, i])
            ways.append((fetch, pltpu.make_async_copy(through.at[span], dst.at[span], sems.at[1, i])))
    for fetch, _ in ways:
        fetch.start()
    for fetch, write in ways:
        fetch.wait()
        write.start()
    for _, write in ways:
        write.wait()


def on_device(
    byte_states, flags, stretch_owner, log_decay, w_x, w_z, w_bc, w_out, pad_vector, w_q, w_k, w_v, w_o
):
    rows, width = byte_states.shape
    heads = log_decay.shape[1]
    inner = w_x.shape[1]
    p = inner // heads
    state_n = w_bc.shape[1] // 2
    n = lax.axis_size("seq")
    split = lax.axis_size("tp")
    line, groups, half = n // 2, split // 2, heads // 2
    count = stretch_owner.shape[0]
    quarter = width // split
    cap = max(2, 2 * count // n)
    wide, part = w_q.shape
    size = wide // split
    units = part // HD
    shape = jax.ShapeDtypeStruct
    args = dict(
        bytes_in=byte_states, flags_in=flags.reshape(1, rows), owner_in=stretch_owner.reshape(1, count),
        decay_in=log_decay.T, wx_in=w_x, wz_in=w_z, wbc_in=w_bc, wout_in=w_out, pad_in=pad_vector,
        wq_in=w_q, wk_in=w_k, wv_in=w_v, wo_in=w_o,
    )
    outs = dict(enc_hbm=shape((rows, quarter), bf16), out_hbm=shape((n, cap, wide), bf16))

    def wide_vmem(*dims):
        return pltpu.VMEM(dims, f32)

    def vmem(*dims):
        return pltpu.VMEM(dims, bf16)

    others_n = max(groups - 1, 1)
    scratch = dict(
        bytes=vmem(rows, width), flags=pltpu.VMEM((1, rows), jnp.int32), owner=pltpu.VMEM((1, count), jnp.int32),
        decay=wide_vmem(heads, rows), wx=vmem(*w_x.shape), wz=vmem(*w_z.shape), wbc=vmem(*w_bc.shape),
        wout=vmem(*w_out.shape), pad=vmem(*pad_vector.shape), wq=vmem(*w_q.shape), wkv=vmem(wide, 2 * part),
        wo=vmem(*w_o.shape), own=DMA((max(len(args), n),)),
        tots=wide_vmem(n, -(-heads // 8) * 8, state_n), ts=DMA, tr=DMA,
        state=wide_vmem(heads, state_n, p), state_out=vmem(heads, state_n, p), state_got=vmem(heads, state_n, p),
        s1r=DMA((heads,)),
        slab_out=vmem(half, state_n, p), slab_got=vmem(line, half, state_n, p),
        s2s=DMA((line, half)), s2r=DMA((line, half)),
        prefix_out=vmem(half, state_n, p), prefix_got=vmem(half, state_n, p), s3s=DMA((half,)), s3r=DMA((half,)),
        start=vmem(heads, state_n, p), gate=wide_vmem(rows, inner), mixed=wide_vmem(rows, inner),
        base=vmem(2, groups, count, quarter), place=vmem(n * cap, count),
        d_send=vmem(groups, count, quarter), d_got=vmem(groups, count, quarter), d_core=DMA((2, groups)),
        d_line=vmem(groups, groups, count, quarter), d_line_s=DMA((others_n, groups)), d_line_r=DMA((groups, groups)),
        e_send=vmem(groups, rows, quarter), e_got=vmem(groups, rows, quarter), e_core=DMA((2, groups)),
        e_sum=wide_vmem(groups, rows, quarter), e_line_send=vmem(groups, rows, quarter),
        e_line_got=vmem(groups, rows, quarter), e_line=DMA((2, others_n)),
        f_send=vmem(groups, count, size), f_got=vmem(groups, count, size), f_core=DMA((2, groups)),
        f_sum=wide_vmem(groups, count, size), f_line_send=vmem(groups, count, size),
        f_line_got=vmem(groups, count, size), f_line=DMA((2, others_n)),
        rows=vmem(line, 2, 2, groups, count, quarter), gr=DMA((line, 2, groups)), gcr=DMA((line, 2)),
        gx=DMA((line,)), gy=DMA((line, others_n)), gd=DMA((line, others_n)), gc=DMA((line, 2)),
        stream=vmem(split, count, size), query=vmem(count, part),
        best=wide_vmem(units, count, 1), total=wide_vmem(units, count, 1), accum=wide_vmem(units, count, HD),
        enc=vmem(rows, quarter), enc_sem=DMA, out=vmem(n, cap, wide),
        send=vmem(n, cap, size), hs=DMA, hr=DMA((n,)),
        hys=DMA((others_n,)), hcs=DMA((groups,)), hcr=DMA((others_n, n)),
    )
    results = pl.pallas_call(
        functools.partial(whole_kernel, list(args) + list(outs) + list(scratch)),
        out_shape=list(outs.values()),
        in_specs=[HBM] * len(args),
        out_specs=[HBM] * len(outs),
        scratch_shapes=list(scratch.values()),
        cost_estimate=cost(60),
        compiler_params=pltpu.CompilerParams(
            collective_id=0, has_side_effects=True, vmem_limit_bytes=GRANT
        ),
    )(*args.values())
    enc_out, main_out = pl.pallas_call(
        hand_out,
        out_shape=list(outs.values()),
        in_specs=[HBM] * len(outs),
        out_specs=[HBM] * len(outs),
        scratch_shapes=[pltpu.VMEM(o.shape, o.dtype) for o in outs.values()] + [DMA((2, 3))],
        cost_estimate=cost(1),
        compiler_params=pltpu.CompilerParams(vmem_limit_bytes=GRANT),
    )(*results)
    return (enc_out, main_out.reshape(n * cap, wide))


def solution(mesh):
    placed = (
        P("seq", None),
        P("seq"),
        P("seq", None),
        P("seq", "tp"),
        P(None, "tp"),
        P(None, "tp"),
        P(),
        P("tp", None),
        P(),
        P(None, "tp"),
        P(None, "tp"),
        P(None, "tp"),
        P("tp", None),
    )
    return jax.shard_map(
        on_device,
        mesh=mesh,
        in_specs=placed,
        out_specs=(P("seq", "tp"), P("seq", None)),
        check_vma=False,
    )
```

```python
import functools
import math
import types

import jax
import jax.numpy as jnp
from jax import lax
from jax.experimental import pallas as pl
from jax.experimental.pallas import tpu as pltpu
from jax.sharding import PartitionSpec as P

HD = 128
eps = 1e-05
f32 = jnp.float32
bf16 = jnp.bfloat16
MESH = pl.DeviceIdType.MESH
VM = pl.BlockSpec(memory_space=pltpu.VMEM)
HBM = pl.BlockSpec(memory_space=pltpu.HBM)
DMA = pltpu.SemaphoreType.DMA
GRANT = 61000000


def cost(us):
    return pl.CostEstimate(flops=us * 10**9, bytes_accessed=us * 3 * 10**6, transcendentals=0)


def mm(a, b):
    return jnp.dot(a, b, preferred_element_type=f32)


def mm_t(a, b):
    return lax.dot_general(a, b, (((1,), (1,)), ((), ())), preferred_element_type=f32)


def t_mm(a, b):
    return lax.dot_general(a, b, (((0,), (0,)), ((), ())), preferred_element_type=f32)


def three(a):
    hi = a.astype(bf16)
    rest = a - hi.astype(f32)
    mid = rest.astype(bf16)
    low = (rest - mid.astype(f32)).astype(bf16)
    return hi, mid, low


def iota(shape, dim):
    return lax.broadcasted_iota(jnp.int32, shape, dim)


def loop(start, stop, body):
    if stop - start <= 8:
        for i in range(start, stop):
            body(i)
    else:
        lax.fori_loop(start, stop, lambda i, _: (body(i), 0)[1], 0)


def others(axis):
    me, n = lax.axis_index(axis), lax.axis_size(axis)
    return [lax.rem(me + d, n) for d in range(1, n)]


def remote(src, dst, send, recv, device):
    return pltpu.make_async_remote_copy(
        src_ref=src, dst_ref=dst, send_sem=send, recv_sem=recv, device_id=device, device_id_type=MESH
    )


def whole_kernel(names, *refs):
    r = types.SimpleNamespace(**dict(zip(names, refs)))
    n, split = lax.axis_size("seq"), lax.axis_size("tp")
    line, groups = n // 2, split // 2
    seq, tp = lax.axis_index("seq"), lax.axis_index("tp")
    z, x = seq // 2, lax.rem(seq, 2)
    hi, lo = tp // 2, lax.rem(tp, 2)
    pair = {"seq": z * 2 + 1 - x}
    core = {"tp": hi * 2 + 1 - lo}
    rest = [lax.rem(hi + e, groups) for e in range(1, groups)]

    def column(g):
        return {"tp": g * 2 + lo}

    def across(g):
        return {"seq": z * 2 + 1 - x, "tp": g * 2 + lo}

    rows, width = r.bytes_in.shape
    heads = r.decay_in.shape[0]
    half = heads // 2
    state_n = r.wbc_in.shape[1] // 2
    p = r.wx_in.shape[1] // heads
    count = r.owner_in.shape[1]
    quarter = width // split
    wide = r.wq_in.shape[0]
    size = wide // split
    part = r.wq_in.shape[1]
    units = part // HD
    cap = r.out_hbm.shape[1]

    fetches = {}
    moves = [
        ("decay", r.decay_in, r.decay),
        ("bytes", r.bytes_in, r.bytes),
        ("wbc", r.wbc_in, r.wbc),
        ("wx", r.wx_in, r.wx),
        ("flags", r.flags_in, r.flags),
        ("wz", r.wz_in, r.wz),
        ("pad", r.pad_in, r.pad),
        ("owner", r.owner_in, r.owner),
        ("wout", r.wout_in, r.wout),
        ("wk", r.wk_in, r.wkv.at[:, pl.ds(0, part)]),
        ("wv", r.wv_in, r.wkv.at[:, pl.ds(part, part)]),
        ("wq", r.wq_in, r.wq),
        ("wo", r.wo_in, r.wo),
    ]
    for i, (name, src, dst) in enumerate(moves):
        fetches[name] = pltpu.make_async_copy(src, dst, r.own.at[i])
    first = ("decay", "bytes", "wbc", "wx")
    for name in first:
        fetches[name].start()

    barrier = pltpu.get_barrier_semaphore()

    def knock(device):
        pl.semaphore_signal(barrier, inc=1, device_id=device, device_id_type=MESH)

    loop(1, n, lambda d: knock({"seq": lax.rem(seq + d, n)}))
    for peer in others("tp"):
        knock({"tp": peer})
    for g in rest:
        knock(across(g))

    for name in first[:-1]:
        fetches[name].wait()
    cum_row = r.decay[...]
    lane = iota(cum_row.shape, 1)
    reach = 1
    while reach < rows:
        cum_row = cum_row + jnp.where(lane >= reach, pltpu.roll(cum_row, reach, 1), 0.0)
        reach *= 2
    last = cum_row[:, rows - 1 : rows]
    filler = jnp.zeros((r.tots.shape[1] - heads, state_n), f32)
    r.tots[seq] = jnp.concatenate([jnp.broadcast_to(last, (heads, state_n)), filler], axis=0)
    def tot_copy(d):
        peer = lax.rem(seq + d, n)
        near = jnp.where(peer // 2 == z, 1, 0)
        return remote(r.tots.at[seq], r.tots.at[seq], r.ts, r.tr.at[near], {"seq": peer})

    def tots_done(some, near):
        there = r.tots.at[pl.ds(0, some)]
        return remote(there, there, r.ts, r.tr.at[near], pair)

    raw = r.bytes[...]
    norm = lax.rsqrt(jnp.mean(jnp.square(raw.astype(f32)), axis=-1, keepdims=True) + eps)
    bc = (mm(raw, r.wbc[...]) * norm).astype(bf16)
    bmat, cmat = bc[:, :state_n], bc[:, state_n:]
    fetches[first[-1]].wait()
    for name in fetches:
        if name not in first:
            fetches[name].start()
    xs = (mm(raw, r.wx[...]) * norm).astype(bf16)
    cum = jnp.concatenate([cum_row, jnp.zeros((128 - heads, rows), f32)], axis=0).T[:, :heads]
    tail = jnp.exp(cum[rows - 1 : rows, :] - cum)
    for h in range(heads):
        shrunk = (xs[:, h * p : (h + 1) * p].astype(f32) * tail[:, h : h + 1]).astype(bf16)
        state = t_mm(bmat, shrunk)
        r.state[h] = state
        r.state_out[h] = state.astype(bf16)

    def state_copy(h):
        return remote(r.state_out.at[h], r.state_got.at[h], r.own.at[h], r.s1r.at[h], pair)

    upward = z < line - 1
    pl.semaphore_wait(barrier, n - 1 + split - 1 + groups - 1)
    loop(1, n, lambda d: tot_copy(d).start())

    for i in range(half):

        @pl.when((x == 0) | upward)
        def _():
            state_copy((1 - x) * half + i).start()

    @pl.when(x == 0)
    def _():
        for i in range(half):
            state_copy(i).start()

    fetches["wz"].wait()
    gate = mm(raw, r.wz[...]) * norm
    gate = gate * jax.nn.sigmoid(gate)
    r.gate[...] = gate
    fetches["flags"].wait()
    flags = r.flags[...]
    upper = (iota((rows, rows), 0) <= iota((rows, rows), 1)).astype(f32).astype(bf16)
    many = jnp.broadcast_to(flags.astype(f32), (16, rows)).astype(bf16)
    rank = mm(many, upper)[0:1, :].astype(jnp.int32) - 1
    hit = (rank == iota((count, rows), 0)) & (flags == 1)
    picker = jnp.where(hit, 1.0, 0.0).astype(bf16)

    def pick(values):
        return sum(mm(picker, piece) for piece in three(values))

    tots_done(1, 1).wait_recv()

    def tot_rows(shard):
        tots = r.tots[shard]
        return [jnp.where(x == 0, tots[i : i + 1], tots[half + i : half + i + 1]) for i in range(half)]

    def slab_copy(d, i):
        return remote(
            r.slab_out.at[i], r.slab_got.at[z, i], r.s2s.at[d, i], r.s2r.at[z, i], {"seq": (z + d) * 2 + x}
        )

    def slab_wait(source, i):
        remote(r.slab_got.at[source, i], r.slab_got.at[source, i], r.s2s.at[0, i], r.s2r.at[source, i], pair).wait_recv()

    @pl.when(upward)
    def _():
        later = tot_rows(z * 2 + 1)
        for i in range(half):
            h = x * half + i
            state_copy(h).wait_recv()
            mine, got = r.state[h], r.state_got[h].astype(f32)
            first, second = jnp.where(x == 0, mine, got), jnp.where(x == 0, got, mine)
            r.slab_out[i] = (first * jnp.exp(later[i]) + second).astype(bf16)

            def reach(d):
                @pl.when(z + d < line)
                def _():
                    slab_copy(d, i).start()

            loop(1, line, reach)


    middle = rows // 2
    for k in range(2):
        a, b = k * middle, (k + 1) * middle
        inter = mm_t(cmat[a:b], bmat[:b])
        causal = iota((middle, b), 0) + a >= iota((middle, b), 1)
        for h in range(heads):
            spans = cum[a:b, h : h + 1] - cum_row[h : h + 1, :b]
            mixing = (inter * jnp.exp(jnp.where(causal, spans, -1e30))).astype(bf16)
            r.mixed[a:b, h * p : (h + 1) * p] = mm(mixing, xs[:b, h * p : (h + 1) * p])
    mixed_picked = pick(r.mixed[...])
    gate_picked = pick(gate)
    grow_picked = jnp.exp(pick(cum))
    c_picked = mm(picker, cmat).astype(bf16)
    for g in range(groups):
        for k in range(2):
            q = g * 2 + k
            r.base[k, g] = mm(picker, r.bytes[:, q * quarter : (q + 1) * quarter]).astype(bf16)
    fetches["pad"].wait()
    fetches["wk"].wait()
    fetches["wv"].wait()
    fetches["wq"].wait()
    pad = jnp.broadcast_to(r.pad[...].astype(f32).reshape(1, -1), (count, r.pad.shape[0]))
    pad_square = jnp.sum(pad * pad, axis=1, keepdims=True)
    pad = pad.astype(bf16)
    pad_kv = mm(pad[:16], r.wkv[width:, :])[0:1]
    pad_q = mm(pad[:16], r.wq[width:, :])[0:1]
    fetches["owner"].wait()
    owner = r.owner[...]
    ranks = -(-n // 128) * 128
    hot = jnp.where(owner == iota((ranks, count), 0), 1.0, 0.0)
    strict = jnp.where(iota((count, count), 0) < iota((count, count), 1), 1.0, 0.0)
    before = mm(hot.astype(bf16), strict.astype(bf16))
    order = jnp.sum(before * hot, axis=0, keepdims=True).astype(jnp.int32)
    slot = owner * cap + order
    r.place[...] = jnp.where(slot == iota((n * cap, count), 0), 1.0, 0.0).astype(bf16)

    def prefix_copy(i):
        return remote(r.prefix_out.at[i], r.prefix_got.at[i], r.s3s.at[i], r.s3r.at[i], pair)

    if n > 2:
        tots_done(n - 2, 0).wait_recv()
    prefix = []
    for i in range(half):

        def step(k, carry):
            moved = jnp.exp(tot_rows(k * 2)[i] + tot_rows(k * 2 + 1)[i])
            slab_wait(k, i)
            return carry * moved + r.slab_got[k, i].astype(f32)

        prefix.append(lax.fori_loop(0, z, step, jnp.zeros((state_n, p), f32)))
        r.prefix_out[i] = prefix[i].astype(bf16)

        @pl.when(z > 0)
        def _():
            prefix_copy(i).start()


    @pl.when(x == 1)
    def _():
        for i in range(half):
            state_copy(i).wait_recv()

    @pl.when((x == 1) & (z == line - 1))
    def _():
        for i in range(half):
            state_copy(half + i).wait_recv()

    tots = r.tots[z * 2]

    def settle(h, i, base, same):
        a, b = tots[i : i + 1], tots[half + i : half + i + 1]
        shrink = jnp.exp(jnp.where((x == 0) == same, a, b))
        moved = base * shrink + r.state_got[h].astype(f32)
        r.start[h] = jnp.where(x == 1, moved, base).astype(bf16)

    for i in range(half):
        settle(x * half + i, i, prefix[i], True)

    @pl.when(z > 0)
    def _():
        for i in range(half):
            prefix_copy(i).wait_recv()

    for i in range(half):
        got = jnp.where(z > 0, r.prefix_got[i].astype(f32), 0.0)
        settle((1 - x) * half + i, i, got, False)

    def piece(slab, xx, g):
        return r.rows.at[slab, lo, xx, g]

    def up_copy(d):
        here = piece(z, x, hi)
        return remote(here, here, r.s2s.at[d, 0], r.gr.at[z, x, hi], {"seq": (z + d) * 2 + x})

    def line_copy(d, e):
        here = piece(z - d, x, hi)
        return remote(here, here, r.gy.at[d, e], r.gr.at[z - d, x, hi], column(rest[e]))

    def pair_copy(d):
        here = piece(z - d, x, hi)
        return remote(here, here, r.gx.at[d], r.gr.at[z - d, x, hi], pair)

    def beyond_copy(e):
        here = piece(z, x, rest[e])
        return remote(here, here, r.gd.at[0, e], r.gr.at[z, x, rest[e]], pair)

    def far_copy(d, e):
        here = piece(z - d, x, hi)
        return remote(here, here, r.gd.at[d, e], r.gr.at[z - d, x, hi], across(rest[e]))

    def core_copy(d, xx):
        here = r.rows.at[z - d, lo, xx]
        return remote(here, here, r.gc.at[d, xx], r.gcr.at[z - d, xx], core)

    def core_wait(d, xx):
        there = r.rows.at[z - d, 1 - lo, xx]
        remote(there, there, r.gc.at[d, xx], r.gcr.at[z - d, xx], core).wait_recv()

    def piece_wait(slab, xx, g):
        here = piece(slab, xx, g)
        remote(here, here, r.gx.at[0], r.gr.at[slab, xx, g], pair).wait_recv()

    def spread(d):
        for e in range(groups - 1):
            far_copy(d, e).start()
        pair_copy(d).start()
        for e in range(groups - 1):
            line_copy(d, e).start()

    def relay_own():
        for e in range(groups - 1):
            complete(e)
        core_copy(0, x).start()

        @pl.when(x == 0)
        def _():
            for e in range(groups - 1):
                beyond_copy(e).start()

    def relay_pair(d):
        @pl.when((d > 0) | (x == 1))
        def _():
            for g in range(groups):
                piece_wait(z - d, 1 - x, g)
            core_copy(d, 1 - x).start()

    def relay(d):
        for g in rest:
            piece_wait(z - d, x, g)
        core_copy(d, x).start()
        relay_pair(d)

        @pl.when(d == 2)
        def _():
            for copy in enc_line:
                copy.start()

    def arrive(d):
        piece_wait(z - d, x, hi)
        spread(d)

    def climb(k):
        d = line - k

        @pl.when(z + d < line)
        def _():
            up_copy(d).start()

    def finish(mixed, gate, cs, grow):
        scaled = []
        for h in range(heads):
            cols = slice(h * p, (h + 1) * p)
            gated = (mixed[:, cols] + mm(cs, r.start[h]) * grow[:, h : h + 1]) * gate[:, cols]
            norm = lax.rsqrt(jnp.mean(gated * gated, axis=1, keepdims=True) + eps)
            scaled.append((gated * norm).astype(bf16))
        return jnp.concatenate(scaled, axis=1)

    def cols(k, g, n):
        return pl.ds(pl.multiple_of((g * 2 + k) * n, 128), n)

    turns = rest + [hi]

    def core_swap(left, weight, n, send, got, sems):
        copies = []
        for e, g in enumerate(turns):
            send[g] = mm(left, weight[:, cols(1 - lo, g, n)]).astype(bf16)
            copies.append(remote(send.at[g], got.at[g], sems.at[0, e], sems.at[1, e], core))
            copies[-1].start()
        return copies

    def line_copies(send, got, sems):
        return [
            remote(send.at[g], got.at[hi], sems.at[0, e], sems.at[1, e], column(g))
            for e, g in enumerate(rest)
        ]

    fetches["wout"].wait()
    def partial_copy(e, k):
        here = r.d_line.at[hi, turns[k]]
        return remote(here, here, r.d_line_s.at[e, k], r.d_line_r.at[hi, turns[k]], column(rest[e]))

    def complete(k):
        g = turns[k]
        for peer in rest:
            there = r.d_line.at[peer, g]
            remote(there, there, r.d_line_s.at[0, 0], r.d_line_r.at[peer, g], core).wait_recv()
        summed = sum(r.d_line[peer, g].astype(f32) for peer in range(groups))
        r.rows[z, lo, x, g] = (r.base[lo, g].astype(f32) + summed).astype(bf16)

    scaled_picked = finish(mixed_picked, gate_picked, c_picked, grow_picked)
    pick_core = core_swap(scaled_picked, r.wout, quarter, r.d_send, r.d_got, r.d_core)
    mine = [mm(scaled_picked, r.wout[:, cols(lo, g, quarter)]) for g in turns]
    scaled = finish(r.mixed[...], r.gate[...], cmat, jnp.exp(cum))
    for e, g in enumerate(turns):
        pick_core[e].wait_recv()
        r.d_line[hi, g] = (mine[e] + r.d_got[g].astype(f32)).astype(bf16)
        if e < len(rest):
            partial_copy(e, e).start()
    for e in range(len(rest)):
        for k in range(groups):
            if k != e:
                partial_copy(e, k).start()
    enc_core = core_swap(scaled, r.wout, quarter, r.e_send, r.e_got, r.e_core)
    for g in range(groups):
        r.e_sum[g] = mm(scaled, r.wout[:, cols(lo, g, quarter)])

    @pl.when(z > 1)
    def _():
        arrive(z)

    complete(len(rest))

    enc_line = line_copies(r.e_line_send, r.e_line_got, r.e_line)
    def close_slab(d):
        @pl.when(z + d < line)
        def _():
            for i in range(half):
                slab_copy(d, i).wait_send()

    loop(1, line, close_slab)
    loop(1, line, climb)

    @pl.when(x == 0)
    def _():
        pair_copy(0).start()

    relay_own()
    for copy in enc_core:
        copy.wait_recv()
    for g in range(groups):
        both = r.e_sum[g] + r.e_got[g].astype(f32)
        r.e_sum[g] = both
        r.e_line_send[g] = both.astype(bf16)

    scale = 1.0 / math.sqrt(HD)

    def project(blocks, weight, pads, factor=1.0):
        square = jnp.sum(sum(jnp.square(b.astype(f32)) for b in blocks), axis=1, keepdims=True)
        norm = lax.rsqrt((square + pad_square[0:1]) / wide + eps) * factor
        return ((mm(jnp.concatenate(blocks, axis=1), weight[:width, :]) + pads) * norm).astype(bf16)

    def attend(blocks, allowed=None):
        kv = project(blocks, r.wkv, pad_kv)
        for h in range(units):
            span = slice(h * HD, (h + 1) * HD)
            scores = mm_t(r.query[:, span], kv[:, span])
            if allowed is not None:
                scores = jnp.where(allowed, scores, -1e30)
            best = r.best[h]
            top = jnp.maximum(best, jnp.max(scores, axis=1, keepdims=True))
            shrink = jnp.exp(best - top)
            expo = jnp.exp(scores - top)
            r.best[h] = top
            r.total[h] = r.total[h] * shrink + jnp.sum(expo, axis=1, keepdims=True)
            r.accum[h] = r.accum[h] * shrink + mm(expo.astype(bf16), kv[:, part + h * HD : part + (h + 1) * HD])

    def block(xx):
        return [r.rows[z, q % 2, xx, q // 2] for q in range(split)]

    def slab(d):
        return [r.rows[z - d, q % 2, :, q // 2].reshape(2 * count, quarter) for q in range(split)]

    def own_slab():
        core_wait(0, x)
        mine = block(x)
        stream = jnp.concatenate(mine + [pad], axis=1)
        for q in range(split):
            r.stream[q] = stream[:, q * size : (q + 1) * size]
        r.query[...] = project(mine, r.wq, pad_q, scale)
        r.best[...] = jnp.full(r.best.shape, -1e30, f32)
        r.total[...] = jnp.zeros(r.total.shape, f32)
        r.accum[...] = jnp.zeros(r.accum.shape, f32)
        attend(mine, iota((count, count), 0) >= iota((count, count), 1))

    def own_pair():
        core_wait(0, 0)
        attend(block(0))

    @pl.when(z == 1)
    def _():
        arrive(1)

    lax.fori_loop(1, z, lambda k, _: (arrive(z - k), 0)[1], 0)
    @pl.when(z > 0)
    def _():
        relay(z)

    own_slab()

    def meet(d):
        core_wait(d, 0)
        core_wait(d, 1)
        attend(slab(d))

    @pl.when(z > 0)
    def _():
        meet(z)

    relay_pair(0)

    @pl.when(z <= 1)
    def _():
        for copy in enc_line:
            copy.start()


    @pl.when(z > 1)
    def _():
        relay(z - 1)


    @pl.when(x == 1)
    def _():
        own_pair()


    def turn(k, _):
        d = z - k

        @pl.when(d > 1)
        def _():
            relay(d - 1)

        meet(d)
        return 0

    lax.fori_loop(1, z, turn, 0)
    attended = jnp.concatenate([(r.accum[h] / r.total[h]).astype(bf16) for h in range(units)], axis=1)

    fetches["wo"].wait()
    main_core = core_swap(attended, r.wo, size, r.f_send, r.f_got, r.f_core)
    mine = [mm(attended, r.wo[:, cols(lo, g, size)]) for g in turns]
    main_line = line_copies(r.f_line_send, r.f_line_got, r.f_line)
    for e, g in enumerate(turns):
        main_core[e].wait_recv()
        both = mine[e] + r.f_got[g].astype(f32)
        r.f_sum[g] = both
        if e < len(rest):
            r.f_line_send[g] = both.astype(bf16)
            main_line[e].start()
    summed = r.stream[tp].astype(f32) + r.f_sum[hi]
    for copy in main_line:
        copy.wait_recv()
    for g in rest:
        summed = summed + r.f_line_got[g].astype(f32)
    r.send[...] = mm(r.place[...], summed.astype(bf16)).astype(bf16).reshape(n, cap, size)

    def spot(e, source):
        column = (lax.rem(hi - e + groups, groups) * 2 + lo) * size
        return r.out.at[source, :, pl.ds(pl.multiple_of(column, 128), size)]

    def far(peer):
        return remote(r.send.at[peer], spot(0, seq), r.hs, r.hr.at[seq], {"seq": peer})

    def far_wait(source):
        remote(spot(0, source), spot(0, source), r.hs, r.hr.at[source], pair).wait_recv()

    def direct(e, source):
        here = spot(0, source)
        got = r.gr.at[source // 2, lax.rem(source, 2), e]
        return remote(here, here, r.hys.at[e - 1], got, {"tp": lax.rem(hi + e, groups) * 2 + lo})

    def beside(e, source):
        here = spot(e, source)
        got = r.gcr.at[source // 2, lax.rem(source, 2)] if e == 0 else r.hcr.at[e - 1, source]
        return remote(here, here, r.hcs.at[e], got, core)

    def pass_on(source):
        for e in range(1, groups):
            direct(e, source).start()
        beside(0, source).start()

    def pass_across(source):
        for e in range(1, groups):
            direct(e, source).wait_recv()
            beside(e, source).start()

    def other(k):
        return k + jnp.where(k >= seq, 1, 0)

    loop(0, n - 1, lambda k: far(other(k)).start())
    r.out[seq, :, pl.ds(pl.multiple_of(tp * size, 128), size)] = r.send[seq]
    pass_on(seq)

    tots_done(n - 1, 0).wait_send()
    for copy in pick_core + enc_core + main_core + enc_line + main_line:
        copy.wait_send()
    for i in range(half):

        @pl.when((x == 0) | upward)
        def _():
            state_copy((1 - x) * half + i).wait_send()

        @pl.when(x == 0)
        def _():
            state_copy(i).wait_send()

        @pl.when(z > 0)
        def _():
            prefix_copy(i).wait_send()

    def close_up(d):
        @pl.when(z + d < line)
        def _():
            up_copy(d).wait_send()

    loop(1, line, close_up)

    for e in range(groups - 1):
        for k in range(groups):
            partial_copy(e, k).wait_send()

    def close_row(d, _):
        core_copy(d, x).wait_send()

        @pl.when(d > 0)
        def _():
            for e in range(groups - 1):
                line_copy(d, e).wait_send()

        @pl.when((d > 0) | (x == 0))
        def _():
            for e in range(groups - 1):
                far_copy(d, e).wait_send()
            pair_copy(d).wait_send()

        @pl.when((d > 0) | (x == 1))
        def _():
            core_copy(d, 1 - x).wait_send()

        return 0

    lax.fori_loop(0, z + 1, close_row, 0)

    def deliver(k):
        far_wait(other(k))
        pass_on(other(k))

    loop(0, n - 1, deliver)
    pass_across(seq)
    loop(0, n - 1, lambda k: pass_across(other(k)))
    for copy in enc_line:
        copy.wait_recv()
    enc = r.bytes[:, pl.ds(pl.multiple_of(tp * quarter, 128), quarter)].astype(f32) + r.e_sum[hi]
    for g in rest:
        enc = enc + r.e_line_got[g].astype(f32)
    r.enc[...] = enc.astype(bf16)
    enc_write = pltpu.make_async_copy(r.enc, r.enc_hbm, r.enc_sem)
    enc_write.start()
    def close(d):
        for e in range(groups):
            beside(e, d).wait_recv()
        write(d).start()

    def write(d):
        return pltpu.make_async_copy(r.out.at[d], r.out_hbm.at[d], r.own.at[d])

    loop(0, n, close)
    sent = r.send.at[pl.ds(0, n - 1)]
    remote(sent, sent, r.hs, r.hr.at[seq], pair).wait_send()
    for e in range(groups):
        column = (lax.rem(hi - e + groups, groups) * 2 + lo) * size
        sent = r.out.at[:, :, pl.ds(pl.multiple_of(column, 128), size)]
        remote(sent, sent, r.hcs.at[e], r.hr.at[seq], core).wait_send()
        if e > 0:
            sent = r.out.at[:, :, pl.ds(pl.multiple_of(tp * size, 128), size)]
            remote(sent, sent, r.hys.at[e - 1], r.hr.at[seq], core).wait_send()
    enc_write.wait()
    loop(0, n, lambda d: write(d).wait())

def hand_out(enc_ref, main_ref, enc_out, main_out, enc, main, sems):
    ways = []
    for src, through, dst, pieces in ((main_ref, main, main_out, 2), (enc_ref, enc, enc_out, 1)):
        step = src.shape[0] // pieces
        for j in range(pieces):
            span, i = pl.ds(j * step, step), len(ways)
            fetch = pltpu.make_async_copy(src.at[span], through.at[span], sems.at[0, i])
            ways.append((fetch, pltpu.make_async_copy(through.at[span], dst.at[span], sems.at[1, i])))
    for fetch, _ in ways:
        fetch.start()
    for fetch, write in ways:
        fetch.wait()
        write.start()
    for _, write in ways:
        write.wait()


def on_device(
    byte_states, flags, stretch_owner, log_decay, w_x, w_z, w_bc, w_out, pad_vector, w_q, w_k, w_v, w_o
):
    rows, width = byte_states.shape
    heads = log_decay.shape[1]
    inner = w_x.shape[1]
    p = inner // heads
    state_n = w_bc.shape[1] // 2
    n = lax.axis_size("seq")
    split = lax.axis_size("tp")
    line, groups, half = n // 2, split // 2, heads // 2
    count = stretch_owner.shape[0]
    quarter = width // split
    cap = max(2, 2 * count // n)
    wide, part = w_q.shape
    size = wide // split
    units = part // HD
    shape = jax.ShapeDtypeStruct
    args = dict(
        bytes_in=byte_states, flags_in=flags.reshape(1, rows), owner_in=stretch_owner.reshape(1, count),
        decay_in=log_decay.T, wx_in=w_x, wz_in=w_z, wbc_in=w_bc, wout_in=w_out, pad_in=pad_vector,
        wq_in=w_q, wk_in=w_k, wv_in=w_v, wo_in=w_o,
    )
    outs = dict(enc_hbm=shape((rows, quarter), bf16), out_hbm=shape((n, cap, wide), bf16))

    def wide_vmem(*dims):
        return pltpu.VMEM(dims, f32)

    def vmem(*dims):
        return pltpu.VMEM(dims, bf16)

    others_n = max(groups - 1, 1)
    scratch = dict(
        bytes=vmem(rows, width), flags=pltpu.VMEM((1, rows), jnp.int32), owner=pltpu.VMEM((1, count), jnp.int32),
        decay=wide_vmem(heads, rows), wx=vmem(*w_x.shape), wz=vmem(*w_z.shape), wbc=vmem(*w_bc.shape),
        wout=vmem(*w_out.shape), pad=vmem(*pad_vector.shape), wq=vmem(*w_q.shape), wkv=vmem(wide, 2 * part),
        wo=vmem(*w_o.shape), own=DMA((max(len(args), n),)),
        tots=wide_vmem(n, -(-heads // 8) * 8, state_n), ts=DMA, tr=DMA((2,)),
        state=wide_vmem(heads, state_n, p), state_out=vmem(heads, state_n, p), state_got=vmem(heads, state_n, p),
        s1r=DMA((heads,)),
        slab_out=vmem(half, state_n, p), slab_got=vmem(line, half, state_n, p),
        s2s=DMA((line, half)), s2r=DMA((line, half)),
        prefix_out=vmem(half, state_n, p), prefix_got=vmem(half, state_n, p), s3s=DMA((half,)), s3r=DMA((half,)),
        start=vmem(heads, state_n, p), gate=wide_vmem(rows, inner), mixed=wide_vmem(rows, inner),
        base=vmem(2, groups, count, quarter), place=vmem(n * cap, count),
        d_send=vmem(groups, count, quarter), d_got=vmem(groups, count, quarter), d_core=DMA((2, groups)),
        d_line=vmem(groups, groups, count, quarter), d_line_s=DMA((others_n, groups)), d_line_r=DMA((groups, groups)),
        e_send=vmem(groups, rows, quarter), e_got=vmem(groups, rows, quarter), e_core=DMA((2, groups)),
        e_sum=wide_vmem(groups, rows, quarter), e_line_send=vmem(groups, rows, quarter),
        e_line_got=vmem(groups, rows, quarter), e_line=DMA((2, others_n)),
        f_send=vmem(groups, count, size), f_got=vmem(groups, count, size), f_core=DMA((2, groups)),
        f_sum=wide_vmem(groups, count, size), f_line_send=vmem(groups, count, size),
        f_line_got=vmem(groups, count, size), f_line=DMA((2, others_n)),
        rows=vmem(line, 2, 2, groups, count, quarter), gr=DMA((line, 2, groups)), gcr=DMA((line, 2)),
        gx=DMA((line,)), gy=DMA((line, others_n)), gd=DMA((line, others_n)), gc=DMA((line, 2)),
        stream=vmem(split, count, size), query=vmem(count, part),
        best=wide_vmem(units, count, 1), total=wide_vmem(units, count, 1), accum=wide_vmem(units, count, HD),
        enc=vmem(rows, quarter), enc_sem=DMA, out=vmem(n, cap, wide),
        send=vmem(n, cap, size), hs=DMA, hr=DMA((n,)),
        hys=DMA((others_n,)), hcs=DMA((groups,)), hcr=DMA((others_n, n)),
    )
    results = pl.pallas_call(
        functools.partial(whole_kernel, list(args) + list(outs) + list(scratch)),
        out_shape=list(outs.values()),
        in_specs=[HBM] * len(args),
        out_specs=[HBM] * len(outs),
        scratch_shapes=list(scratch.values()),
        cost_estimate=cost(60),
        compiler_params=pltpu.CompilerParams(
            collective_id=0, has_side_effects=True, vmem_limit_bytes=GRANT
        ),
    )(*args.values())
    enc_out, main_out = pl.pallas_call(
        hand_out,
        out_shape=list(outs.values()),
        in_specs=[HBM] * len(outs),
        out_specs=[HBM] * len(outs),
        scratch_shapes=[pltpu.VMEM(o.shape, o.dtype) for o in outs.values()] + [DMA((2, 3))],
        cost_estimate=cost(1),
        compiler_params=pltpu.CompilerParams(vmem_limit_bytes=GRANT),
    )(*results)
    return (enc_out, main_out.reshape(n * cap, wide))


def solution(mesh):
    placed = (
        P("seq", None),
        P("seq"),
        P("seq", None),
        P("seq", "tp"),
        P(None, "tp"),
        P(None, "tp"),
        P(),
        P("tp", None),
        P(),
        P(None, "tp"),
        P(None, "tp"),
        P(None, "tp"),
        P("tp", None),
    )
    return jax.shard_map(
        on_device,
        mesh=mesh,
        in_specs=placed,
        out_specs=(P("seq", "tp"), P("seq", None)),
        check_vma=False,
    )
```

```python
import functools
import math
import types

import jax
import jax.numpy as jnp
from jax import lax
from jax.experimental import pallas as pl
from jax.experimental.pallas import tpu as pltpu
from jax.sharding import PartitionSpec as P

HD = 128
eps = 1e-05
f32 = jnp.float32
bf16 = jnp.bfloat16
MESH = pl.DeviceIdType.MESH
VM = pl.BlockSpec(memory_space=pltpu.VMEM)
HBM = pl.BlockSpec(memory_space=pltpu.HBM)
DMA = pltpu.SemaphoreType.DMA
GRANT = 61000000


def cost(us):
    return pl.CostEstimate(flops=us * 10**9, bytes_accessed=us * 3 * 10**6, transcendentals=0)


def mm(a, b):
    return jnp.dot(a, b, preferred_element_type=f32)


def mm_t(a, b):
    return lax.dot_general(a, b, (((1,), (1,)), ((), ())), preferred_element_type=f32)


def t_mm(a, b):
    return lax.dot_general(a, b, (((0,), (0,)), ((), ())), preferred_element_type=f32)


def three(a):
    hi = a.astype(bf16)
    rest = a - hi.astype(f32)
    mid = rest.astype(bf16)
    low = (rest - mid.astype(f32)).astype(bf16)
    return hi, mid, low


def iota(shape, dim):
    return lax.broadcasted_iota(jnp.int32, shape, dim)


def loop(start, stop, body):
    if stop - start <= 8:
        for i in range(start, stop):
            body(i)
    else:
        lax.fori_loop(start, stop, lambda i, _: (body(i), 0)[1], 0)


def others(axis):
    me, n = lax.axis_index(axis), lax.axis_size(axis)
    return [lax.rem(me + d, n) for d in range(1, n)]


def remote(src, dst, send, recv, device):
    return pltpu.make_async_remote_copy(
        src_ref=src, dst_ref=dst, send_sem=send, recv_sem=recv, device_id=device, device_id_type=MESH
    )


def whole_kernel(names, *refs):
    r = types.SimpleNamespace(**dict(zip(names, refs)))
    n, split = lax.axis_size("seq"), lax.axis_size("tp")
    line, groups = n // 2, split // 2
    seq, tp = lax.axis_index("seq"), lax.axis_index("tp")
    z, x = seq // 2, lax.rem(seq, 2)
    hi, lo = tp // 2, lax.rem(tp, 2)
    pair = {"seq": z * 2 + 1 - x}
    core = {"tp": hi * 2 + 1 - lo}
    rest = [lax.rem(hi + e, groups) for e in range(1, groups)]

    def column(g):
        return {"tp": g * 2 + lo}

    def across(g):
        return {"seq": z * 2 + 1 - x, "tp": g * 2 + lo}

    rows, width = r.bytes_in.shape
    heads = r.decay_in.shape[0]
    half = heads // 2
    state_n = r.wbc_in.shape[1] // 2
    p = r.wx_in.shape[1] // heads
    count = r.owner_in.shape[1]
    quarter = width // split
    wide = r.wq_in.shape[0]
    size = wide // split
    part = r.wq_in.shape[1]
    units = part // HD
    cap = r.out_hbm.shape[1]

    fetches = {}
    moves = [
        ("decay", r.decay_in, r.decay),
        ("bytes", r.bytes_in, r.bytes),
        ("wbc", r.wbc_in, r.wbc),
        ("wx", r.wx_in, r.wx),
        ("flags", r.flags_in, r.flags),
        ("wz", r.wz_in, r.wz),
        ("pad", r.pad_in, r.pad),
        ("owner", r.owner_in, r.owner),
        ("wout", r.wout_in, r.wout),
        ("wk", r.wk_in, r.wkv.at[:, pl.ds(0, part)]),
        ("wv", r.wv_in, r.wkv.at[:, pl.ds(part, part)]),
        ("wq", r.wq_in, r.wq),
        ("wo", r.wo_in, r.wo),
    ]
    for i, (name, src, dst) in enumerate(moves):
        fetches[name] = pltpu.make_async_copy(src, dst, r.own.at[i])
    first = ("decay", "bytes", "wbc", "wx")
    for name in first:
        fetches[name].start()

    barrier = pltpu.get_barrier_semaphore()

    def knock(device):
        pl.semaphore_signal(barrier, inc=1, device_id=device, device_id_type=MESH)

    loop(1, n, lambda d: knock({"seq": lax.rem(seq + d, n)}))
    for peer in others("tp"):
        knock({"tp": peer})
    for g in rest:
        knock(across(g))

    for name in first[:-1]:
        fetches[name].wait()
    cum_row = r.decay[...]
    lane = iota(cum_row.shape, 1)
    reach = 1
    while reach < rows:
        cum_row = cum_row + jnp.where(lane >= reach, pltpu.roll(cum_row, reach, 1), 0.0)
        reach *= 2
    last = cum_row[:, rows - 1 : rows]
    filler = jnp.zeros((r.tots.shape[1] - heads, state_n), f32)
    r.tots[seq] = jnp.concatenate([jnp.broadcast_to(last, (heads, state_n)), filler], axis=0)
    def tot_copy(d):
        peer = lax.rem(seq + d, n)
        near = jnp.where(peer // 2 == z, 1, 0)
        return remote(r.tots.at[seq], r.tots.at[seq], r.ts, r.tr.at[near], {"seq": peer})

    def tots_done(some, near):
        there = r.tots.at[pl.ds(0, some)]
        return remote(there, there, r.ts, r.tr.at[near], pair)

    raw = r.bytes[...]
    norm = lax.rsqrt(jnp.mean(jnp.square(raw.astype(f32)), axis=-1, keepdims=True) + eps)
    bc = (mm(raw, r.wbc[...]) * norm).astype(bf16)
    bmat, cmat = bc[:, :state_n], bc[:, state_n:]
    fetches[first[-1]].wait()
    for name in fetches:
        if name not in first:
            fetches[name].start()
    xs = (mm(raw, r.wx[...]) * norm).astype(bf16)
    cum = jnp.concatenate([cum_row, jnp.zeros((128 - heads, rows), f32)], axis=0).T[:, :heads]
    tail = jnp.exp(cum[rows - 1 : rows, :] - cum)
    for h in range(heads):
        shrunk = (xs[:, h * p : (h + 1) * p].astype(f32) * tail[:, h : h + 1]).astype(bf16)
        state = t_mm(bmat, shrunk)
        r.state[h] = state
        r.state_out[h] = state.astype(bf16)

    def state_copy(h):
        return remote(r.state_out.at[h], r.state_got.at[h], r.own.at[h], r.s1r.at[h], pair)

    upward = z < line - 1
    pl.semaphore_wait(barrier, n - 1 + split - 1 + groups - 1)
    loop(1, n, lambda d: tot_copy(d).start())

    for i in range(half):

        @pl.when((x == 0) | upward)
        def _():
            state_copy((1 - x) * half + i).start()

    @pl.when(x == 0)
    def _():
        for i in range(half):
            state_copy(i).start()

    fetches["wz"].wait()
    gate = mm(raw, r.wz[...]) * norm
    gate = gate * jax.nn.sigmoid(gate)
    r.gate[...] = gate
    fetches["flags"].wait()
    flags = r.flags[...]
    upper = (iota((rows, rows), 0) <= iota((rows, rows), 1)).astype(f32).astype(bf16)
    many = jnp.broadcast_to(flags.astype(f32), (16, rows)).astype(bf16)
    rank = mm(many, upper)[0:1, :].astype(jnp.int32) - 1
    hit = (rank == iota((count, rows), 0)) & (flags == 1)
    picker = jnp.where(hit, 1.0, 0.0).astype(bf16)

    def pick(values):
        return sum(mm(picker, piece) for piece in three(values))

    tots_done(1, 1).wait_recv()

    def tot_rows(shard):
        tots = r.tots[shard]
        return [jnp.where(x == 0, tots[i : i + 1], tots[half + i : half + i + 1]) for i in range(half)]

    def slab_copy(d, i):
        return remote(
            r.slab_out.at[i], r.slab_got.at[z, i], r.s2s.at[d, i], r.s2r.at[z, i], {"seq": (z + d) * 2 + x}
        )

    def slab_wait(source, i):
        remote(r.slab_got.at[source, i], r.slab_got.at[source, i], r.s2s.at[0, i], r.s2r.at[source, i], pair).wait_recv()

    @pl.when(upward)
    def _():
        later = tot_rows(z * 2 + 1)
        for i in range(half):
            h = x * half + i
            state_copy(h).wait_recv()
            mine, got = r.state[h], r.state_got[h].astype(f32)
            first, second = jnp.where(x == 0, mine, got), jnp.where(x == 0, got, mine)
            r.slab_out[i] = (first * jnp.exp(later[i]) + second).astype(bf16)

            def reach(k):
                d = line - k

                @pl.when(z + d < line)
                def _():
                    slab_copy(d, i).start()

            loop(1, line, reach)


    middle = rows // 2
    for k in range(2):
        a, b = k * middle, (k + 1) * middle
        inter = mm_t(cmat[a:b], bmat[:b])
        causal = iota((middle, b), 0) + a >= iota((middle, b), 1)
        for h in range(heads):
            spans = cum[a:b, h : h + 1] - cum_row[h : h + 1, :b]
            mixing = (inter * jnp.exp(jnp.where(causal, spans, -1e30))).astype(bf16)
            r.mixed[a:b, h * p : (h + 1) * p] = mm(mixing, xs[:b, h * p : (h + 1) * p])
    mixed_picked = pick(r.mixed[...])
    gate_picked = pick(gate)
    grow_picked = jnp.exp(pick(cum))
    c_picked = mm(picker, cmat).astype(bf16)
    for g in range(groups):
        for k in range(2):
            q = g * 2 + k
            r.base[k, g] = mm(picker, r.bytes[:, q * quarter : (q + 1) * quarter]).astype(bf16)
    fetches["pad"].wait()
    fetches["wk"].wait()
    fetches["wv"].wait()
    fetches["wq"].wait()
    pad = jnp.broadcast_to(r.pad[...].astype(f32).reshape(1, -1), (count, r.pad.shape[0]))
    pad_square = jnp.sum(pad * pad, axis=1, keepdims=True)
    pad = pad.astype(bf16)
    pad_kv = mm(pad[:16], r.wkv[width:, :])[0:1]
    pad_q = mm(pad[:16], r.wq[width:, :])[0:1]
    fetches["owner"].wait()
    owner = r.owner[...]
    ranks = -(-n // 128) * 128
    hot = jnp.where(owner == iota((ranks, count), 0), 1.0, 0.0)
    strict = jnp.where(iota((count, count), 0) < iota((count, count), 1), 1.0, 0.0)
    before = mm(hot.astype(bf16), strict.astype(bf16))
    order = jnp.sum(before * hot, axis=0, keepdims=True).astype(jnp.int32)
    slot = owner * cap + order
    r.place[...] = jnp.where(slot == iota((n * cap, count), 0), 1.0, 0.0).astype(bf16)

    def prefix_copy(i):
        return remote(r.prefix_out.at[i], r.prefix_got.at[i], r.s3s.at[i], r.s3r.at[i], pair)

    if n > 2:
        tots_done(n - 2, 0).wait_recv()
    prefix = []
    for i in range(half):

        def step(k, carry):
            moved = jnp.exp(tot_rows(k * 2)[i] + tot_rows(k * 2 + 1)[i])
            slab_wait(k, i)
            return carry * moved + r.slab_got[k, i].astype(f32)

        prefix.append(lax.fori_loop(0, z, step, jnp.zeros((state_n, p), f32)))
        r.prefix_out[i] = prefix[i].astype(bf16)

        @pl.when(z > 0)
        def _():
            prefix_copy(i).start()


    @pl.when(x == 1)
    def _():
        for i in range(half):
            state_copy(i).wait_recv()

    @pl.when((x == 1) & (z == line - 1))
    def _():
        for i in range(half):
            state_copy(half + i).wait_recv()

    tots = r.tots[z * 2]

    def settle(h, i, base, same):
        a, b = tots[i : i + 1], tots[half + i : half + i + 1]
        shrink = jnp.exp(jnp.where((x == 0) == same, a, b))
        moved = base * shrink + r.state_got[h].astype(f32)
        r.start[h] = jnp.where(x == 1, moved, base).astype(bf16)

    for i in range(half):
        settle(x * half + i, i, prefix[i], True)

    @pl.when(z > 0)
    def _():
        for i in range(half):
            prefix_copy(i).wait_recv()

    for i in range(half):
        got = jnp.where(z > 0, r.prefix_got[i].astype(f32), 0.0)
        settle((1 - x) * half + i, i, got, False)

    def piece(slab, xx, g):
        return r.rows.at[slab, lo, xx, g]

    def up_copy(d):
        here = piece(z, x, hi)
        return remote(here, here, r.s2s.at[d, 0], r.gr.at[z, x, hi], {"seq": (z + d) * 2 + x})

    def line_copy(d, e):
        here = piece(z - d, x, hi)
        return remote(here, here, r.gy.at[d, e], r.gr.at[z - d, x, hi], column(rest[e]))

    def pair_copy(d):
        here = piece(z - d, x, hi)
        return remote(here, here, r.gx.at[d], r.gr.at[z - d, x, hi], pair)

    def beyond_copy(e):
        here = piece(z, x, rest[e])
        return remote(here, here, r.gd.at[0, e], r.gr.at[z, x, rest[e]], pair)

    def far_copy(d, e):
        here = piece(z - d, x, hi)
        return remote(here, here, r.gd.at[d, e], r.gr.at[z - d, x, hi], across(rest[e]))

    def core_copy(d, xx):
        here = r.rows.at[z - d, lo, xx]
        return remote(here, here, r.gc.at[d, xx], r.gcr.at[z - d, xx], core)

    def core_wait(d, xx):
        there = r.rows.at[z - d, 1 - lo, xx]
        remote(there, there, r.gc.at[d, xx], r.gcr.at[z - d, xx], core).wait_recv()

    def piece_wait(slab, xx, g):
        here = piece(slab, xx, g)
        remote(here, here, r.gx.at[0], r.gr.at[slab, xx, g], pair).wait_recv()

    def spread(d):
        for e in range(groups - 1):
            far_copy(d, e).start()
        pair_copy(d).start()
        for e in range(groups - 1):
            line_copy(d, e).start()

    def relay_own():
        for e in range(groups - 1):
            complete(e)
        core_copy(0, x).start()

        @pl.when(x == 0)
        def _():
            for e in range(groups - 1):
                beyond_copy(e).start()

    def relay_pair(d):
        @pl.when((d > 0) | (x == 1))
        def _():
            for g in range(groups):
                piece_wait(z - d, 1 - x, g)
            core_copy(d, 1 - x).start()

    def relay(d):
        for g in rest:
            piece_wait(z - d, x, g)
        core_copy(d, x).start()
        relay_pair(d)

        @pl.when(d == 2)
        def _():
            for copy in enc_line:
                copy.start()

    def arrive(d):
        piece_wait(z - d, x, hi)
        spread(d)

    def climb(k):
        d = line - k

        @pl.when(z + d < line)
        def _():
            up_copy(d).start()

    def finish(mixed, gate, cs, grow):
        scaled = []
        for h in range(heads):
            cols = slice(h * p, (h + 1) * p)
            gated = (mixed[:, cols] + mm(cs, r.start[h]) * grow[:, h : h + 1]) * gate[:, cols]
            norm = lax.rsqrt(jnp.mean(gated * gated, axis=1, keepdims=True) + eps)
            scaled.append((gated * norm).astype(bf16))
        return jnp.concatenate(scaled, axis=1)

    def cols(k, g, n):
        return pl.ds(pl.multiple_of((g * 2 + k) * n, 128), n)

    turns = rest + [hi]

    def core_swap(left, weight, n, send, got, sems):
        copies = []
        for e, g in enumerate(turns):
            send[g] = mm(left, weight[:, cols(1 - lo, g, n)]).astype(bf16)
            copies.append(remote(send.at[g], got.at[g], sems.at[0, e], sems.at[1, e], core))
            copies[-1].start()
        return copies

    def line_copies(send, got, sems):
        return [
            remote(send.at[g], got.at[hi], sems.at[0, e], sems.at[1, e], column(g))
            for e, g in enumerate(rest)
        ]

    fetches["wout"].wait()
    def partial_copy(e, k):
        here = r.d_line.at[hi, turns[k]]
        return remote(here, here, r.d_line_s.at[e, k], r.d_line_r.at[hi, turns[k]], column(rest[e]))

    def complete(k):
        g = turns[k]
        for peer in rest:
            there = r.d_line.at[peer, g]
            remote(there, there, r.d_line_s.at[0, 0], r.d_line_r.at[peer, g], core).wait_recv()
        summed = sum(r.d_line[peer, g].astype(f32) for peer in range(groups))
        r.rows[z, lo, x, g] = (r.base[lo, g].astype(f32) + summed).astype(bf16)

    scaled_picked = finish(mixed_picked, gate_picked, c_picked, grow_picked)
    pick_core = core_swap(scaled_picked, r.wout, quarter, r.d_send, r.d_got, r.d_core)
    mine = [mm(scaled_picked, r.wout[:, cols(lo, g, quarter)]) for g in turns]
    scaled = finish(r.mixed[...], r.gate[...], cmat, jnp.exp(cum))
    for e, g in enumerate(turns):
        pick_core[e].wait_recv()
        r.d_line[hi, g] = (mine[e] + r.d_got[g].astype(f32)).astype(bf16)
        if e < len(rest):
            partial_copy(e, e).start()
    for e in range(len(rest)):
        for k in range(groups):
            if k != e:
                partial_copy(e, k).start()
    enc_core = core_swap(scaled, r.wout, quarter, r.e_send, r.e_got, r.e_core)
    for g in range(groups):
        r.e_sum[g] = mm(scaled, r.wout[:, cols(lo, g, quarter)])

    @pl.when(z > 1)
    def _():
        arrive(z)

    complete(len(rest))

    enc_line = line_copies(r.e_line_send, r.e_line_got, r.e_line)
    def close_slab(d):
        @pl.when(z + d < line)
        def _():
            for i in range(half):
                slab_copy(d, i).wait_send()

    loop(1, line, close_slab)
    loop(1, line, climb)

    @pl.when(x == 0)
    def _():
        pair_copy(0).start()

    relay_own()
    for copy in enc_core:
        copy.wait_recv()
    for g in range(groups):
        both = r.e_sum[g] + r.e_got[g].astype(f32)
        r.e_sum[g] = both
        r.e_line_send[g] = both.astype(bf16)

    scale = 1.0 / math.sqrt(HD)

    def project(blocks, weight, pads, factor=1.0):
        square = jnp.sum(sum(jnp.square(b.astype(f32)) for b in blocks), axis=1, keepdims=True)
        norm = lax.rsqrt((square + pad_square[0:1]) / wide + eps) * factor
        return ((mm(jnp.concatenate(blocks, axis=1), weight[:width, :]) + pads) * norm).astype(bf16)

    def attend(blocks, allowed=None):
        kv = project(blocks, r.wkv, pad_kv)
        for h in range(units):
            span = slice(h * HD, (h + 1) * HD)
            scores = mm_t(r.query[:, span], kv[:, span])
            if allowed is not None:
                scores = jnp.where(allowed, scores, -1e30)
            best = r.best[h]
            top = jnp.maximum(best, jnp.max(scores, axis=1, keepdims=True))
            shrink = jnp.exp(best - top)
            expo = jnp.exp(scores - top)
            r.best[h] = top
            r.total[h] = r.total[h] * shrink + jnp.sum(expo, axis=1, keepdims=True)
            r.accum[h] = r.accum[h] * shrink + mm(expo.astype(bf16), kv[:, part + h * HD : part + (h + 1) * HD])

    def block(xx):
        return [r.rows[z, q % 2, xx, q // 2] for q in range(split)]

    def slab(d):
        return [r.rows[z - d, q % 2, :, q // 2].reshape(2 * count, quarter) for q in range(split)]

    def own_slab():
        core_wait(0, x)
        mine = block(x)
        stream = jnp.concatenate(mine + [pad], axis=1)
        for q in range(split):
            r.stream[q] = stream[:, q * size : (q + 1) * size]
        r.query[...] = project(mine, r.wq, pad_q, scale)
        r.best[...] = jnp.full(r.best.shape, -1e30, f32)
        r.total[...] = jnp.zeros(r.total.shape, f32)
        r.accum[...] = jnp.zeros(r.accum.shape, f32)
        attend(mine, iota((count, count), 0) >= iota((count, count), 1))

    def own_pair():
        core_wait(0, 0)
        attend(block(0))

    @pl.when(z == 1)
    def _():
        arrive(1)

    lax.fori_loop(1, z, lambda k, _: (arrive(z - k), 0)[1], 0)
    @pl.when(z > 0)
    def _():
        relay(z)

    own_slab()

    def meet(d):
        core_wait(d, 0)
        core_wait(d, 1)
        attend(slab(d))

    @pl.when(z > 0)
    def _():
        meet(z)

    relay_pair(0)

    @pl.when(z <= 1)
    def _():
        for copy in enc_line:
            copy.start()


    @pl.when(z > 1)
    def _():
        relay(z - 1)


    @pl.when(x == 1)
    def _():
        own_pair()


    def turn(k, _):
        d = z - k

        @pl.when(d > 1)
        def _():
            relay(d - 1)

        meet(d)
        return 0

    lax.fori_loop(1, z, turn, 0)
    attended = jnp.concatenate([(r.accum[h] / r.total[h]).astype(bf16) for h in range(units)], axis=1)

    fetches["wo"].wait()
    main_core = core_swap(attended, r.wo, size, r.f_send, r.f_got, r.f_core)
    mine = [mm(attended, r.wo[:, cols(lo, g, size)]) for g in turns]
    main_line = line_copies(r.f_line_send, r.f_line_got, r.f_line)
    for e, g in enumerate(turns):
        main_core[e].wait_recv()
        both = mine[e] + r.f_got[g].astype(f32)
        r.f_sum[g] = both
        if e < len(rest):
            r.f_line_send[g] = both.astype(bf16)
            main_line[e].start()
    summed = r.stream[tp].astype(f32) + r.f_sum[hi]
    for copy in main_line:
        copy.wait_recv()
    for g in rest:
        summed = summed + r.f_line_got[g].astype(f32)
    r.send[...] = mm(r.place[...], summed.astype(bf16)).astype(bf16).reshape(n, cap, size)

    def spot(e, source):
        column = (lax.rem(hi - e + groups, groups) * 2 + lo) * size
        return r.out.at[source, :, pl.ds(pl.multiple_of(column, 128), size)]

    def far(peer):
        return remote(r.send.at[peer], spot(0, seq), r.hs, r.hr.at[seq], {"seq": peer})

    def far_wait(source):
        remote(spot(0, source), spot(0, source), r.hs, r.hr.at[source], pair).wait_recv()

    def direct(e, source):
        here = spot(0, source)
        got = r.gr.at[source // 2, lax.rem(source, 2), e]
        return remote(here, here, r.hys.at[e - 1], got, {"tp": lax.rem(hi + e, groups) * 2 + lo})

    def beside(e, source):
        here = spot(e, source)
        got = r.gcr.at[source // 2, lax.rem(source, 2)] if e == 0 else r.hcr.at[e - 1, source]
        return remote(here, here, r.hcs.at[e], got, core)

    def pass_on(source):
        for e in range(1, groups):
            direct(e, source).start()
        beside(0, source).start()

    def pass_across(source):
        for e in range(1, groups):
            direct(e, source).wait_recv()
            beside(e, source).start()

    def other(k):
        return k + jnp.where(k >= seq, 1, 0)

    loop(0, n - 1, lambda k: far(other(k)).start())
    r.out[seq, :, pl.ds(pl.multiple_of(tp * size, 128), size)] = r.send[seq]
    pass_on(seq)

    tots_done(n - 1, 0).wait_send()
    for copy in pick_core + enc_core + main_core + enc_line + main_line:
        copy.wait_send()
    for i in range(half):

        @pl.when((x == 0) | upward)
        def _():
            state_copy((1 - x) * half + i).wait_send()

        @pl.when(x == 0)
        def _():
            state_copy(i).wait_send()

        @pl.when(z > 0)
        def _():
            prefix_copy(i).wait_send()

    def close_up(d):
        @pl.when(z + d < line)
        def _():
            up_copy(d).wait_send()

    loop(1, line, close_up)

    for e in range(groups - 1):
        for k in range(groups):
            partial_copy(e, k).wait_send()

    def close_row(d, _):
        core_copy(d, x).wait_send()

        @pl.when(d > 0)
        def _():
            for e in range(groups - 1):
                line_copy(d, e).wait_send()

        @pl.when((d > 0) | (x == 0))
        def _():
            for e in range(groups - 1):
                far_copy(d, e).wait_send()
            pair_copy(d).wait_send()

        @pl.when((d > 0) | (x == 1))
        def _():
            core_copy(d, 1 - x).wait_send()

        return 0

    lax.fori_loop(0, z + 1, close_row, 0)

    def deliver(k):
        far_wait(other(k))
        pass_on(other(k))

    loop(0, n - 1, deliver)
    pass_across(seq)
    loop(0, n - 1, lambda k: pass_across(other(k)))
    for copy in enc_line:
        copy.wait_recv()
    enc = r.bytes[:, pl.ds(pl.multiple_of(tp * quarter, 128), quarter)].astype(f32) + r.e_sum[hi]
    for g in rest:
        enc = enc + r.e_line_got[g].astype(f32)
    r.enc[...] = enc.astype(bf16)
    enc_write = pltpu.make_async_copy(r.enc, r.enc_hbm, r.enc_sem)
    enc_write.start()
    def close(d):
        for e in range(groups):
            beside(e, d).wait_recv()
        write(d).start()

    def write(d):
        return pltpu.make_async_copy(r.out.at[d], r.out_hbm.at[d], r.own.at[d])

    loop(0, n, close)
    sent = r.send.at[pl.ds(0, n - 1)]
    remote(sent, sent, r.hs, r.hr.at[seq], pair).wait_send()
    for e in range(groups):
        column = (lax.rem(hi - e + groups, groups) * 2 + lo) * size
        sent = r.out.at[:, :, pl.ds(pl.multiple_of(column, 128), size)]
        remote(sent, sent, r.hcs.at[e], r.hr.at[seq], core).wait_send()
        if e > 0:
            sent = r.out.at[:, :, pl.ds(pl.multiple_of(tp * size, 128), size)]
            remote(sent, sent, r.hys.at[e - 1], r.hr.at[seq], core).wait_send()
    enc_write.wait()
    loop(0, n, lambda d: write(d).wait())

def hand_out(enc_ref, main_ref, enc_out, main_out, enc, main, sems):
    ways = []
    for src, through, dst, pieces in ((main_ref, main, main_out, 2), (enc_ref, enc, enc_out, 1)):
        step = src.shape[0] // pieces
        for j in range(pieces):
            span, i = pl.ds(j * step, step), len(ways)
            fetch = pltpu.make_async_copy(src.at[span], through.at[span], sems.at[0, i])
            ways.append((fetch, pltpu.make_async_copy(through.at[span], dst.at[span], sems.at[1, i])))
    for fetch, _ in ways:
        fetch.start()
    for fetch, write in ways:
        fetch.wait()
        write.start()
    for _, write in ways:
        write.wait()


def on_device(
    byte_states, flags, stretch_owner, log_decay, w_x, w_z, w_bc, w_out, pad_vector, w_q, w_k, w_v, w_o
):
    rows, width = byte_states.shape
    heads = log_decay.shape[1]
    inner = w_x.shape[1]
    p = inner // heads
    state_n = w_bc.shape[1] // 2
    n = lax.axis_size("seq")
    split = lax.axis_size("tp")
    line, groups, half = n // 2, split // 2, heads // 2
    count = stretch_owner.shape[0]
    quarter = width // split
    cap = max(2, 2 * count // n)
    wide, part = w_q.shape
    size = wide // split
    units = part // HD
    shape = jax.ShapeDtypeStruct
    args = dict(
        bytes_in=byte_states, flags_in=flags.reshape(1, rows), owner_in=stretch_owner.reshape(1, count),
        decay_in=log_decay.T, wx_in=w_x, wz_in=w_z, wbc_in=w_bc, wout_in=w_out, pad_in=pad_vector,
        wq_in=w_q, wk_in=w_k, wv_in=w_v, wo_in=w_o,
    )
    outs = dict(enc_hbm=shape((rows, quarter), bf16), out_hbm=shape((n, cap, wide), bf16))

    def wide_vmem(*dims):
        return pltpu.VMEM(dims, f32)

    def vmem(*dims):
        return pltpu.VMEM(dims, bf16)

    others_n = max(groups - 1, 1)
    scratch = dict(
        bytes=vmem(rows, width), flags=pltpu.VMEM((1, rows), jnp.int32), owner=pltpu.VMEM((1, count), jnp.int32),
        decay=wide_vmem(heads, rows), wx=vmem(*w_x.shape), wz=vmem(*w_z.shape), wbc=vmem(*w_bc.shape),
        wout=vmem(*w_out.shape), pad=vmem(*pad_vector.shape), wq=vmem(*w_q.shape), wkv=vmem(wide, 2 * part),
        wo=vmem(*w_o.shape), own=DMA((max(len(args), n),)),
        tots=wide_vmem(n, -(-heads // 8) * 8, state_n), ts=DMA, tr=DMA((2,)),
        state=wide_vmem(heads, state_n, p), state_out=vmem(heads, state_n, p), state_got=vmem(heads, state_n, p),
        s1r=DMA((heads,)),
        slab_out=vmem(half, state_n, p), slab_got=vmem(line, half, state_n, p),
        s2s=DMA((line, half)), s2r=DMA((line, half)),
        prefix_out=vmem(half, state_n, p), prefix_got=vmem(half, state_n, p), s3s=DMA((half,)), s3r=DMA((half,)),
        start=vmem(heads, state_n, p), gate=wide_vmem(rows, inner), mixed=wide_vmem(rows, inner),
        base=vmem(2, groups, count, quarter), place=vmem(n * cap, count),
        d_send=vmem(groups, count, quarter), d_got=vmem(groups, count, quarter), d_core=DMA((2, groups)),
        d_line=vmem(groups, groups, count, quarter), d_line_s=DMA((others_n, groups)), d_line_r=DMA((groups, groups)),
        e_send=vmem(groups, rows, quarter), e_got=vmem(groups, rows, quarter), e_core=DMA((2, groups)),
        e_sum=wide_vmem(groups, rows, quarter), e_line_send=vmem(groups, rows, quarter),
        e_line_got=vmem(groups, rows, quarter), e_line=DMA((2, others_n)),
        f_send=vmem(groups, count, size), f_got=vmem(groups, count, size), f_core=DMA((2, groups)),
        f_sum=wide_vmem(groups, count, size), f_line_send=vmem(groups, count, size),
        f_line_got=vmem(groups, count, size), f_line=DMA((2, others_n)),
        rows=vmem(line, 2, 2, groups, count, quarter), gr=DMA((line, 2, groups)), gcr=DMA((line, 2)),
        gx=DMA((line,)), gy=DMA((line, others_n)), gd=DMA((line, others_n)), gc=DMA((line, 2)),
        stream=vmem(split, count, size), query=vmem(count, part),
        best=wide_vmem(units, count, 1), total=wide_vmem(units, count, 1), accum=wide_vmem(units, count, HD),
        enc=vmem(rows, quarter), enc_sem=DMA, out=vmem(n, cap, wide),
        send=vmem(n, cap, size), hs=DMA, hr=DMA((n,)),
        hys=DMA((others_n,)), hcs=DMA((groups,)), hcr=DMA((others_n, n)),
    )
    results = pl.pallas_call(
        functools.partial(whole_kernel, list(args) + list(outs) + list(scratch)),
        out_shape=list(outs.values()),
        in_specs=[HBM] * len(args),
        out_specs=[HBM] * len(outs),
        scratch_shapes=list(scratch.values()),
        cost_estimate=cost(60),
        compiler_params=pltpu.CompilerParams(
            collective_id=0, has_side_effects=True, vmem_limit_bytes=GRANT
        ),
    )(*args.values())
    enc_out, main_out = pl.pallas_call(
        hand_out,
        out_shape=list(outs.values()),
        in_specs=[HBM] * len(outs),
        out_specs=[HBM] * len(outs),
        scratch_shapes=[pltpu.VMEM(o.shape, o.dtype) for o in outs.values()] + [DMA((2, 3))],
        cost_estimate=cost(1),
        compiler_params=pltpu.CompilerParams(vmem_limit_bytes=GRANT),
    )(*results)
    return (enc_out, main_out.reshape(n * cap, wide))


def solution(mesh):
    placed = (
        P("seq", None),
        P("seq"),
        P("seq", None),
        P("seq", "tp"),
        P(None, "tp"),
        P(None, "tp"),
        P(),
        P("tp", None),
        P(),
        P(None, "tp"),
        P(None, "tp"),
        P(None, "tp"),
        P("tp", None),
    )
    return jax.shard_map(
        on_device,
        mesh=mesh,
        in_specs=placed,
        out_specs=(P("seq", "tp"), P("seq", None)),
        check_vma=False,
    )
```
